32 devices in a mesh: grp: 2 (over y), seq: 4 (over z), head: 2 (over x), sub: 2 (over core).
Axes of the slice: x: 2, y: 2, z: 4, core: 2. Of those that a mesh axis runs over, the one named last changes fastest.
Arguments:
- tokens: bfloat16 [4096, 3584], P(('grp', 'seq', 'sub')), parts along dimension 0, may hold values from -12 to 12, as said below
- norm_gain: float32 [2, 3584], replicated, may hold values from 0.1 to 1.9
- w_query: bfloat16 [2, 3584, 2048], P(None, ('seq', 'sub'), 'head'), may hold values from -1 to 1
- w_key: bfloat16 [2, 3584, 512], P(None, ('seq', 'sub')), may hold values from -4 to 4
- w_value: bfloat16 [2, 3584, 512], P(None, ('seq', 'sub')), may hold values from -0.09375 to 0.09375
- w_out: bfloat16 [2, 2048, 3584], P(None, 'head', ('seq', 'sub')), may hold values from -0.125 to 0.125
- modality: int32 [4096], P('grp'), parts along dimension 0, may hold values from 0 to 1, as said below
- doc_ids: int32 [4096], P('grp'), parts along dimension 0, may hold values from 0 to 3, never falling along the last dimension, each value on 1 to 1536 neighbouring positions
Outputs:
- mixed: bfloat16 [4096, 3584], P(('grp', 'seq', 'sub'), 'head'), parts along dimension 0
The draws below stay inside these ranges and needn't reach their ends.
There are 2 independent parts, one for each index of `grp`. The reference program is written for one: setup_inputs(seed, part) draws one part's arguments, and reference() takes and returns one part's arrays. A program takes and returns all parts, laid end to end along the dimension named above; an argument that names none is the same for every part. Nothing has to cross between parts.
Inputs may be any that keep to these rules, and one draw needn't show every extreme that they name: `tokens`: rows carry their own scale. `modality`: positions below 512 are 0; after that, each aligned run of 64 positions is all 0 or all 1. `doc_ids`: never falling along the positions; a document holds at most 1536 positions, and one holds exactly that many.
All inputs are finite; a program needn't handle non-finite values.
Results may differ from the reference program's by a relative error of at most 0.015.
Values may be sent and summed in bfloat16 or wider, within the bound.
No kernel may reach another device: no remote copies, remote signals or barrier semaphores. Data moves between devices by JAX's collectives and lax.ppermute only.
A program may use at most 128 MiB of HBM per device.

```python
import math
import jax
import jax.numpy as jnp
import numpy as np
from jax import lax

D = 3584
HEAD_DIM = 128
KV_HEADS = 4
Q_HEADS = 16
SEQ = 2048
RUN = 64
N_HEAD = 2


def draw_tokens(key, part):
    keys = jax.random.split(jax.random.fold_in(key, 3), 3)
    row_scale = jnp.exp(jax.random.uniform(keys[0], (SEQ, 1), jnp.float32, math.log(0.3), math.log(3.0)))
    col_scale = jnp.exp(jax.random.uniform(keys[1], (1, D), jnp.float32, math.log(0.8), math.log(1.25)))
    values = jnp.clip(jax.random.normal(keys[2], (SEQ, D), jnp.float32), -3.0, 3.0)
    return (values * row_scale * col_scale).astype(jnp.bfloat16)


def query_key(key):
    keys = jax.random.split(jax.random.fold_in(key, 17), 3)
    root = math.sqrt(D)
    queries = 4.0 * jnp.clip(jax.random.normal(keys[0], (2, D, Q_HEADS, HEAD_DIM), jnp.float32), -4.5, 4.5) / root
    keyed = jnp.clip(jax.random.normal(keys[2], (2, D, KV_HEADS, HEAD_DIM), jnp.float32), -4.5, 4.5) / root
    queries = jnp.clip(queries, -1.0, 1.0).reshape(2, D, Q_HEADS * HEAD_DIM)
    keyed = jnp.clip(keyed, -4.0, 4.0).reshape(2, D, KV_HEADS * HEAD_DIM)
    return (queries, keyed)


def draw_w_query(key, part):
    return query_key(key)[0].astype(jnp.bfloat16)


def draw_w_key(key, part):
    return query_key(key)[1].astype(jnp.bfloat16)


def draw_modality(key, part):
    units = SEQ // RUN
    picks = jax.random.randint(jax.random.fold_in(key, 29), (units,), 0, 4)
    starts = jnp.arange(units, dtype=jnp.int32) * RUN
    chosen = jnp.where(starts >= SEQ // 4, (picks > 0).astype(jnp.int32), 0)
    return jnp.repeat(chosen, RUN, total_repeat_length=SEQ).astype(jnp.int32)


def levels(key, extent, cuts, smallest, largest):
    level = 1.0
    for position, shards_of in cuts:
        heights = jax.random.uniform(jax.random.fold_in(jax.random.fold_in(key, 6), position), (shards_of,), jnp.float32, smallest / len(cuts), largest / len(cuts))
        level = level * jnp.repeat(jnp.exp(heights), extent[position] // shards_of).reshape((-1,) + (1,) * (len(extent) - 1 - position))
    return level


def length_profile(count, total, bound, slope):
    portions = [(1 << 20) // math.isqrt(standing ** slope) + 1 for standing in range(2, count + 1)]
    surplus, given = total - bound - (count - 1), [1] * (count - 1)
    while surplus > 0:
        free = [i for i in range(count - 1) if given[i] < bound]
        whole, left = sum([portions[i] for i in free]), surplus
        for i in free:
            more = min(bound - given[i], max(1, left * portions[i] // whole), surplus)
            given[i] = given[i] + more
            surplus = surplus - more
    return np.array([bound] + given)


def uneven(own_key, number_of, total, bound, skew):
    if number_of == 2:
        one = jax.random.randint(own_key, (), max(1, total - bound), min(bound, total - 1) + 1)
        return jnp.stack([one, total - one])
    tallies = jnp.asarray(length_profile(number_of, total, bound, skew), jnp.int32)
    twos = (number_of - 1) // 2
    donor, sink = tallies[1:1 + 2 * twos:2], tallies[2:2 + 2 * twos:2]
    margin = jnp.minimum(donor - 1, bound - sink)
    shifted = jax.random.randint(jax.random.fold_in(own_key, 1), (twos,), 0, 1 << 20) % (margin + 1)
    tallies = tallies.at[1:1 + 2 * twos:2].set(donor - shifted).at[2:2 + 2 * twos:2].set(sink + shifted)
    return tallies[jax.random.permutation(jax.random.fold_in(own_key, 2), number_of)]


def centred(rng, extent, width, reach, cuts=(), kind=jnp.bfloat16):
    result = width * jax.random.normal(rng, extent, jnp.float32)
    if cuts:
        result = result * levels(rng, extent, cuts, -0.22, 0.18)
    return jnp.clip(result, -reach, reach).astype(kind)


def setup_inputs(seed: int = 0, part: int = 0) -> dict:
    seeds = jax.random.split(jax.random.key(seed), 9)
    part_splits = jax.random.split(jax.random.fold_in(seeds[8], part), 9)
    tokens = draw_tokens(jax.random.fold_in(jax.random.fold_in(seeds[8], part), 71), part)
    norm_gain = jnp.clip(1.0 + 0.18 * jax.random.normal(seeds[1], (2, D), jnp.float32), 0.1, 1.9)
    w_query = draw_w_query(jax.random.fold_in(seeds[8], 71), part)
    w_key = draw_w_key(jax.random.fold_in(seeds[8], 71), part)
    w_value = centred(seeds[4], (2, D, KV_HEADS * HEAD_DIM), D ** -0.5, 0.09375, ((1, 8),))
    w_out = centred(seeds[5], (2, Q_HEADS * HEAD_DIM, D), (Q_HEADS * HEAD_DIM) ** -0.5, 0.125, ((1, 2), (2, 8)))
    modality = draw_modality(jax.random.fold_in(jax.random.fold_in(seeds[8], part), 71), part)
    doc_ids = jnp.searchsorted(jnp.cumsum(uneven(part_splits[7], 4, SEQ, SEQ * 3 // 4, 0)), jnp.arange(SEQ), side="right").astype(jnp.int32)
    return {"tokens": tokens, "norm_gain": norm_gain, "w_query": w_query, "w_key": w_key, "w_value": w_value, "w_out": w_out, "modality": modality, "doc_ids": doc_ids}


EPS = 1e-06

def block_ids(modality, doc_ids):
    changed = (modality[1:] != modality[:-1]) | (doc_ids[1:] != doc_ids[:-1])
    begins = jnp.concatenate([jnp.ones((1,), jnp.int32), changed.astype(jnp.int32)])
    return jnp.cumsum(begins).astype(jnp.int32)

def normalize(tokens, norm_gain, generate):
    values32 = tokens.astype(jnp.float32)
    factor = lax.rsqrt(lax.optimization_barrier(jnp.mean(values32 * values32, axis=1, keepdims=True)) + EPS)
    gain = jnp.where(generate, norm_gain[1][None, :], norm_gain[0][None, :])
    return (values32 * factor * gain).astype(jnp.bfloat16)

def reference(tokens, norm_gain, w_query, w_key, w_value, w_out, modality, doc_ids):
    total = tokens.shape[0]
    generate = (modality == 1)[:, None]
    normed = normalize(tokens, norm_gain, generate)

    def project(weight):
        first = jnp.dot(normed, weight[0], preferred_element_type=jnp.float32)
        second = jnp.dot(normed, weight[1], preferred_element_type=jnp.float32)
        return jnp.where(generate, second, first).astype(jnp.bfloat16)
    query = project(w_query).reshape(total, Q_HEADS, HEAD_DIM)
    group = Q_HEADS // KV_HEADS
    keys32 = jnp.repeat(project(w_key).reshape(total, KV_HEADS, HEAD_DIM).astype(jnp.float32), group, axis=1)
    values32 = jnp.repeat(project(w_value).reshape(total, KV_HEADS, HEAD_DIM).astype(jnp.float32), group, axis=1)
    blocks = block_ids(modality, doc_ids)
    positions = jnp.arange(total, dtype=jnp.int32)
    height = math.gcd(total, 256)

    def one_block(number):
        begin = (number * height).astype(jnp.int32)
        rows = lax.dynamic_slice_in_dim(query, begin, height).astype(jnp.float32)
        query_pos = begin + jnp.arange(height, dtype=jnp.int32)
        query_doc = lax.dynamic_slice_in_dim(doc_ids, begin, height)
        query_block = lax.dynamic_slice_in_dim(blocks, begin, height)
        query_mod = lax.dynamic_slice_in_dim(modality, begin, height)
        seen = (query_doc[:, None] == doc_ids[None, :]) & ((positions[None, :] <= query_pos[:, None]) | (query_block[:, None] == blocks[None, :]) & (query_mod[:, None] == 1))
        scores = jnp.einsum('qhd,khd->hqk', rows, keys32) / math.sqrt(HEAD_DIM)
        scores = jnp.where(seen[None], scores, -1e+30)
        highest = lax.optimization_barrier(jnp.max(scores, axis=2, keepdims=True))
        weights = jnp.where(seen[None], jnp.exp(scores - highest), 0.0)
        weight_sum = lax.optimization_barrier(jnp.sum(weights, axis=2))
        probs = lax.optimization_barrier(weights.astype(jnp.bfloat16)).astype(jnp.float32)
        summed = jnp.einsum('hqk,khd->qhd', probs, values32)
        attended = summed / jnp.transpose(weight_sum)[:, :, None]
        return attended.reshape(height, Q_HEADS * HEAD_DIM).astype(jnp.bfloat16)
    attended = lax.map(one_block, jnp.arange(total // height, dtype=jnp.int32))
    attended = attended.reshape(total, Q_HEADS * HEAD_DIM)
    columns = Q_HEADS * HEAD_DIM // N_HEAD
    combined = jnp.zeros(tokens.shape, jnp.float32)
    for number in range(N_HEAD):
        piece = attended[:, number * columns:(number + 1) * columns]
        first = jnp.dot(piece, w_out[0][number * columns:(number + 1) * columns], preferred_element_type=jnp.float32)
        second = jnp.dot(piece, w_out[1][number * columns:(number + 1) * columns], preferred_element_type=jnp.float32)
        partial_sum = jnp.where(generate, second, first).astype(jnp.bfloat16)
        combined = combined + partial_sum.astype(jnp.float32)
    return combined.astype(jnp.bfloat16)
```

```python
import functools
import math

import jax
import jax.numpy as jnp
from jax import lax
from jax.experimental import pallas as pl
from jax.experimental.pallas import tpu as pltpu
from jax.sharding import PartitionSpec as P

HEAD_DIM = 128
KV_HEADS = 4
EPS = 1e-06
LOW = -1e30


def cross(x, axis, bit):
    size = lax.axis_size(axis)
    return lax.ppermute(x, axis, [(i, i ^ bit) for i in range(size)])


def bits_of(size):
    return [1 << i for i in range(size.bit_length() - 1)]


def gather_xor(x, axis):
    blocks = x[None]
    bits = bits_of(lax.axis_size(axis))
    for bit in reversed(bits):
        received = cross(blocks, axis, bit)
        blocks = jnp.concatenate([blocks, received])
    order = [0]
    for bit in reversed(bits):
        order = order + [d ^ bit for d in order]
    return blocks, order


def spans(modality, doc_ids, own_mod, own_doc, own_pos):
    changed = (modality[1:] != modality[:-1]) | (doc_ids[1:] != doc_ids[:-1])
    begins = jnp.concatenate([jnp.ones((1,), jnp.int32), changed.astype(jnp.int32)])
    blocks = jnp.cumsum(begins)
    own_block = lax.dynamic_slice_in_dim(blocks, own_pos[0], own_pos.shape[0])
    low = jnp.sum((doc_ids[None, :] < own_doc[:, None]).astype(jnp.int32), axis=1)
    end = jnp.sum((blocks[None, :] <= own_block[:, None]).astype(jnp.int32), axis=1) - 1
    return low, jnp.where(own_mod == 1, end, own_pos)


def attention_kernel(starts, limits, q_ref, kv_ref, low_ref, high_ref, o_ref, top, total, acc):
    count, size, _ = kv_ref.shape
    rows = q_ref.shape[0]
    heads = q_ref.shape[1] // HEAD_DIM
    kv_local = kv_ref.shape[2] // (2 * HEAD_DIM)
    repeat = heads // kv_local
    scale = 1.0 / math.sqrt(HEAD_DIM)
    top[...] = jnp.full_like(top, LOW)
    total[...] = jnp.zeros_like(total)
    acc[...] = jnp.zeros_like(acc)

    def visit(number, _):
        start = starts[number]

        @pl.when((start <= limits[1]) & (start + size > limits[0]))
        def _():
            key_pos = start + lax.broadcasted_iota(jnp.int32, (rows, size), 1)
            seen = (key_pos >= low_ref[...]) & (key_pos <= high_ref[...])
            for head in range(heads):
                g = head // repeat
                keys = kv_ref[number, :, g * HEAD_DIM : (g + 1) * HEAD_DIM]
                values = kv_ref[number, :, (kv_local + g) * HEAD_DIM : (kv_local + g + 1) * HEAD_DIM]
                query = q_ref[:, head * HEAD_DIM : (head + 1) * HEAD_DIM]
                scores = lax.dot_general(
                    query, keys, (((1,), (1,)), ((), ())), preferred_element_type=jnp.float32
                )
                scores = jnp.where(seen, scores * scale, LOW)
                old = top[head][:, :1]
                new = jnp.maximum(old, jnp.max(scores, axis=1, keepdims=True))
                weights = jnp.where(seen, jnp.exp(scores - new), 0.0)
                shrink = jnp.exp(old - new)
                total[head] = jnp.broadcast_to(
                    total[head][:, :1] * shrink + jnp.sum(weights, axis=1, keepdims=True),
                    (rows, HEAD_DIM),
                )
                top[head] = jnp.broadcast_to(new, (rows, HEAD_DIM))
                acc[head] = acc[head] * shrink + jnp.dot(
                    weights.astype(jnp.bfloat16), values, preferred_element_type=jnp.float32
                )

        return 0

    lax.fori_loop(0, count, visit, 0)
    for head in range(heads):
        o_ref[:, head * HEAD_DIM : (head + 1) * HEAD_DIM] = (acc[head] / total[head]).astype(
            jnp.bfloat16
        )


def attend(query, kv, starts, low, high):
    rows, width = query.shape
    heads = width // HEAD_DIM
    count, size, _ = kv.shape
    vmem = pl.BlockSpec(memory_space=pltpu.VMEM)
    smem = pl.BlockSpec(memory_space=pltpu.SMEM)
    limits = jnp.stack([low[0], high[-1]])
    return pl.pallas_call(
        attention_kernel,
        out_shape=jax.ShapeDtypeStruct((rows, width), jnp.bfloat16),
        in_specs=[smem, smem, vmem, vmem, vmem, vmem],
        out_specs=vmem,
        scratch_shapes=[
            pltpu.VMEM((heads, rows, HEAD_DIM), jnp.float32),
            pltpu.VMEM((heads, rows, HEAD_DIM), jnp.float32),
            pltpu.VMEM((heads, rows, HEAD_DIM), jnp.float32),
        ],
        cost_estimate=pl.CostEstimate(
            flops=4 * rows * count * size * width,
            bytes_accessed=2 * (2 * rows * width + kv.size),
            transcendentals=rows * count * size * heads,
        ),
        compiler_params=pltpu.CompilerParams(vmem_limit_bytes=32 * 1024 * 1024),
        name="attend",
    )(starts, limits, query, kv, low[:, None], high[:, None])


def body(tokens, norm_gain, w_query, w_key, w_value, w_out, modality, doc_ids):
    length, depth = tokens.shape
    n = lax.axis_size("seq")
    subs = lax.axis_size("sub")
    heads_over = lax.axis_size("head")
    z, s = lax.axis_index("seq"), lax.axis_index("sub")
    x, y = lax.axis_index("head"), lax.axis_index("grp")
    seq_bits = bits_of(n)
    width = depth // n

    kv_local = max(KV_HEADS // heads_over, 1)
    kv_first = x * KV_HEADS // heads_over
    key_cols = lax.dynamic_slice_in_dim(w_key, kv_first * HEAD_DIM, kv_local * HEAD_DIM, 2)
    value_cols = lax.dynamic_slice_in_dim(w_value, kv_first * HEAD_DIM, kv_local * HEAD_DIM, 2)
    q_cols = w_query.shape[2]
    kv_cols = 2 * kv_local * HEAD_DIM

    first_pos = (z * subs + s) * length
    own_mod = lax.dynamic_slice_in_dim(modality, first_pos, length)
    own_doc = lax.dynamic_slice_in_dim(doc_ids, first_pos, length)
    own_pos = first_pos + jnp.arange(length, dtype=jnp.int32)
    values32 = tokens.astype(jnp.float32)
    factor = lax.rsqrt(jnp.mean(values32 * values32, axis=1, keepdims=True) + EPS)
    gain = jnp.where((own_mod == 1)[:, None], norm_gain[1][None, :], norm_gain[0][None, :])
    normed = (values32 * factor * gain).astype(jnp.bfloat16)

    def columns(d):
        return lax.dynamic_slice_in_dim(normed, (z ^ d) * width, width, 1)

    order = sorted(range(1, n), key=lambda d: (-(d & 1), -d))
    blocks = {d: cross(columns(d), "seq", d) for d in order}
    blocks[0] = columns(0)
    order = order + [0]

    def share(weight):
        other = cross(weight, "sub", 1)
        both = jnp.where(
            s == 0,
            jnp.concatenate([weight, other], axis=1),
            jnp.concatenate([other, weight], axis=1),
        )
        return both.reshape(2 * width, weight.shape[2])

    w_kv_all = share(jnp.concatenate([key_cols, value_cols], axis=2))
    w_q_all = share(w_query)

    def split(block, mod, first):
        generate = (mod == first)[:, None]
        zero = jnp.zeros_like(block)
        return jnp.concatenate(
            [jnp.where(generate, block, zero), jnp.where(generate, zero, block)], axis=1
        )

    doubled = {}
    for d in order:
        mod = lax.dynamic_slice_in_dim(modality, ((z ^ d) * subs + s) * length, length)
        doubled[d] = split(blocks[d], mod, 0)

    def scatter(weight):
        sums = {d: jnp.dot(doubled[d], weight, preferred_element_type=jnp.float32) for d in order}
        for bit in seq_bits:
            for d in [d for d in order if d in sums and d & bit]:
                received = cross(sums.pop(d).astype(jnp.bfloat16), "seq", bit)
                sums[d ^ bit] = sums[d ^ bit] + received.astype(jnp.float32)
        return sums[0].astype(jnp.bfloat16)

    kv = scatter(w_kv_all)
    query = scatter(w_q_all)

    grps = lax.axis_size("grp")
    mine = lax.dynamic_index_in_dim(w_out, y, 0, keepdims=False)
    theirs = lax.dynamic_index_in_dim(w_out, 1 - y, 0, keepdims=False)
    near, out_order = gather_xor(mine, "seq")
    far = cross(near[1:], "grp", 1)
    far = jnp.concatenate([theirs[None], far])
    near_other = cross(near, "sub", 1)
    far_other = cross(far, "sub", 1)

    kv_all, kv_order = gather_xor(kv, "seq")
    kv_other = cross(kv_all, "sub", 1)
    starts = jnp.stack(
        [((z ^ d) * subs + s) * length for d in kv_order]
        + [((z ^ d) * subs + (1 - s)) * length for d in kv_order]
    ).astype(jnp.int32)
    low, high = spans(modality, doc_ids, own_mod, own_doc, own_pos)
    attended = attend(query, jnp.concatenate([kv_all, kv_other]), starts, low, high)

    both = split(attended, own_mod, y)
    near_half, far_half = jnp.split(both, 2, axis=1)

    def out(near_weight, far_weight):
        return (
            jnp.dot(near_half, near_weight, preferred_element_type=jnp.float32)
            + jnp.dot(far_half, far_weight, preferred_element_type=jnp.float32)
        ).astype(jnp.bfloat16)

    pieces = {}
    for place, d in enumerate(out_order):
        own = out(near[place], far[place])
        other = out(near_other[place], far_other[place])
        pieces[d] = jnp.where(
            s == 0, jnp.concatenate([own, other], axis=1), jnp.concatenate([other, own], axis=1)
        )
    stacked = jnp.stack([pieces[d] for d in range(n)])
    ordered = jnp.concatenate(
        [lax.dynamic_index_in_dim(stacked, z ^ c, 0, keepdims=False) for c in range(n)], axis=1
    )
    if heads_over == 2:
        half = depth // 2
        keep = lax.dynamic_slice_in_dim(ordered, x * half, half, 1)
        send = lax.dynamic_slice_in_dim(ordered, (1 - x) * half, half, 1)
        received = cross(send, "head", 1)
        return (keep.astype(jnp.float32) + received.astype(jnp.float32)).astype(jnp.bfloat16)
    return lax.psum_scatter(ordered, "head", scatter_dimension=1, tiled=True)


def solution(mesh):
    placed = (
        P(("grp", "seq", "sub"), None),
        P(),
        P(None, ("seq", "sub"), "head"),
        P(None, ("seq", "sub"), None),
        P(None, ("seq", "sub"), None),
        P(None, "head", ("seq", "sub")),
        P("grp"),
        P("grp"),
    )
    return jax.shard_map(
        body,
        mesh=mesh,
        in_specs=placed,
        out_specs=P(("grp", "seq", "sub"), "head"),
        check_vma=False,
    )
```

```python
import functools
import math

import jax
import jax.numpy as jnp
from jax import lax
from jax.experimental import pallas as pl
from jax.experimental.pallas import tpu as pltpu
from jax.sharding import PartitionSpec as P

HEAD_DIM = 128
KV_HEADS = 4
EPS = 1e-06
LOW = -1e30


def move(x, axis, pairs):
    return lax.ppermute(x, axis, pairs)


def swap(x, axis):
    return lax.ppermute(x, axis, [(0, 1), (1, 0)])


def from_ahead(x, axis, offset):
    size = lax.axis_size(axis)
    return lax.ppermute(x, axis, [((i + offset) % size, i) for i in range(size)])


def spans(modality, doc_ids, own_mod, own_doc, own_pos):
    changed = (modality[1:] != modality[:-1]) | (doc_ids[1:] != doc_ids[:-1])
    begins = jnp.concatenate([jnp.ones((1,), jnp.int32), changed.astype(jnp.int32)])
    blocks = jnp.cumsum(begins)
    own_block = lax.dynamic_slice_in_dim(blocks, own_pos[0], own_pos.shape[0])
    low = jnp.sum((doc_ids[None, :] < own_doc[:, None]).astype(jnp.int32), axis=1)
    end = jnp.sum((blocks[None, :] <= own_block[:, None]).astype(jnp.int32), axis=1) - 1
    return low, jnp.where(own_mod == 1, end, own_pos)


def attention_kernel(starts, limits, q_ref, kv_ref, low_ref, high_ref, o_ref, top, total, acc):
    count, size, _ = kv_ref.shape
    rows = q_ref.shape[0]
    heads = q_ref.shape[1] // HEAD_DIM
    kv_local = kv_ref.shape[2] // (2 * HEAD_DIM)
    repeat = heads // kv_local
    scale = 1.0 / math.sqrt(HEAD_DIM)
    top[...] = jnp.full_like(top, LOW)
    total[...] = jnp.zeros_like(total)
    acc[...] = jnp.zeros_like(acc)

    def visit(number, _):
        start = starts[number]

        @pl.when((start <= limits[1]) & (start + size > limits[0]))
        def _():
            key_pos = start + lax.broadcasted_iota(jnp.int32, (rows, size), 1)
            seen = (key_pos >= low_ref[...]) & (key_pos <= high_ref[...])
            for head in range(heads):
                g = head // repeat
                keys = kv_ref[number, :, g * HEAD_DIM : (g + 1) * HEAD_DIM]
                values = kv_ref[number, :, (kv_local + g) * HEAD_DIM : (kv_local + g + 1) * HEAD_DIM]
                query = q_ref[:, head * HEAD_DIM : (head + 1) * HEAD_DIM]
                scores = lax.dot_general(
                    query, keys, (((1,), (1,)), ((), ())), preferred_element_type=jnp.float32
                )
                scores = jnp.where(seen, scores * scale, LOW)
                old = top[head][:, :1]
                new = jnp.maximum(old, jnp.max(scores, axis=1, keepdims=True))
                weights = jnp.where(seen, jnp.exp(scores - new), 0.0)
                shrink = jnp.exp(old - new)
                total[head] = jnp.broadcast_to(
                    total[head][:, :1] * shrink + jnp.sum(weights, axis=1, keepdims=True),
                    (rows, HEAD_DIM),
                )
                top[head] = jnp.broadcast_to(new, (rows, HEAD_DIM))
                acc[head] = acc[head] * shrink + jnp.dot(
                    weights.astype(jnp.bfloat16), values, preferred_element_type=jnp.float32
                )

        return 0

    lax.fori_loop(0, count, visit, 0)
    for head in range(heads):
        o_ref[:, head * HEAD_DIM : (head + 1) * HEAD_DIM] = (acc[head] / total[head]).astype(
            jnp.bfloat16
        )


def attend(query, kv, starts, low, high):
    rows, width = query.shape
    heads = width // HEAD_DIM
    count, size, _ = kv.shape
    vmem = pl.BlockSpec(memory_space=pltpu.VMEM)
    smem = pl.BlockSpec(memory_space=pltpu.SMEM)
    limits = jnp.stack([low[0], high[-1]])
    return pl.pallas_call(
        attention_kernel,
        out_shape=jax.ShapeDtypeStruct((rows, width), jnp.bfloat16),
        in_specs=[smem, smem, vmem, vmem, vmem, vmem],
        out_specs=vmem,
        scratch_shapes=[
            pltpu.VMEM((heads, rows, HEAD_DIM), jnp.float32),
            pltpu.VMEM((heads, rows, HEAD_DIM), jnp.float32),
            pltpu.VMEM((heads, rows, HEAD_DIM), jnp.float32),
        ],
        cost_estimate=pl.CostEstimate(
            flops=4 * rows * count * size * width,
            bytes_accessed=2 * (2 * rows * width + kv.size),
            transcendentals=rows * count * size * heads,
        ),
        compiler_params=pltpu.CompilerParams(vmem_limit_bytes=32 * 1024 * 1024),
        name="attend",
    )(starts, limits, query, kv, low[:, None], high[:, None])


def project_kernel(turns, a_ref, near_ref, far_ref, w_near, w_far, o_ref):
    a = a_ref[...]
    zero = jnp.zeros_like(a)
    near = jnp.where(near_ref[...] != 0, a, zero)
    far = jnp.where(far_ref[...] != 0, a, zero)
    o_ref[0] = (
        jnp.dot(near, w_near[0], preferred_element_type=jnp.float32)
        + jnp.dot(far, w_far[0], preferred_element_type=jnp.float32)
    ).astype(jnp.bfloat16)


def project(attended, mod, first, w_near, w_far, turns):
    rows, depth = attended.shape
    count, width = turns.shape[0], w_near.shape[2]
    near = (mod == first).astype(jnp.bfloat16)[:, None]
    whole = lambda i, t: (0, 0)
    piece = lambda i, t: (t[i], 0, 0)
    return pl.pallas_call(
        project_kernel,
        out_shape=jax.ShapeDtypeStruct((count, rows, width), jnp.bfloat16),
        grid_spec=pltpu.PrefetchScalarGridSpec(
            num_scalar_prefetch=1,
            grid=(count,),
            in_specs=[
                pl.BlockSpec((rows, depth), whole),
                pl.BlockSpec((rows, 1), whole),
                pl.BlockSpec((rows, 1), whole),
                pl.BlockSpec((1, depth, width), piece),
                pl.BlockSpec((1, depth, width), piece),
            ],
            out_specs=pl.BlockSpec((1, rows, width), lambda i, t: (i, 0, 0)),
        ),
        cost_estimate=pl.CostEstimate(
            flops=4 * count * rows * depth * width,
            bytes_accessed=4 * count * depth * width + 2 * count * rows * width,
            transcendentals=0,
        ),
        compiler_params=pltpu.CompilerParams(vmem_limit_bytes=32 * 1024 * 1024),
        name="project",
    )(turns, attended, near, 1 - near, w_near, w_far)


def body(tokens, norm_gain, w_query, w_key, w_value, w_out, modality, doc_ids):
    length, depth = tokens.shape
    n = lax.axis_size("seq")
    subs = lax.axis_size("sub")
    heads_over = lax.axis_size("head")
    z, s = lax.axis_index("seq"), lax.axis_index("sub")
    x, y = lax.axis_index("head"), lax.axis_index("grp")
    width = depth // n
    rightward = [[(i, i + 1) for i in range(n - 1) if i <= k] for k in range(n - 1)]
    leftward = [[(i, i - 1) for i in range(1, n) if i >= n - 1 - k] for k in range(n - 1)]

    kv_local = max(KV_HEADS // heads_over, 1)
    kv_first = x * KV_HEADS // heads_over
    key_cols = lax.dynamic_slice_in_dim(w_key, kv_first * HEAD_DIM, kv_local * HEAD_DIM, 2)
    value_cols = lax.dynamic_slice_in_dim(w_value, kv_first * HEAD_DIM, kv_local * HEAD_DIM, 2)

    def turned(r):
        return (z + r) % n

    def part_of(array, place, core):
        return lax.dynamic_slice_in_dim(array, (place * subs + core) * length, length)

    first_pos = (z * subs + s) * length
    own_mod, own_doc = part_of(modality, z, s), part_of(doc_ids, z, s)
    own_pos = first_pos + jnp.arange(length, dtype=jnp.int32)
    with jax.named_scope("norm"):
        values32 = tokens.astype(jnp.float32)
        factor = lax.rsqrt(jnp.mean(values32 * values32, axis=1, keepdims=True) + EPS)
        gain = jnp.where((own_mod == 1)[:, None], norm_gain[1][None, :], norm_gain[0][None, :])
        normed = (values32 * factor * gain).astype(jnp.bfloat16)

    with jax.named_scope("pick_out"):
        mine = lax.dynamic_index_in_dim(w_out, y, 0, keepdims=False)
        theirs = lax.dynamic_index_in_dim(w_out, 1 - y, 0, keepdims=False)
    to_right, to_left = [], []
    send_right, send_left = mine, mine
    for k in range(n - 1):
        with jax.named_scope(f"out_right_{k}"):
            send_right = move(send_right, "seq", [(i, i + 1) for i in range(k, n - 1)])
        with jax.named_scope(f"out_left_{k}"):
            send_left = move(send_left, "seq", [(i, i - 1) for i in range(1, n - k)])
        to_right.append(send_right)
        to_left.append(send_left)
    near, far = [mine], [theirs]
    for r in range(1, n):
        near.append(jnp.where(z + r < n, to_left[r - 1], to_right[n - 1 - r]))
    near_all = jnp.stack(near)
    for r in range(1, n):
        with jax.named_scope(f"out_pair_{r}"):
            far.append(swap(near[r], "grp"))
    far_all = jnp.stack(far)

    def columns(r):
        return lax.dynamic_slice_in_dim(normed, turned(r) * width, width, 1)

    order = sorted(range(1, n), key=lambda r: -max(r, n - r)) + [0]
    blocks = {0: columns(0)}
    for r in order[:-1]:
        with jax.named_scope(f"tokens_{r}"):
            blocks[r] = from_ahead(columns(n - r), "seq", r)

    def share(weight):
        other = swap(weight, "sub")
        both = jnp.where(
            s == 0,
            jnp.concatenate([weight, other], axis=1),
            jnp.concatenate([other, weight], axis=1),
        )
        return both.reshape(2 * width, weight.shape[2])

    with jax.named_scope("share_kv"):
        w_kv_all = share(jnp.concatenate([key_cols, value_cols], axis=2))
    with jax.named_scope("share_q"):
        w_q_all = share(w_query)

    def split(block, mod):
        generate = (mod == 1)[:, None]
        zero = jnp.zeros_like(block)
        return jnp.concatenate(
            [jnp.where(generate, zero, block), jnp.where(generate, block, zero)], axis=1
        )

    doubled = {r: split(blocks[r], part_of(modality, turned(r), s)) for r in order}

    def scatter(weight, name):
        parts = {r: jnp.dot(doubled[r], weight, preferred_element_type=jnp.float32) for r in order}
        right = left = None
        for k in range(n - 1):
            send_right, send_left = parts[n - 1 - k], parts[k + 1]
            if k:
                send_right = send_right + right.astype(jnp.float32)
                send_left = send_left + left.astype(jnp.float32)
            with jax.named_scope(f"{name}_right_{k}"):
                right = move(send_right.astype(jnp.bfloat16), "seq", rightward[k])
            with jax.named_scope(f"{name}_left_{k}"):
                left = move(send_left.astype(jnp.bfloat16), "seq", leftward[k])
        return (parts[0] + right.astype(jnp.float32) + left.astype(jnp.float32)).astype(jnp.bfloat16)

    kv = scatter(w_kv_all, "kv")
    query = scatter(w_q_all, "q")

    same, beside = [kv], []
    for r in range(1, n):
        with jax.named_scope(f"kv_all_{r}"):
            same.append(from_ahead(kv, "seq", r))
    with jax.named_scope("kv_core_0"):
        beside.append(swap(kv, "sub"))
    with jax.named_scope("kv_core_1"):
        others = swap(jnp.stack(same[1:]), "sub")
    kv_all = jnp.concatenate([jnp.stack(same), beside[0][None], others])
    starts = jnp.stack(
        [(turned(r) * subs + s) * length for r in range(n)]
        + [(turned(r) * subs + (1 - s)) * length for r in range(n)]
    ).astype(jnp.int32)
    low, high = spans(modality, doc_ids, own_mod, own_doc, own_pos)
    attended = attend(query, kv_all, starts, low, high)

    with jax.named_scope("attended_core"):
        beside = swap(attended, "sub")
    beside_mod = part_of(modality, z, 1 - s)
    if heads_over != 2:
        places = jnp.arange(n, dtype=jnp.int32)
        turns = (places - z + n) % n
        ours = project(attended, own_mod, y, near_all, far_all, turns)
        sibling = swap(project(beside, beside_mod, y, near_all, far_all, turns), "sub")
        pair = jnp.where(s == 0, jnp.stack([ours, sibling], 1), jnp.stack([sibling, ours], 1))
        wide = jnp.transpose(pair, (2, 0, 1, 3)).reshape(length, depth)
        return lax.psum_scatter(wide, "head", scatter_dimension=1, tiled=True)

    half = jnp.arange(n // 2, dtype=jnp.int32)
    turns_keep = (x * (n // 2) + half - z + n) % n
    turns_send = ((1 - x) * (n // 2) + half - z + n) % n

    def add(a, b):
        return (a.astype(jnp.float32) + b.astype(jnp.float32)).astype(jnp.bfloat16)

    with jax.named_scope("send_ours"):
        got_ours = swap(project(attended, own_mod, y, near_all, far_all, turns_send), "head")
    with jax.named_scope("send_beside"):
        got_beside = swap(project(beside, beside_mod, y, near_all, far_all, turns_send), "head")
    ours = add(project(attended, own_mod, y, near_all, far_all, turns_keep), got_ours)
    theirs = add(project(beside, beside_mod, y, near_all, far_all, turns_keep), got_beside)
    with jax.named_scope("result_core"):
        sibling = swap(theirs, "sub")
    pair = jnp.where(s == 0, jnp.stack([ours, sibling], 1), jnp.stack([sibling, ours], 1))
    return jnp.transpose(pair, (2, 0, 1, 3)).reshape(length, depth // 2)


def solution(mesh):
    placed = (
        P(("grp", "seq", "sub"), None),
        P(),
        P(None, ("seq", "sub"), "head"),
        P(None, ("seq", "sub"), None),
        P(None, ("seq", "sub"), None),
        P(None, "head", ("seq", "sub")),
        P("grp"),
        P("grp"),
    )
    return jax.shard_map(
        body,
        mesh=mesh,
        in_specs=placed,
        out_specs=P(("grp", "seq", "sub"), "head"),
        check_vma=False,
    )
```

```python
import functools
import math

import jax
import jax.numpy as jnp
from jax import lax
from jax.experimental import pallas as pl
from jax.experimental.pallas import tpu as pltpu
from jax.sharding import PartitionSpec as P

HEAD_DIM = 128
KV_HEADS = 4
EPS = 1e-06
LOW = -1e30


def swap(x, axis):
    return lax.ppermute(x, axis, [(0, 1), (1, 0)])


def from_ahead(x, axis, offset):
    size = lax.axis_size(axis)
    return lax.ppermute(x, axis, [((i + offset) % size, i) for i in range(size)])


def after(value, *done):
    return lax.optimization_barrier((value, *done))[0]


def spans(modality, doc_ids, own_mod, own_doc, own_pos):
    changed = (modality[1:] != modality[:-1]) | (doc_ids[1:] != doc_ids[:-1])
    begins = jnp.concatenate([jnp.ones((1,), jnp.int32), changed.astype(jnp.int32)])
    blocks = jnp.cumsum(begins)
    own_block = lax.dynamic_slice_in_dim(blocks, own_pos[0], own_pos.shape[0])
    low = jnp.sum((doc_ids[None, :] < own_doc[:, None]).astype(jnp.int32), axis=1)
    end = jnp.sum((blocks[None, :] <= own_block[:, None]).astype(jnp.int32), axis=1) - 1
    return low, jnp.where(own_mod == 1, end, own_pos)


def attention_kernel(starts, limits, q_ref, kv_ref, low_ref, high_ref, o_ref, top, total, acc):
    count, size, _ = kv_ref.shape
    rows = q_ref.shape[0]
    heads = q_ref.shape[1] // HEAD_DIM
    kv_local = kv_ref.shape[2] // (2 * HEAD_DIM)
    repeat = heads // kv_local
    scale = 1.0 / math.sqrt(HEAD_DIM)
    top[...] = jnp.full_like(top, LOW)
    total[...] = jnp.zeros_like(total)
    acc[...] = jnp.zeros_like(acc)

    def visit(number, _):
        start = starts[number]

        @pl.when((start <= limits[1]) & (start + size > limits[0]))
        def _():
            key_pos = start + lax.broadcasted_iota(jnp.int32, (rows, size), 1)
            seen = (key_pos >= low_ref[...]) & (key_pos <= high_ref[...])
            for head in range(heads):
                g = head // repeat
                keys = kv_ref[number, :, g * HEAD_DIM : (g + 1) * HEAD_DIM]
                values = kv_ref[number, :, (kv_local + g) * HEAD_DIM : (kv_local + g + 1) * HEAD_DIM]
                query = q_ref[:, head * HEAD_DIM : (head + 1) * HEAD_DIM]
                scores = lax.dot_general(
                    query, keys, (((1,), (1,)), ((), ())), preferred_element_type=jnp.float32
                )
                scores = jnp.where(seen, scores * scale, LOW)
                old = top[head][:, :1]
                new = jnp.maximum(old, jnp.max(scores, axis=1, keepdims=True))
                weights = jnp.where(seen, jnp.exp(scores - new), 0.0)
                shrink = jnp.exp(old - new)
                total[head] = jnp.broadcast_to(
                    total[head][:, :1] * shrink + jnp.sum(weights, axis=1, keepdims=True),
                    (rows, HEAD_DIM),
                )
                top[head] = jnp.broadcast_to(new, (rows, HEAD_DIM))
                acc[head] = acc[head] * shrink + jnp.dot(
                    weights.astype(jnp.bfloat16), values, preferred_element_type=jnp.float32
                )

        return 0

    lax.fori_loop(0, count, visit, 0)
    for head in range(heads):
        o_ref[:, head * HEAD_DIM : (head + 1) * HEAD_DIM] = (acc[head] / total[head]).astype(
            jnp.bfloat16
        )


def attend(query, kv, starts, low, high):
    rows, width = query.shape
    heads = width // HEAD_DIM
    count, size, _ = kv.shape
    vmem = pl.BlockSpec(memory_space=pltpu.VMEM)
    smem = pl.BlockSpec(memory_space=pltpu.SMEM)
    limits = jnp.stack([low[0], high[-1]])
    return pl.pallas_call(
        attention_kernel,
        out_shape=jax.ShapeDtypeStruct((rows, width), jnp.bfloat16),
        in_specs=[smem, smem, vmem, vmem, vmem, vmem],
        out_specs=vmem,
        scratch_shapes=[
            pltpu.VMEM((heads, rows, HEAD_DIM), jnp.float32),
            pltpu.VMEM((heads, rows, HEAD_DIM), jnp.float32),
            pltpu.VMEM((heads, rows, HEAD_DIM), jnp.float32),
        ],
        cost_estimate=pl.CostEstimate(
            flops=4 * rows * count * size * width,
            bytes_accessed=2 * (2 * rows * width + kv.size),
            transcendentals=rows * count * size * heads,
        ),
        compiler_params=pltpu.CompilerParams(vmem_limit_bytes=32 * 1024 * 1024),
        name="attend",
    )(starts, limits, query, kv, low[:, None], high[:, None])


def project_kernel(turns, places, ours_ref, beside_ref, ours_near, beside_near, own_ref, *rest):
    steps = (len(rest) - 4) // 4
    near = rest[: 2 * steps]
    far = rest[2 * steps : 4 * steps]
    o_ours, o_beside, held, arrived = rest[4 * steps :]
    count = turns.shape[0]
    size = steps + 1
    place, first = places[0], places[1]

    def wanted(turn):
        slot = jnp.int32(-1)
        for i in range(count):
            slot = jnp.where(turns[i] == turn, i, slot)
        return slot

    def fetch(source, kind, turn, valid):
        slot = wanted(turn)

        @pl.when(valid & (slot >= 0))
        def _():
            at = jnp.maximum(slot, 0)
            pltpu.make_async_copy(source, held.at[kind, at], arrived.at[kind, at]).start()

    fetch(own_ref.at[first], 0, 0, True)
    fetch(own_ref.at[1 - first], 1, 0, True)
    for k in range(steps):
        for kind, refs in ((0, near), (1, far)):
            fetch(refs[k], kind, k + 1, place + k + 1 < size)
            fetch(refs[steps + k], kind, size - 1 - k, place >= k + 1)

    contract = (((1,), (1,)), ((), ()))
    halves = []
    for a_ref, near_ref, o_ref in ((ours_ref, ours_near, o_ours), (beside_ref, beside_near, o_beside)):
        a = a_ref[...]
        mine = near_ref[...] != 0
        zero = jnp.zeros_like(a)
        halves.append((jnp.where(mine, a, zero), jnp.where(mine, zero, a), o_ref))
    for i in range(count):
        for kind in range(2):
            pltpu.make_async_copy(own_ref.at[0], held.at[kind, i], arrived.at[kind, i]).wait()
        for a_near, a_far, o_ref in halves:
            o_ref[i] = (
                lax.dot_general(a_near, held[0, i], contract, preferred_element_type=jnp.float32)
                + lax.dot_general(a_far, held[1, i], contract, preferred_element_type=jnp.float32)
            ).astype(jnp.bfloat16)


def project(ours, beside, ours_near, beside_near, weights, turns, places):
    rows, depth = ours.shape
    count = turns.shape[0]
    width = weights[0].shape[1]
    vmem = pl.BlockSpec(memory_space=pltpu.VMEM)
    smem = pl.BlockSpec(memory_space=pltpu.SMEM)
    shape = jax.ShapeDtypeStruct((count, rows, width), jnp.bfloat16)
    return pl.pallas_call(
        project_kernel,
        out_shape=(shape, shape),
        in_specs=[smem, smem] + [vmem] * 4 + [pl.BlockSpec(memory_space=pl.ANY)] * len(weights),
        out_specs=(vmem, vmem),
        scratch_shapes=[
            pltpu.VMEM((2, count, width, depth), jnp.bfloat16),
            pltpu.SemaphoreType.DMA((2, count)),
        ],
        cost_estimate=pl.CostEstimate(
            flops=8 * count * rows * depth * width,
            bytes_accessed=4 * count * depth * width + 4 * count * rows * width,
            transcendentals=0,
        ),
        compiler_params=pltpu.CompilerParams(vmem_limit_bytes=32 * 1024 * 1024),
        name="project",
    )(turns, places, ours, beside, ours_near[:, None], beside_near[:, None], *weights)


def body(tokens, norm_gain, w_query, w_key, w_value, w_out, modality, doc_ids):
    length, depth = tokens.shape
    n = lax.axis_size("seq")
    subs = lax.axis_size("sub")
    heads_over = lax.axis_size("head")
    z, s = lax.axis_index("seq"), lax.axis_index("sub")
    x, y = lax.axis_index("head"), lax.axis_index("grp")
    width = depth // n
    steps = range(n - 1)

    kv_local = max(KV_HEADS // heads_over, 1)
    kv_first = x * KV_HEADS // heads_over
    key_cols = lax.dynamic_slice_in_dim(w_key, kv_first * HEAD_DIM, kv_local * HEAD_DIM, 2)
    value_cols = lax.dynamic_slice_in_dim(w_value, kv_first * HEAD_DIM, kv_local * HEAD_DIM, 2)
    w_out = jnp.swapaxes(w_out, 1, 2)

    def turned(r):
        return (z + r) % n

    def part_of(array, place, core):
        return lax.dynamic_slice_in_dim(array, (place * subs + core) * length, length)

    first_pos = (z * subs + s) * length
    own_mod, own_doc = part_of(modality, z, s), part_of(doc_ids, z, s)
    own_pos = first_pos + jnp.arange(length, dtype=jnp.int32)
    with jax.named_scope("norm"):
        values32 = tokens.astype(jnp.float32)
        factor = lax.rsqrt(jnp.mean(values32 * values32, axis=1, keepdims=True) + EPS)
        gain = jnp.where((own_mod == 1)[:, None], norm_gain[1][None, :], norm_gain[0][None, :])
        normed = (values32 * factor * gain).astype(jnp.bfloat16)

    def columns(r):
        return lax.dynamic_slice_in_dim(normed, turned(r) * width, width, 1)

    order = sorted(range(1, n), key=lambda r: -max(r, n - r)) + [0]
    blocks = {0: columns(0)}
    for r in order[:-1]:
        with jax.named_scope(f"tokens_{r}"):
            blocks[r] = from_ahead(columns(n - r), "seq", r)

    mine = lax.dynamic_index_in_dim(w_out, y, 0, keepdims=False)
    right, left = [], []

    def step_out(k, *done):
        send_right, send_left = (right[-1], left[-1]) if k else (mine, mine)
        if done:
            send_right, send_left = after((send_right, send_left), *done)
        with jax.named_scope(f"out_right_{k}"):
            right.append(lax.ppermute(send_right, "seq", [(i, i + 1) for i in range(k, n - 1)]))
        with jax.named_scope(f"out_left_{k}"):
            left.append(lax.ppermute(send_left, "seq", [(i, i - 1) for i in range(1, n - k)]))

    step_out(0)

    def share(weight):
        other = swap(weight, "sub")
        both = jnp.where(
            s == 0,
            jnp.concatenate([weight, other], axis=1),
            jnp.concatenate([other, weight], axis=1),
        )
        return both.reshape(2 * width, weight.shape[2])

    with jax.named_scope("share_kv"):
        w_kv_all = share(jnp.concatenate([key_cols, value_cols], axis=2))
    with jax.named_scope("share_q"):
        w_q_all = share(w_query)

    def split(block, mod):
        generate = (mod == 1)[:, None]
        zero = jnp.zeros_like(block)
        return jnp.concatenate(
            [jnp.where(generate, zero, block), jnp.where(generate, block, zero)], axis=1
        )

    doubled = {r: split(blocks[r], part_of(modality, turned(r), s)) for r in order}
    low, high = spans(modality, doc_ids, own_mod, own_doc, own_pos)
    w_kv_all, w_q_all, low, high = lax.optimization_barrier((w_kv_all, w_q_all, low, high))

    class Scatter:
        def __init__(self, weight, name):
            self.parts = {
                r: jnp.dot(doubled[r], weight, preferred_element_type=jnp.float32) for r in order
            }
            self.name = name
            self.got = None

        def sends(self, k):
            pair = self.parts[n - 1 - k], self.parts[k + 1]
            if k:
                pair = tuple(a + b.astype(jnp.float32) for a, b in zip(pair, self.got))
            return tuple(a.astype(jnp.bfloat16) for a in pair)

        def step(self, k, pair):
            with jax.named_scope(f"{self.name}_right_{k}"):
                to_right = lax.ppermute(pair[0], "seq", [(i, i + 1) for i in range(min(k + 1, n - 1))])
            with jax.named_scope(f"{self.name}_left_{k}"):
                to_left = lax.ppermute(
                    pair[1], "seq", [(i, i - 1) for i in range(max(n - 1 - k, 1), n)]
                )
            self.got = lax.optimization_barrier((to_right, to_left))

        def result(self):
            total = self.parts[0] + self.got[0].astype(jnp.float32) + self.got[1].astype(jnp.float32)
            return total.astype(jnp.bfloat16)

    kv_sum, q_sum = Scatter(w_kv_all, "kv"), Scatter(w_q_all, "q")
    kv_pair, q_pair = lax.optimization_barrier((kv_sum.sends(0), q_sum.sends(0)))
    kv_sum.step(0, kv_pair)
    q_sum.step(0, q_pair)
    if n > 2:
        step_out(1, q_pair)
    for k in range(1, n - 1):
        kv_pair = lax.optimization_barrier(kv_sum.sends(k))
        kv_sum.step(k, kv_pair)
        q_pair = after(q_sum.sends(k), kv_sum.got if k < n - 2 else kv_pair)
        q_sum.step(k, q_pair)
        if k + 1 < n - 1:
            step_out(k + 1, q_pair)
    kv = kv_sum.result()

    same = [kv]
    for r in range(1, n):
        with jax.named_scope(f"kv_all_{r}"):
            same.append(from_ahead(kv, "seq", r))
    with jax.named_scope("kv_core_0"):
        beside_0 = swap(kv, "sub")
    with jax.named_scope("kv_core_1"):
        others = swap(jnp.stack(same[1:]), "sub")
    kv_all = jnp.concatenate([jnp.stack(same), beside_0[None], others])
    query = q_sum.result()

    pairs = []
    for k in steps:
        for name, received, there in (
            ("left", left[k], range(n - 1 - k)),
            ("right", right[k], range(k + 1, n)),
        ):
            hops = [(i, i + n) for i in there] + [(i + n, i) for i in there]
            with jax.named_scope(f"out_pair_{name}_{k}"):
                pairs.append(lax.ppermute(received, ("grp", "seq"), hops))
    weights = [w_out] + left + right + pairs[0::2] + pairs[1::2]

    starts = jnp.stack(
        [(turned(r) * subs + s) * length for r in range(n)]
        + [(turned(r) * subs + (1 - s)) * length for r in range(n)]
    ).astype(jnp.int32)
    attended = attend(query, kv_all, starts, low, high)

    with jax.named_scope("attended_core"):
        beside = swap(attended, "sub")
    ours_near = (own_mod == y).astype(jnp.bfloat16)
    beside_near = (part_of(modality, z, 1 - s) == y).astype(jnp.bfloat16)
    places = jnp.stack([z, y]).astype(jnp.int32)

    def out(columns):
        turns = ((columns - z + n) % n).astype(jnp.int32)
        return project(attended, beside, ours_near, beside_near, weights, turns, places)

    def placed(ours, theirs):
        with jax.named_scope("result_core"):
            sibling = swap(theirs, "sub")
        pair = jnp.where(s == 0, jnp.stack([ours, sibling], 1), jnp.stack([sibling, ours], 1))
        return jnp.transpose(pair, (2, 0, 1, 3)).reshape(length, -1)

    if heads_over != 2:
        wide = placed(*out(jnp.arange(n)))
        return lax.psum_scatter(wide, "head", scatter_dimension=1, tiled=True)

    half = jnp.arange(n // 2)

    def add(a, b):
        return (a.astype(jnp.float32) + b.astype(jnp.float32)).astype(jnp.bfloat16)

    send_ours, send_beside = out((1 - x) * (n // 2) + half)
    with jax.named_scope("send_beside"):
        got_beside = swap(send_beside, "head")
    with jax.named_scope("send_ours"):
        got_ours = swap(send_ours, "head")
    keep_ours, keep_beside = out(x * (n // 2) + half)
    return placed(add(keep_ours, got_ours), add(keep_beside, got_beside))


def solution(mesh):
    placed = (
        P(("grp", "seq", "sub"), None),
        P(),
        P(None, ("seq", "sub"), "head"),
        P(None, ("seq", "sub"), None),
        P(None, ("seq", "sub"), None),
        P(None, "head", ("seq", "sub")),
        P("grp"),
        P("grp"),
    )
    return jax.shard_map(
        body,
        mesh=mesh,
        in_specs=placed,
        out_specs=P(("grp", "seq", "sub"), "head"),
        check_vma=False,
    )
```

```python
import functools
import math

import jax
import jax.numpy as jnp
from jax import lax
from jax.experimental import pallas as pl
from jax.experimental.pallas import tpu as pltpu
from jax.sharding import PartitionSpec as P

HEAD_DIM = 128
KV_HEADS = 4
EPS = 1e-06
LOW = -1e30


def swap(x, axis):
    return lax.ppermute(x, axis, [(0, 1), (1, 0)])


def from_ahead(x, axis, offset):
    size = lax.axis_size(axis)
    return lax.ppermute(x, axis, [((i + offset) % size, i) for i in range(size)])


def after(value, *done):
    return lax.optimization_barrier((value, *done))[0]


def spans(modality, doc_ids, own_mod, own_doc, own_pos):
    changed = (modality[1:] != modality[:-1]) | (doc_ids[1:] != doc_ids[:-1])
    begins = jnp.concatenate([jnp.ones((1,), jnp.int32), changed.astype(jnp.int32)])
    blocks = jnp.cumsum(begins)
    own_block = lax.dynamic_slice_in_dim(blocks, own_pos[0], own_pos.shape[0])
    low = jnp.sum((doc_ids[None, :] < own_doc[:, None]).astype(jnp.int32), axis=1)
    end = jnp.sum((blocks[None, :] <= own_block[:, None]).astype(jnp.int32), axis=1) - 1
    return low, jnp.where(own_mod == 1, end, own_pos)


def attention_kernel(starts, limits, q_ref, kv_ref, low_ref, high_ref, o_ref, top, total, acc):
    count, size, _ = kv_ref.shape
    rows = q_ref.shape[0]
    heads = q_ref.shape[1] // HEAD_DIM
    kv_local = kv_ref.shape[2] // (2 * HEAD_DIM)
    repeat = heads // kv_local
    scale = 1.0 / math.sqrt(HEAD_DIM)
    top[...] = jnp.full_like(top, LOW)
    total[...] = jnp.zeros_like(total)
    acc[...] = jnp.zeros_like(acc)

    def visit(number, _):
        start = starts[number]

        @pl.when((start <= limits[1]) & (start + size > limits[0]))
        def _():
            key_pos = start + lax.broadcasted_iota(jnp.int32, (rows, size), 1)
            seen = (key_pos >= low_ref[...]) & (key_pos <= high_ref[...])
            for head in range(heads):
                g = head // repeat
                keys = kv_ref[number, :, g * HEAD_DIM : (g + 1) * HEAD_DIM]
                values = kv_ref[number, :, (kv_local + g) * HEAD_DIM : (kv_local + g + 1) * HEAD_DIM]
                query = q_ref[:, head * HEAD_DIM : (head + 1) * HEAD_DIM]
                scores = lax.dot_general(
                    query, keys, (((1,), (1,)), ((), ())), preferred_element_type=jnp.float32
                )
                scores = jnp.where(seen, scores * scale, LOW)
                old = top[head][:, :1]
                new = jnp.maximum(old, jnp.max(scores, axis=1, keepdims=True))
                weights = jnp.where(seen, jnp.exp(scores - new), 0.0)
                shrink = jnp.exp(old - new)
                total[head] = jnp.broadcast_to(
                    total[head][:, :1] * shrink + jnp.sum(weights, axis=1, keepdims=True),
                    (rows, HEAD_DIM),
                )
                top[head] = jnp.broadcast_to(new, (rows, HEAD_DIM))
                acc[head] = acc[head] * shrink + jnp.dot(
                    weights.astype(jnp.bfloat16), values, preferred_element_type=jnp.float32
                )

        return 0

    lax.fori_loop(0, count, visit, 0)
    for head in range(heads):
        o_ref[:, head * HEAD_DIM : (head + 1) * HEAD_DIM] = (acc[head] / total[head]).astype(
            jnp.bfloat16
        )


def attend(query, kv, starts, low, high):
    rows, width = query.shape
    heads = width // HEAD_DIM
    count, size, _ = kv.shape
    vmem = pl.BlockSpec(memory_space=pltpu.VMEM)
    smem = pl.BlockSpec(memory_space=pltpu.SMEM)
    limits = jnp.stack([low[0], high[-1]])
    return pl.pallas_call(
        attention_kernel,
        out_shape=jax.ShapeDtypeStruct((rows, width), jnp.bfloat16),
        in_specs=[smem, smem, vmem, vmem, vmem, vmem],
        out_specs=vmem,
        scratch_shapes=[
            pltpu.VMEM((heads, rows, HEAD_DIM), jnp.float32),
            pltpu.VMEM((heads, rows, HEAD_DIM), jnp.float32),
            pltpu.VMEM((heads, rows, HEAD_DIM), jnp.float32),
        ],
        cost_estimate=pl.CostEstimate(
            flops=4 * rows * count * size * width,
            bytes_accessed=2 * (2 * rows * width + kv.size),
            transcendentals=rows * count * size * heads,
        ),
        compiler_params=pltpu.CompilerParams(vmem_limit_bytes=32 * 1024 * 1024),
        name="attend",
    )(starts, limits, query, kv, low[:, None], high[:, None])


def project_kernel(turns, ours_ref, beside_ref, ours_mod, beside_mod, all_ref, o_ours, o_beside, held, arrived):
    count = turns.shape[0]
    for i in range(count):
        for kind in range(2):
            pltpu.make_async_copy(all_ref.at[kind, turns[i]], held.at[kind, i], arrived.at[kind, i]).start()
    contract = (((1,), (1,)), ((), ()))
    halves = []
    for a_ref, mod_ref, o_ref in ((ours_ref, ours_mod, o_ours), (beside_ref, beside_mod, o_beside)):
        a = a_ref[...]
        first = mod_ref[...] == 0
        zero = jnp.zeros_like(a)
        halves.append((jnp.where(first, a, zero), jnp.where(first, zero, a), o_ref))
    for i in range(count):
        for kind in range(2):
            pltpu.make_async_copy(all_ref.at[0, 0], held.at[kind, i], arrived.at[kind, i]).wait()
        for a_first, a_second, o_ref in halves:
            o_ref[i] = (
                lax.dot_general(a_first, held[0, i], contract, preferred_element_type=jnp.float32)
                + lax.dot_general(a_second, held[1, i], contract, preferred_element_type=jnp.float32)
            ).astype(jnp.bfloat16)


def project(ours, beside, ours_mod, beside_mod, weights, turns):
    rows, depth = ours.shape
    count = turns.shape[0]
    width = weights.shape[2]
    vmem = pl.BlockSpec(memory_space=pltpu.VMEM)
    smem = pl.BlockSpec(memory_space=pltpu.SMEM)
    shape = jax.ShapeDtypeStruct((count, rows, width), jnp.bfloat16)
    return pl.pallas_call(
        project_kernel,
        out_shape=(shape, shape),
        in_specs=[smem] + [vmem] * 4 + [pl.BlockSpec(memory_space=pl.ANY)],
        out_specs=(vmem, vmem),
        scratch_shapes=[
            pltpu.VMEM((2, count, width, depth), jnp.bfloat16),
            pltpu.SemaphoreType.DMA((2, count)),
        ],
        cost_estimate=pl.CostEstimate(
            flops=8 * count * rows * depth * width,
            bytes_accessed=4 * count * depth * width + 4 * count * rows * width,
            transcendentals=0,
        ),
        compiler_params=pltpu.CompilerParams(vmem_limit_bytes=32 * 1024 * 1024),
        name="project",
    )(turns, ours, beside, ours_mod[:, None], beside_mod[:, None], weights)


def body(tokens, norm_gain, w_query, w_key, w_value, w_out, modality, doc_ids):
    length, depth = tokens.shape
    n = lax.axis_size("seq")
    subs = lax.axis_size("sub")
    heads_over = lax.axis_size("head")
    z, s = lax.axis_index("seq"), lax.axis_index("sub")
    x, y = lax.axis_index("head"), lax.axis_index("grp")
    width = depth // n

    kv_local = max(KV_HEADS // heads_over, 1)
    kv_first = x * KV_HEADS // heads_over
    key_cols = lax.dynamic_slice_in_dim(w_key, kv_first * HEAD_DIM, kv_local * HEAD_DIM, 2)
    value_cols = lax.dynamic_slice_in_dim(w_value, kv_first * HEAD_DIM, kv_local * HEAD_DIM, 2)
    w_out = jnp.swapaxes(w_out, 1, 2)

    def turned(r):
        return (z + r) % n

    def part_of(array, place, core):
        return lax.dynamic_slice_in_dim(array, (place * subs + core) * length, length)

    first_pos = (z * subs + s) * length
    own_mod, own_doc = part_of(modality, z, s), part_of(doc_ids, z, s)
    own_pos = first_pos + jnp.arange(length, dtype=jnp.int32)
    with jax.named_scope("norm"):
        values32 = tokens.astype(jnp.float32)
        factor = lax.rsqrt(jnp.mean(values32 * values32, axis=1, keepdims=True) + EPS)
        gain = jnp.where((own_mod == 1)[:, None], norm_gain[1][None, :], norm_gain[0][None, :])
        normed = (values32 * factor * gain).astype(jnp.bfloat16)

    def columns(r):
        return lax.dynamic_slice_in_dim(normed, turned(r) * width, width, 1)

    order = sorted(range(1, n), key=lambda r: -max(r, n - r)) + [0]
    blocks = {0: columns(0)}
    for r in order[:-1]:
        with jax.named_scope(f"tokens_{r}"):
            blocks[r] = from_ahead(columns(n - r), "seq", r)

    with jax.named_scope("out_gather"):
        mine = lax.dynamic_index_in_dim(w_out, y, 0, keepdims=True)
        weights = lax.all_gather(mine, ("grp", "seq"), axis=0, tiled=True)
        weights = weights.reshape(2, n, *mine.shape[1:])

    def share(weight):
        other = swap(weight, "sub")
        both = jnp.where(
            s == 0,
            jnp.concatenate([weight, other], axis=1),
            jnp.concatenate([other, weight], axis=1),
        )
        return both.reshape(2 * width, weight.shape[2])

    with jax.named_scope("share_kv"):
        w_kv_all = share(jnp.concatenate([key_cols, value_cols], axis=2))
    with jax.named_scope("share_q"):
        w_q_all = share(w_query)

    def split(block, mod):
        generate = (mod == 1)[:, None]
        zero = jnp.zeros_like(block)
        return jnp.concatenate(
            [jnp.where(generate, zero, block), jnp.where(generate, block, zero)], axis=1
        )

    doubled = {r: split(blocks[r], part_of(modality, turned(r), s)) for r in order}
    low, high = spans(modality, doc_ids, own_mod, own_doc, own_pos)
    w_kv_all, w_q_all, low, high = lax.optimization_barrier((w_kv_all, w_q_all, low, high))

    class Scatter:
        def __init__(self, weight, name):
            self.parts = {
                r: jnp.dot(doubled[r], weight, preferred_element_type=jnp.float32) for r in order
            }
            self.name = name
            self.got = None

        def sends(self, k):
            pair = self.parts[n - 1 - k], self.parts[k + 1]
            if k:
                pair = tuple(a + b.astype(jnp.float32) for a, b in zip(pair, self.got))
            return tuple(a.astype(jnp.bfloat16) for a in pair)

        def step(self, k, pair):
            with jax.named_scope(f"{self.name}_right_{k}"):
                to_right = lax.ppermute(pair[0], "seq", [(i, i + 1) for i in range(min(k + 1, n - 1))])
            with jax.named_scope(f"{self.name}_left_{k}"):
                to_left = lax.ppermute(
                    pair[1], "seq", [(i, i - 1) for i in range(max(n - 1 - k, 1), n)]
                )
            self.got = lax.optimization_barrier((to_right, to_left))

        def result(self):
            total = self.parts[0] + self.got[0].astype(jnp.float32) + self.got[1].astype(jnp.float32)
            return total.astype(jnp.bfloat16)

    kv_sum, q_sum = Scatter(w_kv_all, "kv"), Scatter(w_q_all, "q")
    kv_pair, q_pair = lax.optimization_barrier((kv_sum.sends(0), q_sum.sends(0)))
    kv_sum.step(0, kv_pair)
    q_sum.step(0, q_pair)
    for k in range(1, n - 1):
        kv_pair = lax.optimization_barrier(kv_sum.sends(k))
        kv_sum.step(k, kv_pair)
        q_pair = after(q_sum.sends(k), kv_sum.got if k < n - 2 else kv_pair)
        q_sum.step(k, q_pair)
    kv = kv_sum.result()

    same = [kv]
    for r in range(1, n):
        with jax.named_scope(f"kv_all_{r}"):
            same.append(from_ahead(kv, "seq", r))
    with jax.named_scope("kv_core_0"):
        beside_0 = swap(kv, "sub")
    with jax.named_scope("kv_core_1"):
        others = swap(jnp.stack(same[1:]), "sub")
    kv_all = jnp.concatenate([jnp.stack(same), beside_0[None], others])
    query = q_sum.result()

    starts = jnp.stack(
        [(turned(r) * subs + s) * length for r in range(n)]
        + [(turned(r) * subs + (1 - s)) * length for r in range(n)]
    ).astype(jnp.int32)
    attended = attend(query, kv_all, starts, low, high)

    with jax.named_scope("attended_core"):
        beside = swap(attended, "sub")
    beside_mod = part_of(modality, z, 1 - s)

    def out(columns):
        return project(attended, beside, own_mod, beside_mod, weights, columns.astype(jnp.int32))

    def placed(ours, theirs):
        with jax.named_scope("result_core"):
            sibling = swap(theirs, "sub")
        pair = jnp.where(s == 0, jnp.stack([ours, sibling], 1), jnp.stack([sibling, ours], 1))
        return jnp.transpose(pair, (2, 0, 1, 3)).reshape(length, -1)

    if heads_over != 2:
        wide = placed(*out(jnp.arange(n)))
        return lax.psum_scatter(wide, "head", scatter_dimension=1, tiled=True)

    half = jnp.arange(n // 2)

    def add(a, b):
        return (a.astype(jnp.float32) + b.astype(jnp.float32)).astype(jnp.bfloat16)

    send_ours, send_beside = out((1 - x) * (n // 2) + half)
    with jax.named_scope("send_beside"):
        got_beside = swap(send_beside, "head")
    with jax.named_scope("send_ours"):
        got_ours = swap(send_ours, "head")
    keep_ours, keep_beside = out(x * (n // 2) + half)
    return placed(add(keep_ours, got_ours), add(keep_beside, got_beside))


def solution(mesh):
    placed = (
        P(("grp", "seq", "sub"), None),
        P(),
        P(None, ("seq", "sub"), "head"),
        P(None, ("seq", "sub"), None),
        P(None, ("seq", "sub"), None),
        P(None, "head", ("seq", "sub")),
        P("grp"),
        P("grp"),
    )
    return jax.shard_map(
        body,
        mesh=mesh,
        in_specs=placed,
        out_specs=P(("grp", "seq", "sub"), "head"),
        check_vma=False,
    )
```

```python
import math

import jax
import jax.numpy as jnp
from jax import lax
from jax.experimental import pallas as pl
from jax.experimental.pallas import tpu as pltpu
from jax.sharding import PartitionSpec as P


HEAD_DIM = 128
KV_HEADS = 4
EPS = 1e-06
LOW = -1e30


def swap(x, axis):
    return lax.ppermute(x, axis, [(0, 1), (1, 0)])


def from_ahead(x, axis, offset):
    size = lax.axis_size(axis)
    return lax.ppermute(x, axis, [((i + offset) % size, i) for i in range(size)])


def after(value, *done):
    return lax.optimization_barrier((value, *done))[0]


def spans(modality, doc_ids, own_mod, own_doc, own_pos):
    changed = (modality[1:] != modality[:-1]) | (doc_ids[1:] != doc_ids[:-1])
    begins = jnp.concatenate([jnp.ones((1,), jnp.int32), changed.astype(jnp.int32)])
    blocks = jnp.cumsum(begins)
    own_block = lax.dynamic_slice_in_dim(blocks, own_pos[0], own_pos.shape[0])
    low = jnp.sum((doc_ids[None, :] < own_doc[:, None]).astype(jnp.int32), axis=1)
    end = jnp.sum((blocks[None, :] <= own_block[:, None]).astype(jnp.int32), axis=1) - 1
    return low, jnp.where(own_mod == 1, end, own_pos)


def attention_kernel(starts, limits, q_ref, kv_ref, low_ref, high_ref, o_ref, top, total, acc):
    count, size, _ = kv_ref.shape
    rows = q_ref.shape[0]
    heads = q_ref.shape[1] // HEAD_DIM
    kv_local = kv_ref.shape[2] // (2 * HEAD_DIM)
    repeat = heads // kv_local
    scale = 1.0 / math.sqrt(HEAD_DIM)
    top[...] = jnp.full_like(top, LOW)
    total[...] = jnp.zeros_like(total)
    acc[...] = jnp.zeros_like(acc)

    def visit(number, _):
        start = starts[number]

        @pl.when((start <= limits[1]) & (start + size > limits[0]))
        def _():
            key_pos = start + lax.broadcasted_iota(jnp.int32, (rows, size), 1)
            seen = (key_pos >= low_ref[...]) & (key_pos <= high_ref[...])
            for head in range(heads):
                g = head // repeat
                keys = kv_ref[number, :, g * HEAD_DIM : (g + 1) * HEAD_DIM]
                values = kv_ref[number, :, (kv_local + g) * HEAD_DIM : (kv_local + g + 1) * HEAD_DIM]
                query = q_ref[:, head * HEAD_DIM : (head + 1) * HEAD_DIM]
                scores = lax.dot_general(
                    query, keys, (((1,), (1,)), ((), ())), preferred_element_type=jnp.float32
                )
                scores = jnp.where(seen, scores * scale, LOW)
                old = top[head][:, :1]
                new = jnp.maximum(old, jnp.max(scores, axis=1, keepdims=True))
                weights = jnp.where(seen, jnp.exp(scores - new), 0.0)
                shrink = jnp.exp(old - new)
                total[head] = jnp.broadcast_to(
                    total[head][:, :1] * shrink + jnp.sum(weights, axis=1, keepdims=True),
                    (rows, HEAD_DIM),
                )
                top[head] = jnp.broadcast_to(new, (rows, HEAD_DIM))
                acc[head] = acc[head] * shrink + jnp.dot(
                    weights.astype(jnp.bfloat16), values, preferred_element_type=jnp.float32
                )

        return 0

    lax.fori_loop(0, count, visit, 0)
    for head in range(heads):
        o_ref[:, head * HEAD_DIM : (head + 1) * HEAD_DIM] = (acc[head] / total[head]).astype(
            jnp.bfloat16
        )


def attend(query, kv, starts, low, high):
    rows, width = query.shape
    heads = width // HEAD_DIM
    count, size, _ = kv.shape
    vmem = pl.BlockSpec(memory_space=pltpu.VMEM)
    smem = pl.BlockSpec(memory_space=pltpu.SMEM)
    limits = jnp.stack([low[0], high[-1]])
    return pl.pallas_call(
        attention_kernel,
        out_shape=jax.ShapeDtypeStruct((rows, width), jnp.bfloat16),
        in_specs=[smem, smem, vmem, vmem, vmem, vmem],
        out_specs=vmem,
        scratch_shapes=[
            pltpu.VMEM((heads, rows, HEAD_DIM), jnp.float32),
            pltpu.VMEM((heads, rows, HEAD_DIM), jnp.float32),
            pltpu.VMEM((heads, rows, HEAD_DIM), jnp.float32),
        ],
        cost_estimate=pl.CostEstimate(
            flops=4 * rows * count * size * width,
            bytes_accessed=2 * (2 * rows * width + kv.size),
            transcendentals=rows * count * size * heads,
        ),
        compiler_params=pltpu.CompilerParams(vmem_limit_bytes=32 * 1024 * 1024),
        name="attend",
    )(starts, limits, query, kv, low[:, None], high[:, None])


def project_kernel(turns, places, ours_ref, beside_ref, ours_near, beside_near, own_ref, *rest):
    steps = (len(rest) - 4) // 4
    near = rest[: 2 * steps]
    far = rest[2 * steps : 4 * steps]
    o_ours, o_beside, held, arrived = rest[4 * steps :]
    count = turns.shape[0]
    size = steps + 1
    place, first = places[0], places[1]

    def wanted(turn):
        slot = jnp.int32(-1)
        for i in range(count):
            slot = jnp.where(turns[i] == turn, i, slot)
        return slot

    def fetch(source, kind, turn, valid):
        slot = wanted(turn)

        @pl.when(valid & (slot >= 0))
        def _():
            at = jnp.maximum(slot, 0)
            pltpu.make_async_copy(source, held.at[kind, at], arrived.at[kind, at]).start()

    fetch(own_ref.at[first], 0, 0, True)
    fetch(own_ref.at[1 - first], 1, 0, True)
    for k in range(steps):
        for kind, refs in ((0, near), (1, far)):
            fetch(refs[k], kind, k + 1, place + k + 1 < size)
            fetch(refs[steps + k], kind, size - 1 - k, place >= k + 1)

    contract = (((1,), (1,)), ((), ()))
    halves = []
    for a_ref, near_ref, o_ref in ((ours_ref, ours_near, o_ours), (beside_ref, beside_near, o_beside)):
        a = a_ref[...]
        mine = near_ref[...] != 0
        zero = jnp.zeros_like(a)
        halves.append((jnp.where(mine, a, zero), jnp.where(mine, zero, a), o_ref))
    for i in range(count):
        for kind in range(2):
            pltpu.make_async_copy(own_ref.at[0], held.at[kind, i], arrived.at[kind, i]).wait()
        for a_near, a_far, o_ref in halves:
            o_ref[i] = (
                lax.dot_general(a_near, held[0, i], contract, preferred_element_type=jnp.float32)
                + lax.dot_general(a_far, held[1, i], contract, preferred_element_type=jnp.float32)
            ).astype(jnp.bfloat16)


def project(ours, beside, ours_near, beside_near, weights, turns, places):
    rows, depth = ours.shape
    count = turns.shape[0]
    width = weights[0].shape[1]
    vmem = pl.BlockSpec(memory_space=pltpu.VMEM)
    smem = pl.BlockSpec(memory_space=pltpu.SMEM)
    shape = jax.ShapeDtypeStruct((count, rows, width), jnp.bfloat16)
    return pl.pallas_call(
        project_kernel,
        out_shape=(shape, shape),
        in_specs=[smem, smem] + [vmem] * 4 + [pl.BlockSpec(memory_space=pl.ANY)] * len(weights),
        out_specs=(vmem, vmem),
        scratch_shapes=[
            pltpu.VMEM((2, count, width, depth), jnp.bfloat16),
            pltpu.SemaphoreType.DMA((2, count)),
        ],
        cost_estimate=pl.CostEstimate(
            flops=8 * count * rows * depth * width,
            bytes_accessed=4 * count * depth * width + 4 * count * rows * width,
            transcendentals=0,
        ),
        compiler_params=pltpu.CompilerParams(vmem_limit_bytes=32 * 1024 * 1024),
        name="project",
    )(turns, places, ours, beside, ours_near[:, None], beside_near[:, None], *weights)


def body(tokens, norm_gain, w_query, w_key, w_value, w_out, modality, doc_ids):
    length, depth = tokens.shape
    n = lax.axis_size("seq")
    subs = lax.axis_size("sub")
    heads_over = lax.axis_size("head")
    z, s = lax.axis_index("seq"), lax.axis_index("sub")
    x, y = lax.axis_index("head"), lax.axis_index("grp")
    width = depth // n
    steps = range(n - 1)

    kv_local = max(KV_HEADS // heads_over, 1)
    kv_first = x * KV_HEADS // heads_over
    key_cols = lax.dynamic_slice_in_dim(w_key, kv_first * HEAD_DIM, kv_local * HEAD_DIM, 2)
    value_cols = lax.dynamic_slice_in_dim(w_value, kv_first * HEAD_DIM, kv_local * HEAD_DIM, 2)
    w_out = jnp.swapaxes(w_out, 1, 2)

    def turned(r):
        return (z + r) % n

    def part_of(array, place, core):
        return lax.dynamic_slice_in_dim(array, (place * subs + core) * length, length)

    first_pos = (z * subs + s) * length
    own_mod, own_doc = part_of(modality, z, s), part_of(doc_ids, z, s)
    own_pos = first_pos + jnp.arange(length, dtype=jnp.int32)
    values32 = tokens.astype(jnp.float32)
    factor = lax.rsqrt(jnp.mean(values32 * values32, axis=1, keepdims=True) + EPS)
    gain = jnp.where((own_mod == 1)[:, None], norm_gain[1][None, :], norm_gain[0][None, :])
    normed = (values32 * factor * gain).astype(jnp.bfloat16)

    mine = lax.dynamic_index_in_dim(w_out, y, 0, keepdims=False)
    right, left = [], []

    def step_out(k, *done):
        send_right, send_left = (right[-1], left[-1]) if k else (mine, mine)
        if done:
            send_right, send_left = after((send_right, send_left), *done)
        right.append(lax.ppermute(send_right, "seq", [(i, i + 1) for i in range(k, n - 1)]))
        left.append(lax.ppermute(send_left, "seq", [(i, i - 1) for i in range(1, n - k)]))

    step_out(0)

    order = sorted(range(1, n), key=lambda r: -max(r, n - r)) + [0]
    share_rows = heads_over == 2
    rows = length // 2 if share_rows else length

    def columns(r, first=0, count=length):
        return lax.dynamic_slice(normed, (first, turned(r) * width), (count, width))

    blocks = {0: columns(0)}
    for r in order[:-1]:
        blocks[r] = from_ahead(columns(n - r, x * rows if share_rows else 0, rows), "seq", r)
    if share_rows:
        for group in (order[:2], order[2:-1]):
            if group:
                held = jnp.stack([blocks[r] for r in group])
                other = swap(held, "head")
                for i, r in enumerate(group):
                    blocks[r] = jnp.where(
                        x == 0,
                        jnp.concatenate([held[i], other[i]]),
                        jnp.concatenate([other[i], held[i]]),
                    )

    def share(weight):
        other = swap(weight, "sub")
        both = jnp.where(
            s == 0,
            jnp.concatenate([weight, other], axis=1),
            jnp.concatenate([other, weight], axis=1),
        )
        return both.reshape(2 * width, weight.shape[2])

    w_kv_all = share(jnp.concatenate([key_cols, value_cols], axis=2))
    w_q_all = share(w_query)

    def split(block, mod):
        generate = (mod == 1)[:, None]
        zero = jnp.zeros_like(block)
        return jnp.concatenate(
            [jnp.where(generate, zero, block), jnp.where(generate, block, zero)], axis=1
        )

    modality, doc_ids = after((modality, doc_ids), normed)
    doubled = {r: split(blocks[r], part_of(modality, turned(r), s)) for r in order}
    low, high = spans(modality, doc_ids, own_mod, own_doc, own_pos)
    w_kv_all, w_q_all, low, high = lax.optimization_barrier((w_kv_all, w_q_all, low, high))

    class Scatter:
        def __init__(self, weight):
            self.parts = {
                r: jnp.dot(doubled[r], weight, preferred_element_type=jnp.float32) for r in order
            }
            self.got = None

        def sends(self, k):
            pair = self.parts[n - 1 - k], self.parts[k + 1]
            if k:
                pair = tuple(a + b.astype(jnp.float32) for a, b in zip(pair, self.got))
            return tuple(a.astype(jnp.bfloat16) for a in pair)

        def step(self, k, pair):
            to_right = lax.ppermute(pair[0], "seq", [(i, i + 1) for i in range(min(k + 1, n - 1))])
            to_left = lax.ppermute(
                pair[1], "seq", [(i, i - 1) for i in range(max(n - 1 - k, 1), n)]
            )
            self.got = lax.optimization_barrier((to_right, to_left))

        def result(self):
            total = self.parts[0] + self.got[0].astype(jnp.float32) + self.got[1].astype(jnp.float32)
            return total.astype(jnp.bfloat16)

    kv_sum, q_sum = Scatter(w_kv_all), Scatter(w_q_all)
    kv_pair, q_pair = lax.optimization_barrier((kv_sum.sends(0), q_sum.sends(0)))
    kv_sum.step(0, kv_pair)
    q_sum.step(0, q_pair)
    if n > 2:
        step_out(1, q_pair)
    for k in range(1, n - 1):
        kv_pair = lax.optimization_barrier(kv_sum.sends(k))
        kv_sum.step(k, kv_pair)
        q_pair = after(q_sum.sends(k), kv_sum.got if k < n - 2 else kv_pair)
        q_sum.step(k, q_pair)
        if k + 1 < n - 1:
            step_out(k + 1, q_pair)
    kv = kv_sum.result()

    same = [kv]
    for r in range(1, n):
        same.append(from_ahead(kv, "seq", r))
    beside_0 = swap(kv, "sub")
    others = swap(jnp.stack(same[1:]), "sub")
    kv_all = jnp.concatenate([jnp.stack(same), beside_0[None], others])
    query = q_sum.result()

    pairs = []
    for k in steps:
        for received, there in ((left[k], range(n - 1 - k)), (right[k], range(k + 1, n))):
            hops = [(i, i + n) for i in there] + [(i + n, i) for i in there]
            pairs.append(lax.ppermute(received, ("grp", "seq"), hops))
    weights = [w_out] + left + right + pairs[0::2] + pairs[1::2]

    starts = jnp.stack(
        [(turned(r) * subs + s) * length for r in range(n)]
        + [(turned(r) * subs + (1 - s)) * length for r in range(n)]
    ).astype(jnp.int32)
    attended = attend(query, kv_all, starts, low, high)

    beside = swap(attended, "sub")
    ours_near = (own_mod == y).astype(jnp.bfloat16)
    beside_near = (part_of(modality, z, 1 - s) == y).astype(jnp.bfloat16)
    places = jnp.stack([z, y]).astype(jnp.int32)

    def out(columns):
        turns = ((columns - z + n) % n).astype(jnp.int32)
        return project(attended, beside, ours_near, beside_near, weights, turns, places)

    def placed(ours, theirs):
        sibling = swap(theirs, "sub")
        pair = jnp.where(s == 0, jnp.stack([ours, sibling], 1), jnp.stack([sibling, ours], 1))
        return jnp.transpose(pair, (2, 0, 1, 3)).reshape(length, -1)

    if heads_over != 2:
        wide = placed(*out(jnp.arange(n)))
        return lax.psum_scatter(wide, "head", scatter_dimension=1, tiled=True)

    half = jnp.arange(n // 2)

    def add(a, b):
        return (a.astype(jnp.float32) + b.astype(jnp.float32)).astype(jnp.bfloat16)

    send_ours, send_beside = out((1 - x) * (n // 2) + half)
    got_beside = swap(send_beside, "head")
    got_ours = swap(send_ours, "head")
    keep_ours, keep_beside = out(x * (n // 2) + half)
    return placed(add(keep_ours, got_ours), add(keep_beside, got_beside))


def solution(mesh):
    placed = (
        P(("grp", "seq", "sub"), None),
        P(),
        P(None, ("seq", "sub"), "head"),
        P(None, ("seq", "sub"), None),
        P(None, ("seq", "sub"), None),
        P(None, "head", ("seq", "sub")),
        P("grp"),
        P("grp"),
    )
    return jax.shard_map(
        body,
        mesh=mesh,
        in_specs=placed,
        out_specs=P(("grp", "seq", "sub"), "head"),
        check_vma=False,
    )
```

```python
import functools
import math

import jax
import jax.numpy as jnp
from jax import lax
from jax.experimental import pallas as pl
from jax.experimental.pallas import tpu as pltpu
from jax.sharding import PartitionSpec as P


HEAD_DIM = 128
KV_HEADS = 4
EPS = 1e-06
LOW = -1e30


def swap(x, axis):
    return lax.ppermute(x, axis, [(0, 1), (1, 0)])


def cross(x, axis, bit, among=None):
    size = lax.axis_size(axis)
    return lax.ppermute(x, axis, [(i ^ bit, i) for i in (among or range(size))])


def after(value, *done):
    return lax.optimization_barrier((value, *done))[0]


def add(a, b):
    return (a.astype(jnp.float32) + b.astype(jnp.float32)).astype(jnp.bfloat16)


VMEM = pl.BlockSpec(memory_space=pltpu.VMEM)
SMEM = pl.BlockSpec(memory_space=pltpu.SMEM)
ANY = pl.BlockSpec(memory_space=pl.ANY)


def norm_kernel(place, tokens_ref, gain_ref, mod_ref, own_ref, *rest):
    send_refs, scratch = rest[:-1], rest[-1]
    width = own_ref.shape[1]
    values = tokens_ref[...].astype(jnp.float32)
    factor = lax.rsqrt(jnp.mean(values * values, axis=1, keepdims=True) + EPS)
    gain = jnp.where(mod_ref[...] == 1, gain_ref[1:2, :], gain_ref[0:1, :])
    scratch[...] = (values * factor * gain).astype(jnp.bfloat16)

    def columns(d):
        return pl.ds(pl.multiple_of((place[0] ^ d) * width, width), width)

    own_ref[...] = scratch[:, columns(0)]
    for d, ref in enumerate(send_refs, 1):
        rows = ref.shape[0]
        ref[...] = scratch[pl.ds(pl.multiple_of(place[1] * rows, rows), rows), columns(d)]


def norm_columns(tokens, norm_gain, mod, place, n, rows):
    length, depth = tokens.shape
    width = depth // n
    if width % 128:
        values32 = tokens.astype(jnp.float32)
        factor = lax.rsqrt(jnp.mean(values32 * values32, axis=1, keepdims=True) + EPS)
        gain = jnp.where((mod == 1)[:, None], norm_gain[1][None, :], norm_gain[0][None, :])
        normed = (values32 * factor * gain).astype(jnp.bfloat16)
        first = [0] + [place[1] * rows] * (n - 1)
        count = [length] + [rows] * (n - 1)
        return [
            lax.dynamic_slice(normed, (first[d], (place[0] ^ d) * width), (count[d], width))
            for d in range(n)
        ]
    shapes = [jax.ShapeDtypeStruct((length, width), jnp.bfloat16)]
    shapes += [jax.ShapeDtypeStruct((rows, width), jnp.bfloat16)] * (n - 1)
    return pl.pallas_call(
        norm_kernel,
        out_shape=shapes,
        in_specs=[SMEM, VMEM, VMEM, VMEM],
        out_specs=[VMEM] * n,
        scratch_shapes=[pltpu.VMEM((length, depth), jnp.bfloat16)],
        cost_estimate=pl.CostEstimate(
            flops=6 * length * depth, bytes_accessed=4 * length * depth, transcendentals=length
        ),
        compiler_params=pltpu.CompilerParams(vmem_limit_bytes=32 * 1024 * 1024),
        name="norm",
    )(place, tokens, norm_gain, mod[:, None])


def partial_kernel(counts, place, mod_ref, w_kv, w_q, *rest):
    total = sum(counts)
    refs, kv_ref, q_ref, both = rest[:total], rest[total], rest[total + 1], rest[total + 2]
    length, width = both.shape[0] // len(counts), both.shape[1]
    at = 0
    for number, count in enumerate(counts):
        base = number * length
        if count == 1:
            both[base : base + length] = refs[at][...]
        else:
            half = length // 2
            both[pl.ds(pl.multiple_of(base + place[1] * half, half), half)] = refs[at][...]
            both[pl.ds(pl.multiple_of(base + (1 - place[1]) * half, half), half)] = refs[at + 1][...]
        at += count
    block = both[...]
    generate = mod_ref[...] == 1
    zero = jnp.zeros_like(block)
    first, second = jnp.where(generate, zero, block), jnp.where(generate, block, zero)
    for weight, out in ((w_kv, kv_ref), (w_q, q_ref)):
        out[...] = jnp.dot(first, weight[:width], preferred_element_type=jnp.float32) + jnp.dot(
            second, weight[width:], preferred_element_type=jnp.float32
        )


def partial(blocks, mods, w_kv, w_q, place):
    counts = tuple(len(block) for block in blocks)
    arrays = [array for block in blocks for array in block]
    length = mods[0].shape[0]
    rows, width = length * len(blocks), arrays[0].shape[1]
    kv_cols, q_cols = w_kv.shape[1], w_q.shape[1]
    kv, q = pl.pallas_call(
        functools.partial(partial_kernel, counts),
        out_shape=(
            jax.ShapeDtypeStruct((rows, kv_cols), jnp.float32),
            jax.ShapeDtypeStruct((rows, q_cols), jnp.float32),
        ),
        in_specs=[SMEM] + [VMEM] * (3 + len(arrays)),
        out_specs=(VMEM, VMEM),
        scratch_shapes=[pltpu.VMEM((rows, width), jnp.bfloat16)],
        cost_estimate=pl.CostEstimate(
            flops=4 * rows * width * (kv_cols + q_cols),
            bytes_accessed=4 * (width + rows) * (kv_cols + q_cols),
            transcendentals=0,
        ),
        compiler_params=pltpu.CompilerParams(vmem_limit_bytes=40 * 1024 * 1024),
        name="partial",
    )(place, jnp.concatenate(mods)[:, None], w_kv, w_q, *arrays)
    shape = (len(blocks), length, -1)
    return kv.reshape(shape), q.reshape(shape)


def reduce_scatter(parts, split):
    n = len(parts)
    if n != 4:
        sums = dict(enumerate(parts))
        for bit in [1 << i for i in range(n.bit_length() - 1)]:
            for d in [d for d in range(n) if d in sums and d & bit]:
                sums[d ^ bit] = sums[d ^ bit] + cross(sums.pop(d).astype(jnp.bfloat16), "seq", bit)
        return sums[0].astype(jnp.bfloat16)

    def send(pieces, bit, among):
        if split:
            got = []
            for piece in pieces:
                got.append(cross(piece.astype(jnp.bfloat16), "seq", bit, among))
            return [g.astype(jnp.float32) for g in got]
        got = cross(jnp.stack(pieces).astype(jnp.bfloat16), "seq", bit, among)
        return [got[i].astype(jnp.float32) for i in range(len(pieces))]

    far, two = send([parts[3], parts[2]], 1, (1, 2))
    across, own = send([parts[2] + far, parts[3] + two], 3, (1, 2))
    last = cross((parts[1] + across).astype(jnp.bfloat16), "seq", 1)
    return (parts[0] + last.astype(jnp.float32) + own).astype(jnp.bfloat16)


def gather_weights(mine):
    n = lax.axis_size("seq")
    if n == 4:
        z = lax.axis_index("seq")
        inner = (z == 1) | (z == 2)
        one = cross(mine, "seq", 1)
        middle = cross(mine, "seq", 3, (1, 2))
        middle_two = cross(one, "seq", 3, (1, 2))
        outer_two = cross(middle, "seq", 1, (0, 3))
        outer_three = cross(middle_two, "seq", 1, (0, 3))
        near = [mine, one, jnp.where(inner, middle_two, outer_two), jnp.where(inner, middle, outer_three)]
    else:
        near = [mine]
        for bit in reversed([1 << i for i in range(n.bit_length() - 1)]):
            got = cross(jnp.stack(near), "seq", bit)
            near = near + [got[i] for i in range(len(near))]
        order = [0]
        for bit in reversed([1 << i for i in range(n.bit_length() - 1)]):
            order = order + [d ^ bit for d in order]
        near = [near[order.index(d)] for d in range(n)]
    far = []
    for d in range(1, n):
        far.append(swap(near[d], "grp"))
    return near[1:], far


def spans(modality, doc_ids, own_mod, own_doc, own_pos):
    changed = (modality[1:] != modality[:-1]) | (doc_ids[1:] != doc_ids[:-1])
    begins = jnp.concatenate([jnp.ones((1,), jnp.int32), changed.astype(jnp.int32)])
    blocks = jnp.cumsum(begins)
    own_block = lax.dynamic_slice_in_dim(blocks, own_pos[0], own_pos.shape[0])
    low = jnp.sum((doc_ids[None, :] < own_doc[:, None]).astype(jnp.int32), axis=1)
    end = jnp.sum((blocks[None, :] <= own_block[:, None]).astype(jnp.int32), axis=1) - 1
    return low, jnp.where(own_mod == 1, end, own_pos)


def attention_kernel(starts, limits, q_ref, kv_ref, low_ref, high_ref, o_ref, top, total, acc):
    count, size, _ = kv_ref.shape
    rows = q_ref.shape[0]
    heads = q_ref.shape[1] // HEAD_DIM
    kv_local = kv_ref.shape[2] // (2 * HEAD_DIM)
    repeat = heads // kv_local
    scale = 1.0 / math.sqrt(HEAD_DIM)
    top[...] = jnp.full_like(top, LOW)
    total[...] = jnp.zeros_like(total)
    acc[...] = jnp.zeros_like(acc)

    def visit(number, _):
        start = starts[number]

        @pl.when((start <= limits[1]) & (start + size > limits[0]))
        def _():
            key_pos = start + lax.broadcasted_iota(jnp.int32, (rows, size), 1)
            seen = (key_pos >= low_ref[...]) & (key_pos <= high_ref[...])
            for head in range(heads):
                g = head // repeat
                keys = kv_ref[number, :, g * HEAD_DIM : (g + 1) * HEAD_DIM]
                values = kv_ref[number, :, (kv_local + g) * HEAD_DIM : (kv_local + g + 1) * HEAD_DIM]
                query = q_ref[:, head * HEAD_DIM : (head + 1) * HEAD_DIM]
                scores = lax.dot_general(
                    query, keys, (((1,), (1,)), ((), ())), preferred_element_type=jnp.float32
                )
                scores = jnp.where(seen, scores * scale, LOW)
                old = top[head][:, :1]
                new = jnp.maximum(old, jnp.max(scores, axis=1, keepdims=True))
                weights = jnp.where(seen, jnp.exp(scores - new), 0.0)
                shrink = jnp.exp(old - new)
                total[head] = jnp.broadcast_to(
                    total[head][:, :1] * shrink + jnp.sum(weights, axis=1, keepdims=True),
                    (rows, HEAD_DIM),
                )
                top[head] = jnp.broadcast_to(new, (rows, HEAD_DIM))
                acc[head] = acc[head] * shrink + jnp.dot(
                    weights.astype(jnp.bfloat16), values, preferred_element_type=jnp.float32
                )

        return 0

    lax.fori_loop(0, count, visit, 0)
    for head in range(heads):
        o_ref[:, head * HEAD_DIM : (head + 1) * HEAD_DIM] = (acc[head] / total[head]).astype(
            jnp.bfloat16
        )


def attend(query, kv, starts, low, high):
    rows, width = query.shape
    heads = width // HEAD_DIM
    count, size, _ = kv.shape
    vmem = pl.BlockSpec(memory_space=pltpu.VMEM)
    smem = pl.BlockSpec(memory_space=pltpu.SMEM)
    limits = jnp.stack([low[0], high[-1]])
    return pl.pallas_call(
        attention_kernel,
        out_shape=jax.ShapeDtypeStruct((rows, width), jnp.bfloat16),
        in_specs=[smem, smem, vmem, vmem, vmem, vmem],
        out_specs=vmem,
        scratch_shapes=[
            pltpu.VMEM((heads, rows, HEAD_DIM), jnp.float32),
            pltpu.VMEM((heads, rows, HEAD_DIM), jnp.float32),
            pltpu.VMEM((heads, rows, HEAD_DIM), jnp.float32),
        ],
        cost_estimate=pl.CostEstimate(
            flops=4 * rows * count * size * width,
            bytes_accessed=2 * (2 * rows * width + kv.size),
            transcendentals=rows * count * size * heads,
        ),
        compiler_params=pltpu.CompilerParams(vmem_limit_bytes=32 * 1024 * 1024),
        name="attend",
    )(starts, limits, query, kv, low[:, None], high[:, None])


def project_kernel(turns, place, ours_ref, beside_ref, ours_near, beside_near, own_ref, *rest):
    n = (len(rest) - 4) // 2 + 1
    near, far = rest[: n - 1], rest[n - 1 : 2 * n - 2]
    o_ours, o_beside, held, arrived = rest[2 * n - 2 :]
    count = turns.shape[0]
    first = place[2]

    def fetch(source, kind, d):
        slot = jnp.int32(-1)
        for i in range(count):
            slot = jnp.where(turns[i] == d, i, slot)

        @pl.when(slot >= 0)
        def _():
            at = jnp.maximum(slot, 0)
            pltpu.make_async_copy(source, held.at[kind, at], arrived.at[kind, at]).start()

    for d in range(n):
        fetch(near[d - 1] if d else own_ref.at[first], 0, d)
        fetch(far[d - 1] if d else own_ref.at[1 - first], 1, d)

    contract = (((1,), (1,)), ((), ()))
    halves = []
    for a_ref, near_ref, o_ref in ((ours_ref, ours_near, o_ours), (beside_ref, beside_near, o_beside)):
        a = a_ref[...]
        mine = near_ref[...] != 0
        zero = jnp.zeros_like(a)
        halves.append((jnp.where(mine, a, zero), jnp.where(mine, zero, a), o_ref))
    for i in range(count):
        for kind in range(2):
            pltpu.make_async_copy(own_ref.at[0], held.at[kind, i], arrived.at[kind, i]).wait()
        for a_near, a_far, o_ref in halves:
            o_ref[i] = (
                lax.dot_general(a_near, held[0, i], contract, preferred_element_type=jnp.float32)
                + lax.dot_general(a_far, held[1, i], contract, preferred_element_type=jnp.float32)
            ).astype(jnp.bfloat16)


def project(ours, beside, ours_near, beside_near, weights, turns, place):
    rows, depth = ours.shape
    count = turns.shape[0]
    width = weights[0].shape[1]
    shape = jax.ShapeDtypeStruct((count, rows, width), jnp.bfloat16)
    return pl.pallas_call(
        project_kernel,
        out_shape=(shape, shape),
        in_specs=[SMEM, SMEM] + [VMEM] * 4 + [ANY] * len(weights),
        out_specs=(VMEM, VMEM),
        scratch_shapes=[
            pltpu.VMEM((2, count, width, depth), jnp.bfloat16),
            pltpu.SemaphoreType.DMA((2, count)),
        ],
        cost_estimate=pl.CostEstimate(
            flops=8 * count * rows * depth * width,
            bytes_accessed=4 * count * depth * width + 4 * count * rows * width,
            transcendentals=0,
        ),
        compiler_params=pltpu.CompilerParams(vmem_limit_bytes=32 * 1024 * 1024),
        name="project",
    )(turns, place, ours, beside, ours_near[:, None], beside_near[:, None], *weights)


def body(tokens, norm_gain, w_query, w_key, w_value, w_out, modality, doc_ids):
    length, depth = tokens.shape
    n = lax.axis_size("seq")
    subs = lax.axis_size("sub")
    heads_over = lax.axis_size("head")
    z, s = lax.axis_index("seq"), lax.axis_index("sub")
    x, y = lax.axis_index("head"), lax.axis_index("grp")
    width = depth // n
    place = jnp.stack([z, x, y]).astype(jnp.int32)

    kv_local = max(KV_HEADS // heads_over, 1)
    kv_first = x * KV_HEADS // heads_over
    w_out = jnp.swapaxes(w_out, 1, 2)

    def part_of(array, place, core):
        return lax.dynamic_slice_in_dim(array, (place * subs + core) * length, length)

    mine = lax.dynamic_index_in_dim(w_out, y, 0, keepdims=False)
    near, far = gather_weights(mine)
    weights = [w_out] + near + far

    own_mod = part_of(modality, z, s)
    share_rows = heads_over == 2
    rows = length // 2 if share_rows else length
    sends = norm_columns(tokens, norm_gain, own_mod, place, n, rows)
    blocks = {0: (sends[0],)}
    for d in range(n - 1, 0, -1):
        blocks[d] = (cross(sends[d], "seq", d),)

    def share(weight):
        other = swap(weight, "sub")
        both = jnp.where(
            s == 0,
            jnp.concatenate([weight, other], axis=1),
            jnp.concatenate([other, weight], axis=1),
        )
        return both.reshape(2 * width, weight.shape[2])

    key_cols = lax.dynamic_slice_in_dim(w_key, kv_first * HEAD_DIM, kv_local * HEAD_DIM, 2)
    value_cols = lax.dynamic_slice_in_dim(w_value, kv_first * HEAD_DIM, kv_local * HEAD_DIM, 2)
    w_kv_all = share(jnp.concatenate([key_cols, value_cols], axis=2))
    w_q_all = share(w_query)
    modality, doc_ids = after((modality, doc_ids), sends[0])
    own_doc = part_of(doc_ids, z, s)
    own_pos = (z * subs + s) * length + jnp.arange(length, dtype=jnp.int32)
    low, high = spans(modality, doc_ids, part_of(modality, z, s), own_doc, own_pos)
    for d in range(1, n):
        blocks[d] = after(blocks[d], w_kv_all, w_q_all, low, high)

    early = list(range(n - 1, 1, -1))
    if share_rows:
        for group in (early, [1]):
            held = jnp.stack([blocks[d][0] for d in group])
            other = swap(held, "head")
            for i, d in enumerate(group):
                blocks[d] = (blocks[d][0], other[i])
    parts = {}
    for group in (early, [1, 0]):
        kv, q = partial(
            [blocks[d] for d in group],
            [part_of(modality, z ^ d, s) for d in group],
            w_kv_all,
            w_q_all,
            place,
        )
        for i, d in enumerate(group):
            parts[d] = kv[i], q[i]
    kv = reduce_scatter([parts[d][0] for d in range(n)], False)
    query = reduce_scatter([parts[d][1] for d in range(n)], True)

    same = [kv]
    for d in range(1, n):
        same.append(cross(kv, "seq", d))
    beside_0 = swap(kv, "sub")
    others = swap(jnp.stack(same[1:]), "sub")
    kv_all = jnp.concatenate([jnp.stack(same), beside_0[None], others])
    starts = jnp.stack(
        [((z ^ d) * subs + s) * length for d in range(n)]
        + [((z ^ d) * subs + (1 - s)) * length for d in range(n)]
    ).astype(jnp.int32)
    attended = attend(query, kv_all, starts, low, high)

    beside = swap(attended, "sub")
    ours_near = (own_mod == y).astype(jnp.bfloat16)
    beside_near = (part_of(modality, z, 1 - s) == y).astype(jnp.bfloat16)

    def out(columns):
        turns = (columns ^ z).astype(jnp.int32)
        return project(attended, beside, ours_near, beside_near, weights, turns, place)

    def placed(ours, theirs):
        sibling = swap(theirs, "sub")
        pair = jnp.where(s == 0, jnp.stack([ours, sibling], 1), jnp.stack([sibling, ours], 1))
        return jnp.transpose(pair, (2, 0, 1, 3)).reshape(length, -1)

    if heads_over != 2:
        wide = placed(*out(jnp.arange(n)))
        return lax.psum_scatter(wide, "head", scatter_dimension=1, tiled=True)

    half = jnp.arange(n // 2)
    send_ours, send_beside = out((1 - x) * (n // 2) + half)
    got_beside = swap(send_beside, "head")
    got_ours = swap(send_ours, "head")
    keep_ours, keep_beside = out(x * (n // 2) + half)
    return placed(add(keep_ours, got_ours), add(keep_beside, got_beside))


def solution(mesh):
    placed = (
        P(("grp", "seq", "sub"), None),
        P(),
        P(None, ("seq", "sub"), "head"),
        P(None, ("seq", "sub"), None),
        P(None, ("seq", "sub"), None),
        P(None, "head", ("seq", "sub")),
        P("grp"),
        P("grp"),
    )
    return jax.shard_map(
        body,
        mesh=mesh,
        in_specs=placed,
        out_specs=P(("grp", "seq", "sub"), "head"),
        check_vma=False,
    )
```

```python
import functools
import math

import jax
import jax.numpy as jnp
from jax import lax
from jax.experimental import pallas as pl
from jax.experimental.pallas import tpu as pltpu
from jax.sharding import PartitionSpec as P


HEAD_DIM = 128
KV_HEADS = 4
EPS = 1e-06
LOW = -1e30


def swap(x, axis):
    return lax.ppermute(x, axis, [(0, 1), (1, 0)])


def cross(x, axis, bit, among=None):
    size = lax.axis_size(axis)
    return lax.ppermute(x, axis, [(i ^ bit, i) for i in (among or range(size))])


def after(value, *done):
    return lax.optimization_barrier((value, *done))[0]


def add(a, b):
    return (a.astype(jnp.float32) + b.astype(jnp.float32)).astype(jnp.bfloat16)


VMEM = pl.BlockSpec(memory_space=pltpu.VMEM)
SMEM = pl.BlockSpec(memory_space=pltpu.SMEM)
ANY = pl.BlockSpec(memory_space=pl.ANY)


def norm_kernel(place, tokens_ref, gain_ref, mod_ref, own_ref, *rest):
    send_refs, scratch = rest[:-1], rest[-1]
    width = own_ref.shape[1]
    values = tokens_ref[...].astype(jnp.float32)
    factor = lax.rsqrt(jnp.mean(values * values, axis=1, keepdims=True) + EPS)
    gain = jnp.where(mod_ref[...] == 1, gain_ref[1:2, :], gain_ref[0:1, :])
    scratch[...] = (values * factor * gain).astype(jnp.bfloat16)

    def columns(d):
        return pl.ds(pl.multiple_of((place[0] ^ d) * width, width), width)

    own_ref[...] = scratch[:, columns(0)]
    for d, ref in enumerate(send_refs, 1):
        rows = ref.shape[0]
        ref[...] = scratch[pl.ds(pl.multiple_of(place[1] * rows, rows), rows), columns(d)]


def norm_columns(tokens, norm_gain, mod, place, n, rows):
    length, depth = tokens.shape
    width = depth // n
    if width % 128:
        values32 = tokens.astype(jnp.float32)
        factor = lax.rsqrt(jnp.mean(values32 * values32, axis=1, keepdims=True) + EPS)
        gain = jnp.where((mod == 1)[:, None], norm_gain[1][None, :], norm_gain[0][None, :])
        normed = (values32 * factor * gain).astype(jnp.bfloat16)
        first = [0] + [place[1] * rows] * (n - 1)
        count = [length] + [rows] * (n - 1)
        return [
            lax.dynamic_slice(normed, (first[d], (place[0] ^ d) * width), (count[d], width))
            for d in range(n)
        ]
    shapes = [jax.ShapeDtypeStruct((length, width), jnp.bfloat16)]
    shapes += [jax.ShapeDtypeStruct((rows, width), jnp.bfloat16)] * (n - 1)
    return pl.pallas_call(
        norm_kernel,
        out_shape=shapes,
        in_specs=[SMEM, VMEM, VMEM, VMEM],
        out_specs=[VMEM] * n,
        scratch_shapes=[pltpu.VMEM((length, depth), jnp.bfloat16)],
        cost_estimate=pl.CostEstimate(
            flops=6 * length * depth, bytes_accessed=4 * length * depth, transcendentals=length
        ),
        compiler_params=pltpu.CompilerParams(vmem_limit_bytes=32 * 1024 * 1024),
        name="norm",
    )(place, tokens, norm_gain, mod[:, None])


def partial_kernel(counts, narrow, place, mod_ref, w_kv, w_q, *rest):
    total = sum(counts)
    refs, outs, (both, held_kv, held_q, arrived) = rest[:total], rest[total:-4], rest[-4:]
    copies = []
    for i, (weight, held) in enumerate(((w_kv, held_kv), (w_q, held_q))):
        copies.append(pltpu.make_async_copy(weight, held, arrived.at[i]))
        copies[-1].start()
    length, width = both.shape[0] // len(counts), both.shape[1]
    at = 0
    for number, count in enumerate(counts):
        base = number * length
        if count == 1:
            both[base : base + length] = refs[at][...]
        else:
            half = length // 2
            both[pl.ds(pl.multiple_of(base + place[1] * half, half), half)] = refs[at][...]
            both[pl.ds(pl.multiple_of(base + (1 - place[1]) * half, half), half)] = refs[at + 1][...]
        at += count
    block = both[...]
    generate = mod_ref[...] == 1
    zero = jnp.zeros_like(block)
    first, second = jnp.where(generate, zero, block), jnp.where(generate, block, zero)
    for i, held in enumerate((held_kv, held_q)):
        copies[i].wait()
        value = jnp.dot(first, held[:width], preferred_element_type=jnp.float32) + jnp.dot(
            second, held[width:], preferred_element_type=jnp.float32
        )
        outs[i][...] = value
        if narrow:
            outs[2 + i][...] = value.astype(jnp.bfloat16)


def partial(blocks, mods, w_kv, w_q, place, narrow):
    counts = tuple(len(block) for block in blocks)
    arrays = [array for block in blocks for array in block]
    length = mods[0].shape[0]
    rows, width = length * len(blocks), arrays[0].shape[1]
    kv_cols, q_cols = w_kv.shape[1], w_q.shape[1]
    shapes = [
        jax.ShapeDtypeStruct((rows, cols), dtype)
        for dtype in (jnp.float32, jnp.bfloat16)[: 1 + narrow]
        for cols in (kv_cols, q_cols)
    ]
    values = pl.pallas_call(
        functools.partial(partial_kernel, counts, narrow),
        out_shape=shapes,
        in_specs=[SMEM, VMEM, ANY, ANY] + [VMEM] * len(arrays),
        out_specs=[VMEM] * len(shapes),
        scratch_shapes=[
            pltpu.VMEM((rows, width), jnp.bfloat16),
            pltpu.VMEM(w_kv.shape, jnp.bfloat16),
            pltpu.VMEM(w_q.shape, jnp.bfloat16),
            pltpu.SemaphoreType.DMA((2,)),
        ],
        cost_estimate=pl.CostEstimate(
            flops=4 * rows * width * (kv_cols + q_cols),
            bytes_accessed=4 * (width + rows) * (kv_cols + q_cols),
            transcendentals=0,
        ),
        compiler_params=pltpu.CompilerParams(vmem_limit_bytes=40 * 1024 * 1024),
        name="partial",
    )(place, jnp.concatenate(mods)[:, None], w_kv, w_q, *arrays)
    return [value.reshape(len(blocks), length, -1) for value in values]


def halving(parts):
    n = len(parts)
    sums = dict(enumerate(parts))
    for bit in [1 << i for i in range(n.bit_length() - 1)]:
        for d in [d for d in range(n) if d in sums and d & bit]:
            sums[d ^ bit] = sums[d ^ bit] + cross(sums.pop(d).astype(jnp.bfloat16), "seq", bit)
    return sums[0].astype(jnp.bfloat16)


def along_four(parts, three, two):
    wide = [p.astype(jnp.float32) for p in parts]

    def hop(value, bit, among):
        return cross(value, "seq", bit, among).astype(jnp.float32)

    if two is None:
        got = hop(three, 1, (1, 2))
        send = (jnp.stack([wide[2], wide[3]]) + got).astype(jnp.bfloat16)
        got = hop(send, 3, (1, 2))
        across, own = got[0], got[1]
    else:
        far = hop(three, 1, (1, 2))
        close = hop(two, 1, (1, 2))
        send = (wide[2] + far).astype(jnp.bfloat16)
        across = hop(send, 3, (1, 2))
        own = hop((wide[3] + after(close, send)).astype(jnp.bfloat16), 3, (1, 2))
    last = hop((wide[1] + across).astype(jnp.bfloat16), 1, None)
    return (wide[0] + last + own).astype(jnp.bfloat16)


def gather_weights(mine):
    n = lax.axis_size("seq")
    if n == 4:
        z = lax.axis_index("seq")
        inner = (z == 1) | (z == 2)
        one = cross(mine, "seq", 1)
        middle = cross(mine, "seq", 3, (1, 2))
        middle_two = cross(one, "seq", 3, (1, 2))
        outer_two = cross(middle, "seq", 1, (0, 3))
        outer_three = cross(middle_two, "seq", 1, (0, 3))
        near = [mine, one, jnp.where(inner, middle_two, outer_two), jnp.where(inner, middle, outer_three)]
    else:
        near = [mine]
        for bit in reversed([1 << i for i in range(n.bit_length() - 1)]):
            got = cross(jnp.stack(near), "seq", bit)
            near = near + [got[i] for i in range(len(near))]
        order = [0]
        for bit in reversed([1 << i for i in range(n.bit_length() - 1)]):
            order = order + [d ^ bit for d in order]
        near = [near[order.index(d)] for d in range(n)]
    far = []
    for d in range(1, n):
        far.append(swap(near[d], "grp"))
    return near[1:], far


def spans(modality, doc_ids, own_mod, own_doc, own_pos):
    changed = (modality[1:] != modality[:-1]) | (doc_ids[1:] != doc_ids[:-1])
    begins = jnp.concatenate([jnp.ones((1,), jnp.int32), changed.astype(jnp.int32)])
    blocks = jnp.cumsum(begins)
    own_block = lax.dynamic_slice_in_dim(blocks, own_pos[0], own_pos.shape[0])
    low = jnp.sum((doc_ids[None, :] < own_doc[:, None]).astype(jnp.int32), axis=1)
    end = jnp.sum((blocks[None, :] <= own_block[:, None]).astype(jnp.int32), axis=1) - 1
    return low, jnp.where(own_mod == 1, end, own_pos)


def attention_kernel(starts, limits, q_ref, kv_ref, low_ref, high_ref, o_ref, top, total, acc):
    count, size, _ = kv_ref.shape
    rows = q_ref.shape[0]
    heads = q_ref.shape[1] // HEAD_DIM
    kv_local = kv_ref.shape[2] // (2 * HEAD_DIM)
    repeat = heads // kv_local
    scale = 1.0 / math.sqrt(HEAD_DIM)
    top[...] = jnp.full_like(top, LOW)
    total[...] = jnp.zeros_like(total)
    acc[...] = jnp.zeros_like(acc)

    def visit(number, _):
        start = starts[number]

        @pl.when((start <= limits[1]) & (start + size > limits[0]))
        def _():
            key_pos = start + lax.broadcasted_iota(jnp.int32, (rows, size), 1)
            seen = (key_pos >= low_ref[...]) & (key_pos <= high_ref[...])
            for head in range(heads):
                g = head // repeat
                keys = kv_ref[number, :, g * HEAD_DIM : (g + 1) * HEAD_DIM]
                values = kv_ref[number, :, (kv_local + g) * HEAD_DIM : (kv_local + g + 1) * HEAD_DIM]
                query = q_ref[:, head * HEAD_DIM : (head + 1) * HEAD_DIM]
                scores = lax.dot_general(
                    query, keys, (((1,), (1,)), ((), ())), preferred_element_type=jnp.float32
                )
                scores = jnp.where(seen, scores * scale, LOW)
                old = top[head][:, :1]
                new = jnp.maximum(old, jnp.max(scores, axis=1, keepdims=True))
                weights = jnp.where(seen, jnp.exp(scores - new), 0.0)
                shrink = jnp.exp(old - new)
                total[head] = jnp.broadcast_to(
                    total[head][:, :1] * shrink + jnp.sum(weights, axis=1, keepdims=True),
                    (rows, HEAD_DIM),
                )
                top[head] = jnp.broadcast_to(new, (rows, HEAD_DIM))
                acc[head] = acc[head] * shrink + jnp.dot(
                    weights.astype(jnp.bfloat16), values, preferred_element_type=jnp.float32
                )

        return 0

    lax.fori_loop(0, count, visit, 0)
    for head in range(heads):
        o_ref[:, head * HEAD_DIM : (head + 1) * HEAD_DIM] = (acc[head] / total[head]).astype(
            jnp.bfloat16
        )


def attend(query, kv, starts, low, high):
    rows, width = query.shape
    heads = width // HEAD_DIM
    count, size, _ = kv.shape
    vmem = pl.BlockSpec(memory_space=pltpu.VMEM)
    smem = pl.BlockSpec(memory_space=pltpu.SMEM)
    limits = jnp.stack([low[0], high[-1]])
    return pl.pallas_call(
        attention_kernel,
        out_shape=jax.ShapeDtypeStruct((rows, width), jnp.bfloat16),
        in_specs=[smem, smem, vmem, vmem, vmem, vmem],
        out_specs=vmem,
        scratch_shapes=[
            pltpu.VMEM((heads, rows, HEAD_DIM), jnp.float32),
            pltpu.VMEM((heads, rows, HEAD_DIM), jnp.float32),
            pltpu.VMEM((heads, rows, HEAD_DIM), jnp.float32),
        ],
        cost_estimate=pl.CostEstimate(
            flops=4 * rows * count * size * width,
            bytes_accessed=2 * (2 * rows * width + kv.size),
            transcendentals=rows * count * size * heads,
        ),
        compiler_params=pltpu.CompilerParams(vmem_limit_bytes=32 * 1024 * 1024),
        name="attend",
    )(starts, limits, query, kv, low[:, None], high[:, None])


def project_kernel(turns, place, ours_ref, beside_ref, ours_near, beside_near, own_ref, *rest):
    n = (len(rest) - 5) // 2 + 1
    near, far = rest[: n - 1], rest[n - 1 : 2 * n - 2]
    o_ours, o_beside, held, lhs, arrived = rest[2 * n - 2 :]
    count = turns.shape[0]
    first = place[2]

    def fetch(source, kind, d):
        slot = jnp.int32(-1)
        for i in range(count):
            slot = jnp.where(turns[i] == d, i, slot)

        @pl.when(slot >= 0)
        def _():
            at = jnp.maximum(slot, 0)
            pltpu.make_async_copy(source, held.at[kind, at], arrived.at[kind, at]).start()

    for d in range(n):
        fetch(near[d - 1] if d else own_ref.at[first], 0, d)
        fetch(far[d - 1] if d else own_ref.at[1 - first], 1, d)

    rows = ours_ref.shape[0]
    for base, a_ref, near_ref in ((0, ours_ref, ours_near), (rows, beside_ref, beside_near)):
        a = a_ref[...]
        mine = near_ref[...] != 0
        zero = jnp.zeros_like(a)
        lhs[0, base : base + rows] = jnp.where(mine, a, zero)
        lhs[1, base : base + rows] = jnp.where(mine, zero, a)
    contract = (((1,), (1,)), ((), ()))
    for i in range(count):
        value = None
        for kind in range(2):
            pltpu.make_async_copy(own_ref.at[0], held.at[kind, i], arrived.at[kind, i]).wait()
            term = lax.dot_general(
                lhs[kind], held[kind, i], contract, preferred_element_type=jnp.float32
            )
            value = term if value is None else value + term
        value = value.astype(jnp.bfloat16)
        o_ours[i] = value[:rows]
        o_beside[i] = value[rows:]


def project(ours, beside, ours_near, beside_near, weights, turns, place):
    rows, depth = ours.shape
    count = turns.shape[0]
    width = weights[0].shape[1]
    shape = jax.ShapeDtypeStruct((count, rows, width), jnp.bfloat16)
    return pl.pallas_call(
        project_kernel,
        out_shape=(shape, shape),
        in_specs=[SMEM, SMEM] + [VMEM] * 4 + [ANY] * len(weights),
        out_specs=(VMEM, VMEM),
        scratch_shapes=[
            pltpu.VMEM((2, count, width, depth), jnp.bfloat16),
            pltpu.VMEM((2, 2 * rows, depth), jnp.bfloat16),
            pltpu.SemaphoreType.DMA((2, count)),
        ],
        cost_estimate=pl.CostEstimate(
            flops=8 * count * rows * depth * width,
            bytes_accessed=4 * count * depth * width + 4 * count * rows * width,
            transcendentals=0,
        ),
        compiler_params=pltpu.CompilerParams(vmem_limit_bytes=32 * 1024 * 1024),
        name="project",
    )(turns, place, ours, beside, ours_near[:, None], beside_near[:, None], *weights)


def body(tokens, norm_gain, w_query, w_key, w_value, w_out, modality, doc_ids):
    length, depth = tokens.shape
    n = lax.axis_size("seq")
    subs = lax.axis_size("sub")
    heads_over = lax.axis_size("head")
    z, s = lax.axis_index("seq"), lax.axis_index("sub")
    x, y = lax.axis_index("head"), lax.axis_index("grp")
    width = depth // n
    place = jnp.stack([z, x, y]).astype(jnp.int32)

    kv_local = max(KV_HEADS // heads_over, 1)
    kv_first = x * KV_HEADS // heads_over
    w_out = jnp.swapaxes(w_out, 1, 2)

    def part_of(array, place, core):
        return lax.dynamic_slice_in_dim(array, (place * subs + core) * length, length)

    mine = lax.dynamic_index_in_dim(w_out, y, 0, keepdims=False)
    near, far = gather_weights(mine)
    weights = [w_out] + near + far

    own_mod = part_of(modality, z, s)
    share_rows = heads_over == 2
    rows = length // 2 if share_rows else length
    sends = norm_columns(tokens, norm_gain, own_mod, place, n, rows)
    blocks = {0: (sends[0],)}
    for d in range(n - 1, 0, -1):
        blocks[d] = (cross(sends[d], "seq", d),)

    w_query, w_key, w_value = after((w_query, w_key, w_value), sends[0])

    def share(weight):
        other = swap(weight, "sub")
        both = jnp.where(
            s == 0,
            jnp.concatenate([weight, other], axis=1),
            jnp.concatenate([other, weight], axis=1),
        )
        return both.reshape(2 * width, weight.shape[2])

    key_cols = lax.dynamic_slice_in_dim(w_key, kv_first * HEAD_DIM, kv_local * HEAD_DIM, 2)
    value_cols = lax.dynamic_slice_in_dim(w_value, kv_first * HEAD_DIM, kv_local * HEAD_DIM, 2)
    w_kv_all = share(jnp.concatenate([key_cols, value_cols], axis=2))
    w_q_all = share(w_query)
    modality, doc_ids = after((modality, doc_ids), sends[0])
    own_doc = part_of(doc_ids, z, s)
    own_pos = (z * subs + s) * length + jnp.arange(length, dtype=jnp.int32)
    low, high = spans(modality, doc_ids, part_of(modality, z, s), own_doc, own_pos)
    for d in range(1, n):
        blocks[d] = after(blocks[d], w_kv_all, w_q_all, low, high)

    if share_rows:
        for d in range(n - 1, 0, -1):
            blocks[d] = (*blocks[d], swap(blocks[d][0], "head"))

    def parts_of(group, narrow):
        mods = [part_of(modality, z ^ d, s) for d in group]
        return partial([blocks[d] for d in group], mods, w_kv_all, w_q_all, place, narrow)

    if n == 4:
        kv_early, q_early, kv_rounded, q_rounded = parts_of([3, 2], True)
        kv_ends, q_three, q_two = kv_rounded, q_rounded[0], q_rounded[1]
        kv_late, q_late = parts_of([1, 0], False)
        kv_early, q_early = after((kv_early, q_early), kv_late, q_late)
        kv = along_four([kv_late[1], kv_late[0], kv_early[1], kv_early[0]], kv_ends, None)
        query = along_four([q_late[1], q_late[0], q_early[1], q_early[0]], q_three, q_two)
    else:
        kv_parts, q_parts = [], []
        for d in range(n):
            kv_part, q_part = parts_of([d], False)
            kv_parts.append(kv_part[0])
            q_parts.append(q_part[0])
        kv, query = halving(kv_parts), halving(q_parts)

    same = [kv]
    for d in range(1, n):
        same.append(cross(kv, "seq", d))
    beside_0 = swap(kv, "sub")
    others = swap(jnp.stack(same[1:]), "sub")
    kv_all = jnp.concatenate([jnp.stack(same), beside_0[None], others])
    starts = jnp.stack(
        [((z ^ d) * subs + s) * length for d in range(n)]
        + [((z ^ d) * subs + (1 - s)) * length for d in range(n)]
    ).astype(jnp.int32)
    attended = attend(query, kv_all, starts, low, high)

    beside = swap(attended, "sub")
    ours_near = (own_mod == y).astype(jnp.bfloat16)
    beside_near = (part_of(modality, z, 1 - s) == y).astype(jnp.bfloat16)

    def out(columns):
        turns = (columns ^ z).astype(jnp.int32)
        return project(attended, beside, ours_near, beside_near, weights, turns, place)

    def placed(ours, theirs):
        sibling = swap(theirs, "sub")
        pair = jnp.where(s == 0, jnp.stack([ours, sibling], 1), jnp.stack([sibling, ours], 1))
        return jnp.transpose(pair, (2, 0, 1, 3)).reshape(length, -1)

    if heads_over != 2:
        wide = placed(*out(jnp.arange(n)))
        return lax.psum_scatter(wide, "head", scatter_dimension=1, tiled=True)

    half = jnp.arange(n // 2)
    send_ours, send_beside = out((1 - x) * (n // 2) + half)
    got_beside = swap(send_beside, "head")
    got_ours = swap(send_ours, "head")
    keep_ours, keep_beside = out(x * (n // 2) + half)
    return placed(add(keep_ours, got_ours), add(keep_beside, got_beside))


def solution(mesh):
    placed = (
        P(("grp", "seq", "sub"), None),
        P(),
        P(None, ("seq", "sub"), "head"),
        P(None, ("seq", "sub"), None),
        P(None, ("seq", "sub"), None),
        P(None, "head", ("seq", "sub")),
        P("grp"),
        P("grp"),
    )
    return jax.shard_map(
        body,
        mesh=mesh,
        in_specs=placed,
        out_specs=P(("grp", "seq", "sub"), "head"),
        check_vma=False,
    )
```

```python
import functools
import math

import jax
import jax.numpy as jnp
from jax import lax
from jax.experimental import pallas as pl
from jax.experimental.pallas import tpu as pltpu
from jax.sharding import PartitionSpec as P


HEAD_DIM = 128
KV_HEADS = 4
EPS = 1e-06
LOW = -1e30


def swap(x, axis):
    return lax.ppermute(x, axis, [(0, 1), (1, 0)])


def cross(x, axis, bit, among=None):
    size = lax.axis_size(axis)
    return lax.ppermute(x, axis, [(i ^ bit, i) for i in (among or range(size))])


def after(value, *done):
    return lax.optimization_barrier((value, *done))[0]


def add(a, b):
    return (a.astype(jnp.float32) + b.astype(jnp.float32)).astype(jnp.bfloat16)


VMEM = pl.BlockSpec(memory_space=pltpu.VMEM)
SMEM = pl.BlockSpec(memory_space=pltpu.SMEM)
HBM = pl.BlockSpec(memory_space=pltpu.HBM)


def norm_kernel(place, tokens_ref, gain_ref, mod_ref, own_ref, *rest):
    send_refs, scratch = rest[:-1], rest[-1]
    width = own_ref.shape[1]
    values = tokens_ref[...].astype(jnp.float32)
    factor = lax.rsqrt(jnp.mean(values * values, axis=1, keepdims=True) + EPS)
    gain = jnp.where(mod_ref[...] == 1, gain_ref[1:2, :], gain_ref[0:1, :])
    scratch[...] = (values * factor * gain).astype(jnp.bfloat16)

    def columns(d):
        return pl.ds(pl.multiple_of((place[0] ^ d) * width, width), width)

    own_ref[...] = scratch[:, columns(0)]
    for d, ref in enumerate(send_refs, 1):
        rows = ref.shape[0]
        ref[...] = scratch[pl.ds(pl.multiple_of(place[1] * rows, rows), rows), columns(d)]


def norm_columns(tokens, norm_gain, mod, place, n, rows):
    length, depth = tokens.shape
    width = depth // n
    if width % 128:
        values32 = tokens.astype(jnp.float32)
        factor = lax.rsqrt(jnp.mean(values32 * values32, axis=1, keepdims=True) + EPS)
        gain = jnp.where((mod == 1)[:, None], norm_gain[1][None, :], norm_gain[0][None, :])
        normed = (values32 * factor * gain).astype(jnp.bfloat16)
        first = [0] + [place[1] * rows] * (n - 1)
        count = [length] + [rows] * (n - 1)
        return [
            lax.dynamic_slice(normed, (first[d], (place[0] ^ d) * width), (count[d], width))
            for d in range(n)
        ]
    shapes = [jax.ShapeDtypeStruct((length, width), jnp.bfloat16)]
    shapes += [jax.ShapeDtypeStruct((rows, width), jnp.bfloat16)] * (n - 1)
    return pl.pallas_call(
        norm_kernel,
        out_shape=shapes,
        in_specs=[SMEM, VMEM, VMEM, VMEM],
        out_specs=[VMEM] * n,
        scratch_shapes=[pltpu.VMEM((length, depth), jnp.bfloat16)],
        cost_estimate=pl.CostEstimate(
            flops=6 * length * depth, bytes_accessed=4 * length * depth, transcendentals=length
        ),
        compiler_params=pltpu.CompilerParams(vmem_limit_bytes=32 * 1024 * 1024),
        name="norm",
    )(place, tokens, norm_gain, mod[:, None])


def partial_kernel(counts, narrow, place, mod_ref, *rest):
    total = sum(counts)
    sources, refs, outs = rest[:6], rest[6 : 6 + total], rest[6 + total : -4]
    both, held_kv, held_q, arrived = rest[-4:]
    kv_half = held_kv.shape[2] // 2
    depth = held_kv.shape[1] // 2
    copies = []
    for i, source in enumerate(sources):
        core = place[3] if i % 2 == 0 else 1 - place[3]
        at = pl.ds(pl.multiple_of(core * depth, depth), depth)
        target = (
            held_kv.at[:, at, 0:kv_half],
            held_kv.at[:, at, kv_half : 2 * kv_half],
            held_q.at[:, at],
        )[i // 2]
        copies.append(pltpu.make_async_copy(source, target, arrived.at[i]))
        copies[-1].start()
    length = both.shape[0] // len(counts)
    at = 0
    for number, count in enumerate(counts):
        base = number * length
        if count == 1:
            both[base : base + length] = refs[at][...]
        else:
            half = length // 2
            both[pl.ds(pl.multiple_of(base + place[1] * half, half), half)] = refs[at][...]
            both[pl.ds(pl.multiple_of(base + (1 - place[1]) * half, half), half)] = refs[at + 1][...]
        at += count
    block = both[...]
    generate = mod_ref[...] == 1
    zero = jnp.zeros_like(block)
    first, second = jnp.where(generate, zero, block), jnp.where(generate, block, zero)
    for i, held in enumerate((held_kv, held_q)):
        for copy in (copies[:4], copies[4:])[i]:
            copy.wait()
        value = jnp.dot(first, held[0], preferred_element_type=jnp.float32) + jnp.dot(
            second, held[1], preferred_element_type=jnp.float32
        )
        outs[i][...] = value
        if narrow:
            outs[2 + i][...] = value.astype(jnp.bfloat16)


def partial(blocks, mods, weights, place, narrow):
    counts = tuple(len(block) for block in blocks)
    arrays = [array for block in blocks for array in block]
    length = mods[0].shape[0]
    rows, width = length * len(blocks), arrays[0].shape[1]
    kv_cols, q_cols = 2 * weights[0].shape[2], weights[4].shape[2]
    shapes = [
        jax.ShapeDtypeStruct((rows, cols), dtype)
        for dtype in (jnp.float32, jnp.bfloat16)[: 1 + narrow]
        for cols in (kv_cols, q_cols)
    ]
    values = pl.pallas_call(
        functools.partial(partial_kernel, counts, narrow),
        out_shape=shapes,
        in_specs=[SMEM, VMEM] + [HBM] * len(weights) + [VMEM] * len(arrays),
        out_specs=[VMEM] * len(shapes),
        scratch_shapes=[
            pltpu.VMEM((rows, width), jnp.bfloat16),
            pltpu.VMEM((2, width, kv_cols), jnp.bfloat16),
            pltpu.VMEM((2, width, q_cols), jnp.bfloat16),
            pltpu.SemaphoreType.DMA((len(weights),)),
        ],
        cost_estimate=pl.CostEstimate(
            flops=4 * rows * width * (kv_cols + q_cols),
            bytes_accessed=4 * (width + rows) * (kv_cols + q_cols),
            transcendentals=0,
        ),
        compiler_params=pltpu.CompilerParams(vmem_limit_bytes=40 * 1024 * 1024),
        name="partial",
    )(place, jnp.concatenate(mods)[:, None], *weights, *arrays)
    return [value.reshape(len(blocks), length, -1) for value in values]


def halving(parts):
    n = len(parts)
    sums = dict(enumerate(parts))
    for bit in [1 << i for i in range(n.bit_length() - 1)]:
        for d in [d for d in range(n) if d in sums and d & bit]:
            sums[d ^ bit] = sums[d ^ bit] + cross(sums.pop(d).astype(jnp.bfloat16), "seq", bit)
    return sums[0].astype(jnp.bfloat16)


def along_four(parts, three, two):
    wide = [p.astype(jnp.float32) for p in parts]

    def hop(value, bit, among):
        return cross(value, "seq", bit, among).astype(jnp.float32)

    if two is None:
        got = hop(three, 1, (1, 2))
        send = (jnp.stack([wide[2], wide[3]]) + got).astype(jnp.bfloat16)
        got = hop(send, 3, (1, 2))
        across, own = got[0], got[1]
    else:
        far = hop(three, 1, (1, 2))
        close = hop(two, 1, (1, 2))
        send = (wide[2] + far).astype(jnp.bfloat16)
        across = hop(send, 3, (1, 2))
        own = hop((wide[3] + after(close, send)).astype(jnp.bfloat16), 3, (1, 2))
    last = hop((wide[1] + across).astype(jnp.bfloat16), 1, None)
    return (wide[0] + last + own).astype(jnp.bfloat16)


def gather_weights(mine):
    n = lax.axis_size("seq")
    if n == 4:
        z = lax.axis_index("seq")
        inner = (z == 1) | (z == 2)
        one = cross(mine, "seq", 1)
        middle = cross(mine, "seq", 3, (1, 2))
        middle_two = cross(one, "seq", 3, (1, 2))
        outer_two = cross(middle, "seq", 1, (0, 3))
        outer_three = cross(middle_two, "seq", 1, (0, 3))
        near = [mine, one, jnp.where(inner, middle_two, outer_two), jnp.where(inner, middle, outer_three)]
    else:
        near = [mine]
        for bit in reversed([1 << i for i in range(n.bit_length() - 1)]):
            got = cross(jnp.stack(near), "seq", bit)
            near = near + [got[i] for i in range(len(near))]
        order = [0]
        for bit in reversed([1 << i for i in range(n.bit_length() - 1)]):
            order = order + [d ^ bit for d in order]
        near = [near[order.index(d)] for d in range(n)]
    far = []
    for d in range(1, n):
        far.append(swap(near[d], "grp"))
    return near[1:], far


def spans(modality, doc_ids, own_mod, own_doc, own_pos):
    changed = (modality[1:] != modality[:-1]) | (doc_ids[1:] != doc_ids[:-1])
    begins = jnp.concatenate([jnp.ones((1,), jnp.int32), changed.astype(jnp.int32)])
    blocks = jnp.cumsum(begins)
    own_block = lax.dynamic_slice_in_dim(blocks, own_pos[0], own_pos.shape[0])
    low = jnp.sum((doc_ids[None, :] < own_doc[:, None]).astype(jnp.int32), axis=1)
    end = jnp.sum((blocks[None, :] <= own_block[:, None]).astype(jnp.int32), axis=1) - 1
    return low, jnp.where(own_mod == 1, end, own_pos)


def attention_kernel(starts, limits, q_ref, kv_ref, low_ref, high_ref, o_ref, top, total, acc):
    count, size, _ = kv_ref.shape
    rows = q_ref.shape[0]
    heads = q_ref.shape[1] // HEAD_DIM
    kv_local = kv_ref.shape[2] // (2 * HEAD_DIM)
    repeat = heads // kv_local
    scale = math.log2(math.e) / math.sqrt(HEAD_DIM)
    top[...] = jnp.full_like(top, LOW / 10)
    total[...] = jnp.zeros_like(total)
    acc[...] = jnp.zeros_like(acc)
    transposed = (((1,), (1,)), ((), ()))

    def visit(number, _):
        start = starts[number]
        last = start + size - 1

        def block(masked):
            if masked:
                key_pos = start + lax.broadcasted_iota(jnp.int32, (size, rows), 0)
                seen = (key_pos >= low_ref[...]) & (key_pos <= high_ref[...])
            for g in range(kv_local):
                keys = kv_ref[number, :, g * HEAD_DIM : (g + 1) * HEAD_DIM]
                values = kv_ref[number, :, (kv_local + g) * HEAD_DIM : (kv_local + g + 1) * HEAD_DIM]
                values = values.T
                for head in range(g * repeat, (g + 1) * repeat):
                    query = q_ref[:, head * HEAD_DIM : (head + 1) * HEAD_DIM]
                    scores = lax.dot_general(
                        keys, query, transposed, preferred_element_type=jnp.float32
                    )
                    if masked:
                        scores = jnp.where(seen, scores, LOW)
                    old = top[head : head + 1]
                    new = jnp.maximum(old, jnp.max(scores, axis=0, keepdims=True))
                    weights = jnp.exp2((scores - new) * scale)
                    shrink = jnp.exp2((old - new) * scale)
                    total[head : head + 1] = total[head : head + 1] * shrink + jnp.sum(
                        weights, axis=0, keepdims=True
                    )
                    top[head : head + 1] = new
                    acc[head] = acc[head] * shrink + jnp.dot(
                        values, weights.astype(jnp.bfloat16), preferred_element_type=jnp.float32
                    )

        inside = (start >= limits[2]) & (last <= limits[3])

        @pl.when(inside)
        def _():
            block(False)

        @pl.when(jnp.logical_not(inside) & (start <= limits[1]) & (last >= limits[0]))
        def _():
            block(True)

        return 0

    lax.fori_loop(0, count, visit, 0)
    for head in range(heads):
        o_ref[:, head * HEAD_DIM : (head + 1) * HEAD_DIM] = (
            (acc[head] / total[head : head + 1]).T.astype(jnp.bfloat16)
        )


def attend(query, kv, starts, low, high):
    rows, width = query.shape
    heads = width // HEAD_DIM
    count, size, _ = kv.shape
    limits = jnp.stack([low[0], high[-1], low[-1], high[0]])
    return pl.pallas_call(
        attention_kernel,
        out_shape=jax.ShapeDtypeStruct((rows, width), jnp.bfloat16),
        in_specs=[SMEM, SMEM, VMEM, VMEM, VMEM, VMEM],
        out_specs=VMEM,
        scratch_shapes=[
            pltpu.VMEM((heads, rows), jnp.float32),
            pltpu.VMEM((heads, rows), jnp.float32),
            pltpu.VMEM((heads, HEAD_DIM, rows), jnp.float32),
        ],
        cost_estimate=pl.CostEstimate(
            flops=4 * rows * count * size * width,
            bytes_accessed=2 * (2 * rows * width + kv.size),
            transcendentals=rows * count * size * heads,
        ),
        compiler_params=pltpu.CompilerParams(vmem_limit_bytes=32 * 1024 * 1024),
        name="attend",
    )(starts, limits, query, kv, low[None, :], high[None, :])


def project_kernel(turns, place, ours_ref, beside_ref, ours_near, beside_near, own_ref, *rest):
    n = (len(rest) - 5) // 2 + 1
    near, far = rest[: n - 1], rest[n - 1 : 2 * n - 2]
    o_ours, o_beside, held, lhs, arrived = rest[2 * n - 2 :]
    count = turns.shape[0]
    first = place[2]

    def fetch(source, kind, d):
        slot = jnp.int32(-1)
        for i in range(count):
            slot = jnp.where(turns[i] == d, i, slot)

        @pl.when(slot >= 0)
        def _():
            at = jnp.maximum(slot, 0)
            pltpu.make_async_copy(source, held.at[kind, at], arrived.at[kind, at]).start()

    for d in range(n):
        fetch(near[d - 1] if d else own_ref.at[first], 0, d)
        fetch(far[d - 1] if d else own_ref.at[1 - first], 1, d)

    rows = ours_ref.shape[0]
    for base, a_ref, near_ref in ((0, ours_ref, ours_near), (rows, beside_ref, beside_near)):
        a = a_ref[...]
        mine = near_ref[...] != 0
        zero = jnp.zeros_like(a)
        lhs[0, base : base + rows] = jnp.where(mine, a, zero)
        lhs[1, base : base + rows] = jnp.where(mine, zero, a)
    contract = (((1,), (1,)), ((), ()))
    for i in range(count):
        value = None
        for kind in range(2):
            pltpu.make_async_copy(own_ref.at[0], held.at[kind, i], arrived.at[kind, i]).wait()
            term = lax.dot_general(
                lhs[kind], held[kind, i], contract, preferred_element_type=jnp.float32
            )
            value = term if value is None else value + term
        value = value.astype(jnp.bfloat16)
        o_ours[i] = value[:rows]
        o_beside[i] = value[rows:]


def project(ours, beside, ours_near, beside_near, weights, turns, place):
    rows, depth = ours.shape
    count = turns.shape[0]
    width = weights[0].shape[1]
    shape = jax.ShapeDtypeStruct((count, rows, width), jnp.bfloat16)
    return pl.pallas_call(
        project_kernel,
        out_shape=(shape, shape),
        in_specs=[SMEM, SMEM] + [VMEM] * 4 + [HBM] * len(weights),
        out_specs=(VMEM, VMEM),
        scratch_shapes=[
            pltpu.VMEM((2, count, width, depth), jnp.bfloat16),
            pltpu.VMEM((2, 2 * rows, depth), jnp.bfloat16),
            pltpu.SemaphoreType.DMA((2, count)),
        ],
        cost_estimate=pl.CostEstimate(
            flops=8 * count * rows * depth * width,
            bytes_accessed=4 * count * depth * width + 4 * count * rows * width,
            transcendentals=0,
        ),
        compiler_params=pltpu.CompilerParams(vmem_limit_bytes=32 * 1024 * 1024),
        name="project",
    )(turns, place, ours, beside, ours_near[:, None], beside_near[:, None], *weights)


def body(tokens, norm_gain, w_query, w_key, w_value, w_out, modality, doc_ids):
    length, _ = tokens.shape
    n = lax.axis_size("seq")
    subs = lax.axis_size("sub")
    heads_over = lax.axis_size("head")
    z, s = lax.axis_index("seq"), lax.axis_index("sub")
    x, y = lax.axis_index("head"), lax.axis_index("grp")
    place = jnp.stack([z, x, y, s]).astype(jnp.int32)

    kv_local = max(KV_HEADS // heads_over, 1)
    kv_first = x * KV_HEADS // heads_over
    w_out = jnp.swapaxes(w_out, 1, 2)

    def part_of(array, place, core):
        return lax.dynamic_slice_in_dim(array, (place * subs + core) * length, length)

    mine = lax.dynamic_index_in_dim(w_out, y, 0, keepdims=False)
    near, far = gather_weights(mine)
    weights = [w_out] + near + far

    own_mod = part_of(modality, z, s)
    share_rows = heads_over == 2
    rows = length // 2 if share_rows else length
    sends = norm_columns(tokens, norm_gain, own_mod, place, n, rows)
    blocks = {0: (sends[0],)}
    for d in range(n - 1, 0, -1):
        blocks[d] = (cross(sends[d], "seq", d),)

    w_query, w_key, w_value = after((w_query, w_key, w_value), sends[0])

    key_cols = lax.dynamic_slice_in_dim(w_key, kv_first * HEAD_DIM, kv_local * HEAD_DIM, 2)
    value_cols = lax.dynamic_slice_in_dim(w_value, kv_first * HEAD_DIM, kv_local * HEAD_DIM, 2)
    row_weights = []
    for weight in (key_cols, value_cols, w_query):
        row_weights += [weight, swap(weight, "sub")]
    modality, doc_ids = after((modality, doc_ids), sends[0])
    own_doc = part_of(doc_ids, z, s)
    own_pos = (z * subs + s) * length + jnp.arange(length, dtype=jnp.int32)
    low, high = spans(modality, doc_ids, part_of(modality, z, s), own_doc, own_pos)
    blocks[1] = after(blocks[1], low, high)

    if share_rows:
        for d in range(n - 1, 0, -1):
            blocks[d] = (*blocks[d], swap(blocks[d][0], "head"))

    def parts_of(group, narrow):
        mods = [part_of(modality, z ^ d, s) for d in group]
        return partial([blocks[d] for d in group], mods, row_weights, place, narrow)

    if n == 4:
        kv_early, q_early, kv_rounded, q_rounded = parts_of([3, 2], True)
        kv_ends, q_three, q_two = kv_rounded, q_rounded[0], q_rounded[1]
        kv_late, q_late = parts_of([1, 0], False)
        kv_early, q_early = after((kv_early, q_early), kv_late, q_late)
        kv = along_four([kv_late[1], kv_late[0], kv_early[1], kv_early[0]], kv_ends, None)
        query = along_four([q_late[1], q_late[0], q_early[1], q_early[0]], q_three, q_two)
    else:
        kv_parts, q_parts = [], []
        for d in range(n):
            kv_part, q_part = parts_of([d], False)
            kv_parts.append(kv_part[0])
            q_parts.append(q_part[0])
        kv, query = halving(kv_parts), halving(q_parts)

    same = [kv]
    for d in range(1, n):
        same.append(cross(kv, "seq", d))
    beside_0 = swap(kv, "sub")
    others = swap(jnp.stack(same[1:]), "sub")
    kv_all = jnp.concatenate([jnp.stack(same), beside_0[None], others])
    starts = jnp.stack(
        [((z ^ d) * subs + s) * length for d in range(n)]
        + [((z ^ d) * subs + (1 - s)) * length for d in range(n)]
    ).astype(jnp.int32)
    attended = attend(query, kv_all, starts, low, high)

    beside = swap(attended, "sub")
    ours_near = (own_mod == y).astype(jnp.bfloat16)
    beside_near = (part_of(modality, z, 1 - s) == y).astype(jnp.bfloat16)

    def out(columns):
        turns = (columns ^ z).astype(jnp.int32)
        return project(attended, beside, ours_near, beside_near, weights, turns, place)

    def placed(ours, theirs):
        sibling = swap(theirs, "sub")
        pair = jnp.where(s == 0, jnp.stack([ours, sibling], 1), jnp.stack([sibling, ours], 1))
        return jnp.transpose(pair, (2, 0, 1, 3)).reshape(length, -1)

    if heads_over != 2:
        wide = placed(*out(jnp.arange(n)))
        return lax.psum_scatter(wide, "head", scatter_dimension=1, tiled=True)

    half = jnp.arange(n // 2)
    send_ours, send_beside = out((1 - x) * (n // 2) + half)
    got_beside = swap(send_beside, "head")
    got_ours = swap(send_ours, "head")
    keep_ours, keep_beside = out(x * (n // 2) + half)
    return placed(add(keep_ours, got_ours), add(keep_beside, got_beside))


def solution(mesh):
    placed = (
        P(("grp", "seq", "sub"), None),
        P(),
        P(None, ("seq", "sub"), "head"),
        P(None, ("seq", "sub"), None),
        P(None, ("seq", "sub"), None),
        P(None, "head", ("seq", "sub")),
        P("grp"),
        P("grp"),
    )
    return jax.shard_map(
        body,
        mesh=mesh,
        in_specs=placed,
        out_specs=P(("grp", "seq", "sub"), "head"),
        check_vma=False,
    )
```

```python
import functools
import math

import jax
import jax.numpy as jnp
from jax import lax
from jax.experimental import pallas as pl
from jax.experimental.pallas import tpu as pltpu
from jax.sharding import PartitionSpec as P


HEAD_DIM = 128
KV_HEADS = 4
EPS = 1e-06
LOW = -1e30


def swap(x, axis):
    return lax.ppermute(x, axis, [(0, 1), (1, 0)])


def cross(x, axis, bit, among=None):
    size = lax.axis_size(axis)
    return lax.ppermute(x, axis, [(i ^ bit, i) for i in (among or range(size))])


def after(value, *done):
    return lax.optimization_barrier((value, *done))[0]


def add(a, b):
    return (a.astype(jnp.float32) + b.astype(jnp.float32)).astype(jnp.bfloat16)


VMEM = pl.BlockSpec(memory_space=pltpu.VMEM)
SMEM = pl.BlockSpec(memory_space=pltpu.SMEM)
HBM = pl.BlockSpec(memory_space=pltpu.HBM)


def in_hbm(x):
    return pltpu.with_memory_space_constraint(x, pltpu.HBM)


def norm_kernel(place, tokens_ref, gain_ref, mod_ref, own_ref, *rest):
    send_refs, scratch = rest[:-1], rest[-1]
    width = own_ref.shape[1]
    values = tokens_ref[...].astype(jnp.float32)
    factor = lax.rsqrt(jnp.mean(values * values, axis=1, keepdims=True) + EPS)
    gain = jnp.where(mod_ref[...] == 1, gain_ref[1:2, :], gain_ref[0:1, :])
    scratch[...] = (values * factor * gain).astype(jnp.bfloat16)

    def columns(d):
        return pl.ds(pl.multiple_of((place[0] ^ d) * width, width), width)

    own_ref[...] = scratch[:, columns(0)]
    for d, ref in enumerate(send_refs, 1):
        rows = ref.shape[0]
        ref[...] = scratch[pl.ds(pl.multiple_of(place[1] * rows, rows), rows), columns(d)]


def norm_columns(tokens, norm_gain, mod, place, n, rows):
    length, depth = tokens.shape
    width = depth // n
    if width % 128:
        values32 = tokens.astype(jnp.float32)
        factor = lax.rsqrt(jnp.mean(values32 * values32, axis=1, keepdims=True) + EPS)
        gain = jnp.where((mod == 1)[:, None], norm_gain[1][None, :], norm_gain[0][None, :])
        normed = (values32 * factor * gain).astype(jnp.bfloat16)
        first = [0] + [place[1] * rows] * (n - 1)
        count = [length] + [rows] * (n - 1)
        return [
            lax.dynamic_slice(normed, (first[d], (place[0] ^ d) * width), (count[d], width))
            for d in range(n)
        ]
    shapes = [jax.ShapeDtypeStruct((length, width), jnp.bfloat16)]
    shapes += [jax.ShapeDtypeStruct((rows, width), jnp.bfloat16)] * (n - 1)
    return pl.pallas_call(
        norm_kernel,
        out_shape=shapes,
        in_specs=[SMEM, VMEM, VMEM, VMEM],
        out_specs=[VMEM] * n,
        scratch_shapes=[pltpu.VMEM((length, depth), jnp.bfloat16)],
        cost_estimate=pl.CostEstimate(
            flops=6 * length * depth, bytes_accessed=4 * length * depth, transcendentals=length
        ),
        compiler_params=pltpu.CompilerParams(vmem_limit_bytes=32 * 1024 * 1024),
        name="norm",
    )(place, tokens, norm_gain, mod[:, None])


def partial_kernel(counts, narrow, place, mod_ref, *rest):
    total = sum(counts)
    sources, refs, outs = rest[:6], rest[6 : 6 + total], rest[6 + total : -4]
    both, held_kv, held_q, arrived = rest[-4:]
    kv_half = held_kv.shape[2] // 2
    depth = held_kv.shape[1] // 2
    copies = []
    for i, source in enumerate(sources):
        core = place[3] if i % 2 == 0 else 1 - place[3]
        at = pl.ds(pl.multiple_of(core * depth, depth), depth)
        target = (
            held_kv.at[:, at, 0:kv_half],
            held_kv.at[:, at, kv_half : 2 * kv_half],
            held_q.at[:, at],
        )[i // 2]
        copies.append(pltpu.make_async_copy(source, target, arrived.at[i]))
        copies[-1].start()
    length = both.shape[0] // len(counts)
    at = 0
    for number, count in enumerate(counts):
        base = number * length
        if count == 1:
            both[base : base + length] = refs[at][...]
        else:
            half = length // 2
            both[pl.ds(pl.multiple_of(base + place[1] * half, half), half)] = refs[at][...]
            both[pl.ds(pl.multiple_of(base + (1 - place[1]) * half, half), half)] = refs[at + 1][...]
        at += count
    block = both[...]
    generate = mod_ref[...] == 1
    zero = jnp.zeros_like(block)
    first, second = jnp.where(generate, zero, block), jnp.where(generate, block, zero)
    for i, held in enumerate((held_kv, held_q)):
        for copy in (copies[:4], copies[4:])[i]:
            copy.wait()
        value = jnp.dot(first, held[0], preferred_element_type=jnp.float32) + jnp.dot(
            second, held[1], preferred_element_type=jnp.float32
        )
        outs[i][...] = value
        if narrow:
            outs[2 + i][...] = value.astype(jnp.bfloat16)


def partial(blocks, mods, weights, place, narrow):
    counts = tuple(len(block) for block in blocks)
    arrays = [array for block in blocks for array in block]
    length = mods[0].shape[0]
    rows, width = length * len(blocks), arrays[0].shape[1]
    kv_cols, q_cols = 2 * weights[0].shape[2], weights[4].shape[2]
    shapes = [
        jax.ShapeDtypeStruct((rows, cols), dtype)
        for dtype in (jnp.float32, jnp.bfloat16)[: 1 + narrow]
        for cols in (kv_cols, q_cols)
    ]
    values = pl.pallas_call(
        functools.partial(partial_kernel, counts, narrow),
        out_shape=shapes,
        in_specs=[SMEM, VMEM] + [HBM] * len(weights) + [VMEM] * len(arrays),
        out_specs=[VMEM] * len(shapes),
        scratch_shapes=[
            pltpu.VMEM((rows, width), jnp.bfloat16),
            pltpu.VMEM((2, width, kv_cols), jnp.bfloat16),
            pltpu.VMEM((2, width, q_cols), jnp.bfloat16),
            pltpu.SemaphoreType.DMA((len(weights),)),
        ],
        cost_estimate=pl.CostEstimate(
            flops=4 * rows * width * (kv_cols + q_cols),
            bytes_accessed=4 * (width + rows) * (kv_cols + q_cols),
            transcendentals=0,
        ),
        compiler_params=pltpu.CompilerParams(vmem_limit_bytes=40 * 1024 * 1024),
        name="partial",
    )(place, jnp.concatenate(mods)[:, None], *[in_hbm(w) for w in weights], *arrays)
    return [value.reshape(len(blocks), length, -1) for value in values]


def halving(parts):
    n = len(parts)
    sums = dict(enumerate(parts))
    for bit in [1 << i for i in range(n.bit_length() - 1)]:
        for d in [d for d in range(n) if d in sums and d & bit]:
            sums[d ^ bit] = sums[d ^ bit] + cross(sums.pop(d).astype(jnp.bfloat16), "seq", bit)
    return sums[0].astype(jnp.bfloat16)


def along_four(parts, three, two):
    wide = [p.astype(jnp.float32) for p in parts]

    def hop(value, bit, among):
        return cross(value, "seq", bit, among)

    def plus(a, b):
        return (a + b.astype(jnp.float32)).astype(jnp.bfloat16)

    if two is None:
        got = hop(three, 1, (1, 2))
        got = hop(plus(jnp.stack([wide[2], wide[3]]), got), 3, (1, 2))
        across, own = got[0], got[1]
    else:
        far = hop(three, 1, (1, 2))
        close = hop(two, 1, (1, 2))
        send = plus(wide[2], far)
        across = hop(send, 3, (1, 2))
        own = hop(plus(wide[3], after(close, send)), 3, (1, 2))
    last = hop(plus(wide[1], across), 1, None)
    return (wide[0] + last.astype(jnp.float32) + own.astype(jnp.float32)).astype(jnp.bfloat16)


def gather_weights(mine):
    n = lax.axis_size("seq")
    if n == 4:
        z = lax.axis_index("seq")
        inner = (z == 1) | (z == 2)
        one = cross(mine, "seq", 1)
        middle = cross(mine, "seq", 3, (1, 2))
        middle_two = cross(one, "seq", 3, (1, 2))
        outer_two = cross(middle, "seq", 1, (0, 3))
        outer_three = cross(middle_two, "seq", 1, (0, 3))
        near = [mine, one, jnp.where(inner, middle_two, outer_two), jnp.where(inner, middle, outer_three)]
    else:
        near = [mine]
        for bit in reversed([1 << i for i in range(n.bit_length() - 1)]):
            got = cross(jnp.stack(near), "seq", bit)
            near = near + [got[i] for i in range(len(near))]
        order = [0]
        for bit in reversed([1 << i for i in range(n.bit_length() - 1)]):
            order = order + [d ^ bit for d in order]
        near = [near[order.index(d)] for d in range(n)]
    far = []
    for d in range(1, n):
        far.append(swap(near[d], "grp"))
    return near[1:], far


def spans(modality, doc_ids, own_mod, own_doc, own_pos):
    changed = (modality[1:] != modality[:-1]) | (doc_ids[1:] != doc_ids[:-1])
    begins = jnp.concatenate([jnp.ones((1,), jnp.int32), changed.astype(jnp.int32)])
    blocks = jnp.cumsum(begins)
    own_block = lax.dynamic_slice_in_dim(blocks, own_pos[0], own_pos.shape[0])
    low = jnp.sum((doc_ids[None, :] < own_doc[:, None]).astype(jnp.int32), axis=1)
    end = jnp.sum((blocks[None, :] <= own_block[:, None]).astype(jnp.int32), axis=1) - 1
    return low, jnp.where(own_mod == 1, end, own_pos)


def attention_kernel(starts, limits, q_ref, kv_ref, low_ref, high_ref, o_ref, queries, top, total, acc):
    count, size, _ = kv_ref.shape
    rows = q_ref.shape[0]
    kv_local, many = queries.shape[0], queries.shape[1]
    repeat = many // rows
    scale = math.log2(math.e) / math.sqrt(HEAD_DIM)
    top[...] = jnp.full_like(top, LOW / 10)
    total[...] = jnp.zeros_like(total)
    acc[...] = jnp.zeros_like(acc)
    for head in range(kv_local * repeat):
        g, r = head // repeat, head % repeat
        queries[g, r * rows : (r + 1) * rows] = q_ref[:, head * HEAD_DIM : (head + 1) * HEAD_DIM]
    transposed = (((1,), (1,)), ((), ()))

    def visit(number, _):
        start = starts[number]
        last = start + size - 1

        def block(masked):
            for g in range(kv_local):
                keys = kv_ref[number, :, g * HEAD_DIM : (g + 1) * HEAD_DIM]
                values = kv_ref[number, :, (kv_local + g) * HEAD_DIM : (kv_local + g + 1) * HEAD_DIM]
                scores = lax.dot_general(
                    queries[g], keys, transposed, preferred_element_type=jnp.float32
                )
                if masked:
                    key_pos = start + lax.broadcasted_iota(jnp.int32, (many, size), 1)
                    seen = (key_pos >= low_ref[...]) & (key_pos <= high_ref[...])
                    scores = jnp.where(seen, scores, LOW)
                old = top[g]
                new = jnp.maximum(old, jnp.max(scores, axis=1, keepdims=True))
                weights = jnp.exp2((scores - jnp.tile(new, (1, size // 128))) * scale)
                shrink = jnp.exp2((old - new) * scale)
                total[g] = total[g] * shrink + jnp.sum(weights, axis=1, keepdims=True)
                top[g] = new
                acc[g] = acc[g] * shrink + jnp.dot(
                    weights.astype(jnp.bfloat16), values, preferred_element_type=jnp.float32
                )

        inside = (start >= limits[2]) & (last <= limits[3])

        @pl.when(inside)
        def _():
            block(False)

        @pl.when(jnp.logical_not(inside) & (start <= limits[1]) & (last >= limits[0]))
        def _():
            block(True)

        return 0

    lax.fori_loop(0, count, visit, 0)
    for head in range(kv_local * repeat):
        g, at = head // repeat, pl.ds((head % repeat) * rows, rows)
        o_ref[:, head * HEAD_DIM : (head + 1) * HEAD_DIM] = (acc[g, at] / total[g, at]).astype(
            jnp.bfloat16
        )


def attend(query, kv, starts, low, high):
    rows, width = query.shape
    heads = width // HEAD_DIM
    count, size, _ = kv.shape
    kv_local = kv.shape[2] // (2 * HEAD_DIM)
    many = rows * heads // kv_local
    limits = jnp.stack([low[0], high[-1], low[-1], high[0]])
    return pl.pallas_call(
        attention_kernel,
        out_shape=jax.ShapeDtypeStruct((rows, width), jnp.bfloat16),
        in_specs=[SMEM, SMEM, VMEM, VMEM, VMEM, VMEM],
        out_specs=VMEM,
        scratch_shapes=[
            pltpu.VMEM((kv_local, many, HEAD_DIM), jnp.bfloat16),
            pltpu.VMEM((kv_local, many, HEAD_DIM), jnp.float32),
            pltpu.VMEM((kv_local, many, HEAD_DIM), jnp.float32),
            pltpu.VMEM((kv_local, many, HEAD_DIM), jnp.float32),
        ],
        cost_estimate=pl.CostEstimate(
            flops=4 * rows * count * size * width,
            bytes_accessed=2 * (2 * rows * width + kv.size),
            transcendentals=rows * count * size * heads,
        ),
        compiler_params=pltpu.CompilerParams(vmem_limit_bytes=32 * 1024 * 1024),
        name="attend",
    )(starts, limits, query, kv, jnp.tile(low, many // rows)[:, None], jnp.tile(high, many // rows)[:, None])


def project_kernel(turns, place, ours_ref, beside_ref, ours_near, beside_near, own_ref, *rest):
    n = (len(rest) - 5) // 2 + 1
    near, far = rest[: n - 1], rest[n - 1 : 2 * n - 2]
    o_ours, o_beside, held, lhs, arrived = rest[2 * n - 2 :]
    count = turns.shape[0]
    first = place[2]

    def fetch(i, d):
        @pl.when(turns[i] == d)
        def _():
            sources = (near[d - 1], far[d - 1]) if d else (own_ref.at[first], own_ref.at[1 - first])
            for kind, source in enumerate(sources):
                pltpu.make_async_copy(source, held.at[kind, i], arrived.at[kind, i]).start()

    for i in range(count):
        for d in range(n):
            fetch(i, d)

    rows = ours_ref.shape[0]
    for base, a_ref, near_ref in ((0, ours_ref, ours_near), (rows, beside_ref, beside_near)):
        a = a_ref[...]
        mine = near_ref[...] != 0
        zero = jnp.zeros_like(a)
        lhs[0, base : base + rows] = jnp.where(mine, a, zero)
        lhs[1, base : base + rows] = jnp.where(mine, zero, a)
    contract = (((1,), (1,)), ((), ()))
    for i in range(count):
        value = None
        for kind in range(2):
            pltpu.make_async_copy(own_ref.at[0], held.at[kind, i], arrived.at[kind, i]).wait()
            term = lax.dot_general(
                lhs[kind], held[kind, i], contract, preferred_element_type=jnp.float32
            )
            value = term if value is None else value + term
        value = value.astype(jnp.bfloat16)
        o_ours[i] = value[:rows]
        o_beside[i] = value[rows:]


def project(ours, beside, ours_near, beside_near, weights, turns, place):
    rows, depth = ours.shape
    count = turns.shape[0]
    width = weights[0].shape[1]
    shape = jax.ShapeDtypeStruct((count, rows, width), jnp.bfloat16)
    return pl.pallas_call(
        project_kernel,
        out_shape=(shape, shape),
        in_specs=[SMEM, SMEM] + [VMEM] * 4 + [HBM] * len(weights),
        out_specs=(VMEM, VMEM),
        scratch_shapes=[
            pltpu.VMEM((2, count, width, depth), jnp.bfloat16),
            pltpu.VMEM((2, 2 * rows, depth), jnp.bfloat16),
            pltpu.SemaphoreType.DMA((2, count)),
        ],
        cost_estimate=pl.CostEstimate(
            flops=8 * count * rows * depth * width,
            bytes_accessed=4 * count * depth * width + 4 * count * rows * width,
            transcendentals=0,
        ),
        compiler_params=pltpu.CompilerParams(vmem_limit_bytes=32 * 1024 * 1024),
        name="project",
    )(turns, place, ours, beside, ours_near[:, None], beside_near[:, None], *weights)


def body(tokens, norm_gain, w_query, w_key, w_value, w_out, modality, doc_ids):
    length, _ = tokens.shape
    n = lax.axis_size("seq")
    subs = lax.axis_size("sub")
    heads_over = lax.axis_size("head")
    z, s = lax.axis_index("seq"), lax.axis_index("sub")
    x, y = lax.axis_index("head"), lax.axis_index("grp")
    place = jnp.stack([z, x, y, s]).astype(jnp.int32)

    kv_local = max(KV_HEADS // heads_over, 1)
    kv_first = x * KV_HEADS // heads_over
    w_out = jnp.swapaxes(w_out, 1, 2)

    def part_of(array, place, core):
        return lax.dynamic_slice_in_dim(array, (place * subs + core) * length, length)

    mine = lax.dynamic_index_in_dim(w_out, y, 0, keepdims=False)
    near, far = gather_weights(mine)
    weights = [w_out] + near + far

    own_mod = part_of(modality, z, s)
    share_rows = heads_over == 2
    rows = length // 2 if share_rows else length
    sends = norm_columns(tokens, norm_gain, own_mod, place, n, rows)
    blocks = {0: (sends[0],)}
    for d in range(n - 1, 0, -1):
        blocks[d] = (cross(sends[d], "seq", d),)

    w_query, w_key, w_value = after((w_query, w_key, w_value), sends[0])

    key_cols = lax.dynamic_slice_in_dim(w_key, kv_first * HEAD_DIM, kv_local * HEAD_DIM, 2)
    value_cols = lax.dynamic_slice_in_dim(w_value, kv_first * HEAD_DIM, kv_local * HEAD_DIM, 2)
    row_weights = []
    for weight in (key_cols, value_cols, w_query):
        row_weights += [weight, swap(weight, "sub")]
    modality, doc_ids = after((modality, doc_ids), sends[0])
    own_doc = part_of(doc_ids, z, s)
    own_pos = (z * subs + s) * length + jnp.arange(length, dtype=jnp.int32)
    low, high = spans(modality, doc_ids, part_of(modality, z, s), own_doc, own_pos)
    blocks[1] = after(blocks[1], low, high)

    if share_rows:
        for d in range(n - 1, 0, -1):
            blocks[d] = (*blocks[d], swap(blocks[d][0], "head"))

    def parts_of(group, narrow):
        mods = [part_of(modality, z ^ d, s) for d in group]
        return partial([blocks[d] for d in group], mods, row_weights, place, narrow)

    if n == 4:
        kv_early, q_early, kv_rounded, q_rounded = parts_of([3, 2], True)
        kv_ends, q_three, q_two = kv_rounded, q_rounded[0], q_rounded[1]
        kv_late, q_late = parts_of([1, 0], False)
        kv_early, q_early = after((kv_early, q_early), kv_late, q_late)
        kv = along_four([kv_late[1], kv_late[0], kv_early[1], kv_early[0]], kv_ends, None)
        query = along_four([q_late[1], q_late[0], q_early[1], q_early[0]], q_three, q_two)
    else:
        kv_parts, q_parts = [], []
        for d in range(n):
            kv_part, q_part = parts_of([d], False)
            kv_parts.append(kv_part[0])
            q_parts.append(q_part[0])
        kv, query = halving(kv_parts), halving(q_parts)

    same = [kv]
    for d in range(1, n):
        same.append(cross(kv, "seq", d))
    beside_0 = swap(kv, "sub")
    others = swap(jnp.stack(same[1:]), "sub")
    kv_all = jnp.concatenate([jnp.stack(same), beside_0[None], others])
    starts = jnp.stack(
        [((z ^ d) * subs + s) * length for d in range(n)]
        + [((z ^ d) * subs + (1 - s)) * length for d in range(n)]
    ).astype(jnp.int32)
    attended = attend(query, kv_all, starts, low, high)

    beside = swap(attended, "sub")
    ours_near = (own_mod == y).astype(jnp.bfloat16)
    beside_near = (part_of(modality, z, 1 - s) == y).astype(jnp.bfloat16)

    def out(columns):
        turns = (columns ^ z).astype(jnp.int32)
        return project(attended, beside, ours_near, beside_near, weights, turns, place)

    def placed(ours, theirs):
        sibling = swap(theirs, "sub")
        pair = jnp.where(s == 0, jnp.stack([ours, sibling], 1), jnp.stack([sibling, ours], 1))
        return jnp.transpose(pair, (2, 0, 1, 3)).reshape(length, -1)

    if heads_over != 2:
        wide = placed(*out(jnp.arange(n)))
        return lax.psum_scatter(wide, "head", scatter_dimension=1, tiled=True)

    half = jnp.arange(n // 2)
    send_ours, send_beside = out((1 - x) * (n // 2) + half)
    got_beside = swap(send_beside, "head")
    got_ours = swap(send_ours, "head")
    keep_ours, keep_beside = out(x * (n // 2) + half)
    return placed(add(keep_ours, got_ours), add(keep_beside, got_beside))


def solution(mesh):
    placed = (
        P(("grp", "seq", "sub"), None),
        P(),
        P(None, ("seq", "sub"), "head"),
        P(None, ("seq", "sub"), None),
        P(None, ("seq", "sub"), None),
        P(None, "head", ("seq", "sub")),
        P("grp"),
        P("grp"),
    )
    return jax.shard_map(
        body,
        mesh=mesh,
        in_specs=placed,
        out_specs=P(("grp", "seq", "sub"), "head"),
        check_vma=False,
    )
```

```python
import functools
import math

import jax
import jax.numpy as jnp
from jax import lax
from jax.experimental import pallas as pl
from jax.experimental.pallas import tpu as pltpu
from jax.sharding import PartitionSpec as P


HEAD_DIM = 128
KV_HEADS = 4
EPS = 1e-06
LOW = -1e30


def swap(x, axis):
    return lax.ppermute(x, axis, [(0, 1), (1, 0)])


def cross(x, axis, bit, among=None):
    size = lax.axis_size(axis)
    return lax.ppermute(x, axis, [(i ^ bit, i) for i in (among or range(size))])


def after(value, *done):
    return lax.optimization_barrier((value, *done))[0]


def add(a, b):
    return (a.astype(jnp.float32) + b.astype(jnp.float32)).astype(jnp.bfloat16)


VMEM = pl.BlockSpec(memory_space=pltpu.VMEM)
SMEM = pl.BlockSpec(memory_space=pltpu.SMEM)
HBM = pl.BlockSpec(memory_space=pltpu.HBM)


def in_hbm(x):
    return pltpu.with_memory_space_constraint(x, pltpu.HBM)


def norm_kernel(place, tokens_ref, gain_ref, mod_ref, own_ref, *rest):
    send_refs, scratch = rest[:-1], rest[-1]
    width = own_ref.shape[1]
    values = tokens_ref[...].astype(jnp.float32)
    factor = lax.rsqrt(jnp.mean(values * values, axis=1, keepdims=True) + EPS)
    gain = jnp.where(mod_ref[...] == 1, gain_ref[1:2, :], gain_ref[0:1, :])
    scratch[...] = (values * factor * gain).astype(jnp.bfloat16)

    def columns(d):
        return pl.ds(pl.multiple_of((place[0] ^ d) * width, width), width)

    own_ref[...] = scratch[:, columns(0)]
    for d, ref in enumerate(send_refs, 1):
        rows = ref.shape[0]
        ref[...] = scratch[pl.ds(pl.multiple_of(place[1] * rows, rows), rows), columns(d)]


def norm_columns(tokens, norm_gain, mod, place, n, rows):
    length, depth = tokens.shape
    width = depth // n
    if width % 128:
        values32 = tokens.astype(jnp.float32)
        factor = lax.rsqrt(jnp.mean(values32 * values32, axis=1, keepdims=True) + EPS)
        gain = jnp.where((mod == 1)[:, None], norm_gain[1][None, :], norm_gain[0][None, :])
        normed = (values32 * factor * gain).astype(jnp.bfloat16)
        first = [0] + [place[1] * rows] * (n - 1)
        count = [length] + [rows] * (n - 1)
        return [
            lax.dynamic_slice(normed, (first[d], (place[0] ^ d) * width), (count[d], width))
            for d in range(n)
        ]
    shapes = [jax.ShapeDtypeStruct((length, width), jnp.bfloat16)]
    shapes += [jax.ShapeDtypeStruct((rows, width), jnp.bfloat16)] * (n - 1)
    return pl.pallas_call(
        norm_kernel,
        out_shape=shapes,
        in_specs=[SMEM, VMEM, VMEM, VMEM],
        out_specs=[VMEM] * n,
        scratch_shapes=[pltpu.VMEM((length, depth), jnp.bfloat16)],
        cost_estimate=pl.CostEstimate(
            flops=6 * length * depth, bytes_accessed=4 * length * depth, transcendentals=length
        ),
        compiler_params=pltpu.CompilerParams(vmem_limit_bytes=32 * 1024 * 1024),
        name="norm",
    )(place, tokens, norm_gain, mod[:, None])


def partial_kernel(counts, narrow, place, mod_ref, *rest):
    total = sum(counts)
    sources, refs, outs = rest[:6], rest[6 : 6 + total], rest[6 + total : -4]
    both, held_kv, held_q, arrived = rest[-4:]
    kv_half = held_kv.shape[2] // 2
    depth = held_kv.shape[1] // 2
    copies = []
    for i, source in enumerate(sources):
        core = place[3] if i % 2 == 0 else 1 - place[3]
        at = pl.ds(pl.multiple_of(core * depth, depth), depth)
        target = (
            held_kv.at[:, at, 0:kv_half],
            held_kv.at[:, at, kv_half : 2 * kv_half],
            held_q.at[:, at],
        )[i // 2]
        copies.append(pltpu.make_async_copy(source, target, arrived.at[i]))
        copies[-1].start()
    length = both.shape[0] // len(counts)
    at = 0
    for number, count in enumerate(counts):
        base = number * length
        if count == 1:
            both[base : base + length] = refs[at][...]
        else:
            half = length // 2
            both[pl.ds(pl.multiple_of(base + place[1] * half, half), half)] = refs[at][...]
            both[pl.ds(pl.multiple_of(base + (1 - place[1]) * half, half), half)] = refs[at + 1][...]
        at += count
    block = both[...]
    generate = mod_ref[...] == 1
    zero = jnp.zeros_like(block)
    first, second = jnp.where(generate, zero, block), jnp.where(generate, block, zero)
    for i, held in enumerate((held_kv, held_q)):
        for copy in (copies[:4], copies[4:])[i]:
            copy.wait()
        value = jnp.dot(first, held[0], preferred_element_type=jnp.float32) + jnp.dot(
            second, held[1], preferred_element_type=jnp.float32
        )
        outs[i][...] = value
        if narrow:
            outs[2 + i][...] = value.astype(jnp.bfloat16)


def partial(blocks, mods, weights, place, narrow):
    counts = tuple(len(block) for block in blocks)
    arrays = [array for block in blocks for array in block]
    length = mods[0].shape[0]
    rows, width = length * len(blocks), arrays[0].shape[1]
    kv_cols, q_cols = 2 * weights[0].shape[2], weights[4].shape[2]
    shapes = [
        jax.ShapeDtypeStruct((rows, cols), dtype)
        for dtype in (jnp.float32, jnp.bfloat16)[: 1 + narrow]
        for cols in (kv_cols, q_cols)
    ]
    values = pl.pallas_call(
        functools.partial(partial_kernel, counts, narrow),
        out_shape=shapes,
        in_specs=[SMEM, VMEM] + [HBM] * len(weights) + [VMEM] * len(arrays),
        out_specs=[VMEM] * len(shapes),
        scratch_shapes=[
            pltpu.VMEM((rows, width), jnp.bfloat16),
            pltpu.VMEM((2, width, kv_cols), jnp.bfloat16),
            pltpu.VMEM((2, width, q_cols), jnp.bfloat16),
            pltpu.SemaphoreType.DMA((len(weights),)),
        ],
        cost_estimate=pl.CostEstimate(
            flops=4 * rows * width * (kv_cols + q_cols),
            bytes_accessed=4 * (width + rows) * (kv_cols + q_cols),
            transcendentals=0,
        ),
        compiler_params=pltpu.CompilerParams(vmem_limit_bytes=40 * 1024 * 1024),
        name="partial",
    )(place, jnp.concatenate(mods)[:, None], *[in_hbm(w) for w in weights], *arrays)
    return [value.reshape(len(blocks), length, -1) for value in values]


def halving(parts):
    n = len(parts)
    sums = dict(enumerate(parts))
    for bit in [1 << i for i in range(n.bit_length() - 1)]:
        for d in [d for d in range(n) if d in sums and d & bit]:
            sums[d ^ bit] = sums[d ^ bit] + cross(sums.pop(d).astype(jnp.bfloat16), "seq", bit)
    return sums[0].astype(jnp.bfloat16)


def along_four(parts, three, two):
    wide = [p.astype(jnp.float32) for p in parts]

    def hop(value, bit, among):
        return cross(value, "seq", bit, among)

    def plus(a, b):
        return (a + b.astype(jnp.float32)).astype(jnp.bfloat16)

    if two is None:
        got = hop(three, 1, (1, 2))
        got = hop(plus(jnp.stack([wide[2], wide[3]]), got), 3, (1, 2))
        across, own = got[0], got[1]
    else:
        far = hop(three, 1, (1, 2))
        close = hop(two, 1, (1, 2))
        send = plus(wide[2], far)
        across = hop(send, 3, (1, 2))
        own = hop(plus(wide[3], after(close, send)), 3, (1, 2))
    last = hop(plus(wide[1], across), 1, None)
    return (wide[0] + last.astype(jnp.float32) + own.astype(jnp.float32)).astype(jnp.bfloat16)


def gather_weights(mine):
    n = lax.axis_size("seq")
    if n == 4:
        z = lax.axis_index("seq")
        inner = (z == 1) | (z == 2)
        one = cross(mine, "seq", 1)
        middle = cross(mine, "seq", 3, (1, 2))
        middle_two = cross(one, "seq", 3, (1, 2))
        outer_two = cross(middle, "seq", 1, (0, 3))
        outer_three = cross(middle_two, "seq", 1, (0, 3))
        near = [mine, one, jnp.where(inner, middle_two, outer_two), jnp.where(inner, middle, outer_three)]
    else:
        near = [mine]
        for bit in reversed([1 << i for i in range(n.bit_length() - 1)]):
            got = cross(jnp.stack(near), "seq", bit)
            near = near + [got[i] for i in range(len(near))]
        order = [0]
        for bit in reversed([1 << i for i in range(n.bit_length() - 1)]):
            order = order + [d ^ bit for d in order]
        near = [near[order.index(d)] for d in range(n)]
    far = []
    for d in range(1, n):
        far.append(swap(near[d], "grp"))
    return near[1:], far


def spans(modality, doc_ids, own_mod, own_doc, own_pos):
    changed = (modality[1:] != modality[:-1]) | (doc_ids[1:] != doc_ids[:-1])
    begins = jnp.concatenate([jnp.ones((1,), jnp.int32), changed.astype(jnp.int32)])
    blocks = jnp.cumsum(begins)
    own_block = lax.dynamic_slice_in_dim(blocks, own_pos[0], own_pos.shape[0])
    low = jnp.sum((doc_ids[None, :] < own_doc[:, None]).astype(jnp.int32), axis=1)
    end = jnp.sum((blocks[None, :] <= own_block[:, None]).astype(jnp.int32), axis=1) - 1
    return low, jnp.where(own_mod == 1, end, own_pos)


def attention_kernel(starts, limits, q_ref, kv_ref, low_ref, high_ref, o_ref, queries, top, total, acc):
    count, size, _ = kv_ref.shape
    rows = q_ref.shape[0]
    kv_local, many = queries.shape[0], queries.shape[1]
    repeat = many // rows
    scale = math.log2(math.e) / math.sqrt(HEAD_DIM)
    top[...] = jnp.full_like(top, LOW / 10)
    total[...] = jnp.zeros_like(total)
    acc[...] = jnp.zeros_like(acc)
    for head in range(kv_local * repeat):
        g, r = head // repeat, head % repeat
        queries[g, r * rows : (r + 1) * rows] = q_ref[:, head * HEAD_DIM : (head + 1) * HEAD_DIM]
    transposed = (((1,), (1,)), ((), ()))

    def visit(number, _):
        start = starts[number]
        last = start + size - 1

        def block(masked):
            for g in range(kv_local):
                keys = kv_ref[number, :, g * HEAD_DIM : (g + 1) * HEAD_DIM]
                values = kv_ref[number, :, (kv_local + g) * HEAD_DIM : (kv_local + g + 1) * HEAD_DIM]
                scores = lax.dot_general(
                    queries[g], keys, transposed, preferred_element_type=jnp.float32
                )
                if masked:
                    key_pos = start + lax.broadcasted_iota(jnp.int32, (many, size), 1)
                    seen = (key_pos >= low_ref[...]) & (key_pos <= high_ref[...])
                    scores = jnp.where(seen, scores, LOW)
                old = top[g]
                new = jnp.maximum(old, jnp.max(scores, axis=1, keepdims=True))
                weights = jnp.exp2((scores - jnp.tile(new, (1, size // 128))) * scale)
                shrink = jnp.exp2((old - new) * scale)
                total[g] = total[g] * shrink + jnp.sum(weights, axis=1, keepdims=True)
                top[g] = new
                acc[g] = acc[g] * shrink + jnp.dot(
                    weights.astype(jnp.bfloat16), values, preferred_element_type=jnp.float32
                )

        inside = (start >= limits[2]) & (last <= limits[3])

        @pl.when(inside)
        def _():
            block(False)

        @pl.when(jnp.logical_not(inside) & (start <= limits[1]) & (last >= limits[0]))
        def _():
            block(True)

        return 0

    lax.fori_loop(0, count, visit, 0)
    for head in range(kv_local * repeat):
        g, at = head // repeat, pl.ds((head % repeat) * rows, rows)
        o_ref[:, head * HEAD_DIM : (head + 1) * HEAD_DIM] = (acc[g, at] / total[g, at]).astype(
            jnp.bfloat16
        )


def attend(query, kv, starts, low, high):
    rows, width = query.shape
    heads = width // HEAD_DIM
    count, size, _ = kv.shape
    kv_local = kv.shape[2] // (2 * HEAD_DIM)
    many = rows * heads // kv_local
    limits = jnp.stack([low[0], high[-1], low[-1], high[0]])
    return pl.pallas_call(
        attention_kernel,
        out_shape=jax.ShapeDtypeStruct((rows, width), jnp.bfloat16),
        in_specs=[SMEM, SMEM, VMEM, VMEM, VMEM, VMEM],
        out_specs=VMEM,
        scratch_shapes=[
            pltpu.VMEM((kv_local, many, HEAD_DIM), jnp.bfloat16),
            pltpu.VMEM((kv_local, many, HEAD_DIM), jnp.float32),
            pltpu.VMEM((kv_local, many, HEAD_DIM), jnp.float32),
            pltpu.VMEM((kv_local, many, HEAD_DIM), jnp.float32),
        ],
        cost_estimate=pl.CostEstimate(
            flops=4 * rows * count * size * width,
            bytes_accessed=2 * (2 * rows * width + kv.size),
            transcendentals=rows * count * size * heads,
        ),
        compiler_params=pltpu.CompilerParams(vmem_limit_bytes=32 * 1024 * 1024),
        name="attend",
    )(starts, limits, query, kv, jnp.tile(low, many // rows)[:, None], jnp.tile(high, many // rows)[:, None])


def project_kernel(turns, place, ours_ref, beside_ref, ours_near, beside_near, own_ref, *rest):
    n = (len(rest) - 5) // 2 + 1
    near, far = rest[: n - 1], rest[n - 1 : 2 * n - 2]
    o_ours, o_beside, held, lhs, arrived = rest[2 * n - 2 :]
    count = turns.shape[0]
    first = place[2]

    def fetch(i, d):
        @pl.when(turns[i] == d)
        def _():
            sources = (near[d - 1], far[d - 1]) if d else (own_ref.at[first], own_ref.at[1 - first])
            for kind, source in enumerate(sources):
                pltpu.make_async_copy(source, held.at[kind, i], arrived.at[kind, i]).start()

    for i in range(count):
        for d in range(n):
            fetch(i, d)

    rows = ours_ref.shape[0]
    for base, a_ref, near_ref in ((0, ours_ref, ours_near), (rows, beside_ref, beside_near)):
        a = a_ref[...]
        mine = near_ref[...] != 0
        zero = jnp.zeros_like(a)
        lhs[0, base : base + rows] = jnp.where(mine, a, zero)
        lhs[1, base : base + rows] = jnp.where(mine, zero, a)
    contract = (((1,), (1,)), ((), ()))
    for i in range(count):
        value = None
        for kind in range(2):
            pltpu.make_async_copy(own_ref.at[0], held.at[kind, i], arrived.at[kind, i]).wait()
            term = lax.dot_general(
                lhs[kind], held[kind, i], contract, preferred_element_type=jnp.float32
            )
            value = term if value is None else value + term
        value = value.astype(jnp.bfloat16)
        o_ours[i] = value[:rows]
        o_beside[i] = value[rows:]


def project(ours, beside, ours_near, beside_near, weights, turns, place):
    rows, depth = ours.shape
    count = turns.shape[0]
    width = weights[0].shape[1]
    shape = jax.ShapeDtypeStruct((count, rows, width), jnp.bfloat16)
    return pl.pallas_call(
        project_kernel,
        out_shape=(shape, shape),
        in_specs=[SMEM, SMEM] + [VMEM] * 4 + [HBM] * len(weights),
        out_specs=(VMEM, VMEM),
        scratch_shapes=[
            pltpu.VMEM((2, count, width, depth), jnp.bfloat16),
            pltpu.VMEM((2, 2 * rows, depth), jnp.bfloat16),
            pltpu.SemaphoreType.DMA((2, count)),
        ],
        cost_estimate=pl.CostEstimate(
            flops=8 * count * rows * depth * width,
            bytes_accessed=4 * count * depth * width + 4 * count * rows * width,
            transcendentals=0,
        ),
        compiler_params=pltpu.CompilerParams(vmem_limit_bytes=32 * 1024 * 1024),
        name="project",
    )(turns, place, ours, beside, ours_near[:, None], beside_near[:, None], *weights)


def body(tokens, norm_gain, w_query, w_key, w_value, w_out, modality, doc_ids):
    length, _ = tokens.shape
    n = lax.axis_size("seq")
    subs = lax.axis_size("sub")
    heads_over = lax.axis_size("head")
    z, s = lax.axis_index("seq"), lax.axis_index("sub")
    x, y = lax.axis_index("head"), lax.axis_index("grp")
    place = jnp.stack([z, x, y, s]).astype(jnp.int32)

    kv_local = max(KV_HEADS // heads_over, 1)
    kv_first = x * KV_HEADS // heads_over
    w_out = jnp.swapaxes(w_out, 1, 2)

    def part_of(array, place, core):
        return lax.dynamic_slice_in_dim(array, (place * subs + core) * length, length)

    mine = lax.dynamic_index_in_dim(w_out, y, 0, keepdims=False)
    near, far = gather_weights(mine)
    weights = [w_out] + near + far

    own_mod = part_of(modality, z, s)
    share_rows = heads_over == 2
    rows = length // 2 if share_rows else length
    sends = norm_columns(tokens, norm_gain, own_mod, place, n, rows)
    blocks = {0: (sends[0],)}
    for d in range(n - 1, 0, -1):
        blocks[d] = (cross(sends[d], "seq", d),)

    w_query, w_key, w_value = after((w_query, w_key, w_value), sends[0])

    key_cols = lax.dynamic_slice_in_dim(w_key, kv_first * HEAD_DIM, kv_local * HEAD_DIM, 2)
    value_cols = lax.dynamic_slice_in_dim(w_value, kv_first * HEAD_DIM, kv_local * HEAD_DIM, 2)
    row_weights = []
    for weight in (key_cols, value_cols, w_query):
        row_weights += [weight, swap(weight, "sub")]
    modality, doc_ids = after((modality, doc_ids), sends[0])
    own_doc = part_of(doc_ids, z, s)
    own_pos = (z * subs + s) * length + jnp.arange(length, dtype=jnp.int32)
    low, high = spans(modality, doc_ids, part_of(modality, z, s), own_doc, own_pos)
    blocks[1] = after(blocks[1], low, high)

    if share_rows:
        for d in range(n - 1, 0, -1):
            blocks[d] = (*blocks[d], swap(blocks[d][0], "head"))

    def parts_of(group, narrow):
        mods = [part_of(modality, z ^ d, s) for d in group]
        return partial([blocks[d] for d in group], mods, row_weights, place, narrow)

    if n == 4:
        kv_early, q_early, kv_rounded, q_rounded = parts_of([3, 2], True)
        kv_ends, q_three, q_two = kv_rounded, q_rounded[0], q_rounded[1]
        kv_late, q_late = parts_of([1, 0], False)
        kv_early, q_early = after((kv_early, q_early), kv_late, q_late)
        kv = along_four([kv_late[1], kv_late[0], kv_early[1], kv_early[0]], kv_ends, None)
        query = along_four([q_late[1], q_late[0], q_early[1], q_early[0]], q_three, q_two)
    else:
        kv_parts, q_parts = [], []
        for d in range(n):
            kv_part, q_part = parts_of([d], False)
            kv_parts.append(kv_part[0])
            q_parts.append(q_part[0])
        kv, query = halving(kv_parts), halving(q_parts)

    same = [kv]
    for d in range(1, n):
        same.append(cross(kv, "seq", d))
    beside_0 = swap(kv, "sub")
    held = jnp.stack(same[1:])
    others = swap(held, "sub")
    kv_all = jnp.concatenate([jnp.stack(same), beside_0[None], others])
    starts = jnp.stack(
        [((z ^ d) * subs + s) * length for d in range(n)]
        + [((z ^ d) * subs + (1 - s)) * length for d in range(n)]
    ).astype(jnp.int32)
    attended = attend(query, kv_all, starts, low, high)

    beside = swap(attended, "sub")
    ours_near = (own_mod == y).astype(jnp.bfloat16)
    beside_near = (part_of(modality, z, 1 - s) == y).astype(jnp.bfloat16)

    def out(columns):
        turns = (columns ^ z).astype(jnp.int32)
        return project(attended, beside, ours_near, beside_near, weights, turns, place)

    def placed(ours, theirs):
        sibling = swap(theirs, "sub")
        pair = jnp.where(s == 0, jnp.stack([ours, sibling], 1), jnp.stack([sibling, ours], 1))
        return jnp.transpose(pair, (2, 0, 1, 3)).reshape(length, -1)

    if heads_over != 2:
        wide = placed(*out(jnp.arange(n)))
        return lax.psum_scatter(wide, "head", scatter_dimension=1, tiled=True)

    half = n // 2
    ours, theirs = [], []
    sent = [out((1 - x) * half + jnp.arange(i, i + 1)) for i in range(half)]
    for send_ours, send_beside in sent:
        theirs.append(swap(send_beside, "head"))
        ours.append(swap(send_ours, "head"))
    keep_ours, keep_beside = out(x * half + jnp.arange(half))
    return placed(
        add(keep_ours, jnp.concatenate(ours)), add(keep_beside, jnp.concatenate(theirs))
    )


def solution(mesh):
    placed = (
        P(("grp", "seq", "sub"), None),
        P(),
        P(None, ("seq", "sub"), "head"),
        P(None, ("seq", "sub"), None),
        P(None, ("seq", "sub"), None),
        P(None, "head", ("seq", "sub")),
        P("grp"),
        P("grp"),
    )
    return jax.shard_map(
        body,
        mesh=mesh,
        in_specs=placed,
        out_specs=P(("grp", "seq", "sub"), "head"),
        check_vma=False,
    )
```

```python
import functools
import math

import jax
import jax.numpy as jnp
from jax import lax
from jax.experimental import pallas as pl
from jax.experimental.pallas import tpu as pltpu
from jax.sharding import PartitionSpec as P


HEAD_DIM = 128
KV_HEADS = 4
RUN = 64
EPS = 1e-06
LOW = -1e30


def swap(x, axis):
    return lax.ppermute(x, axis, [(0, 1), (1, 0)])


def cross(x, axis, bit, among=None):
    size = lax.axis_size(axis)
    return lax.ppermute(x, axis, [(i ^ bit, i) for i in (among or range(size))])


def after(value, *done):
    return lax.optimization_barrier((value, *done))[0]


def add(a, b):
    return (a.astype(jnp.float32) + b.astype(jnp.float32)).astype(jnp.bfloat16)


VMEM = pl.BlockSpec(memory_space=pltpu.VMEM)
SMEM = pl.BlockSpec(memory_space=pltpu.SMEM)
HBM = pl.BlockSpec(memory_space=pltpu.HBM)


def in_hbm(x):
    return pltpu.with_memory_space_constraint(x, pltpu.HBM)


def norm_kernel(place, modality, tokens_ref, gain_ref, own_ref, *rest):
    send_refs, scratch = rest[:-1], rest[-1]
    width = own_ref.shape[1]
    for at in range(0, tokens_ref.shape[0], RUN):
        values = tokens_ref[at : at + RUN].astype(jnp.float32)
        factor = lax.rsqrt(jnp.mean(values * values, axis=1, keepdims=True) + EPS)
        gain = jnp.where(modality[place[4] + at] == 1, gain_ref[1:2, :], gain_ref[0:1, :])
        scratch[at : at + RUN] = (values * factor * gain).astype(jnp.bfloat16)

    def columns(d):
        return pl.ds(pl.multiple_of((place[0] ^ d) * width, width), width)

    own_ref[...] = scratch[:, columns(0)]
    for d, ref in enumerate(send_refs, 1):
        rows = ref.shape[0]
        ref[...] = scratch[pl.ds(pl.multiple_of(place[1] * rows, rows), rows), columns(d)]


def norm_columns(tokens, norm_gain, modality, mod, place, n, rows):
    length, depth = tokens.shape
    width = depth // n
    if width % 128:
        values32 = tokens.astype(jnp.float32)
        factor = lax.rsqrt(jnp.mean(values32 * values32, axis=1, keepdims=True) + EPS)
        gain = jnp.where((mod == 1)[:, None], norm_gain[1][None, :], norm_gain[0][None, :])
        normed = (values32 * factor * gain).astype(jnp.bfloat16)
        first = [0] + [place[1] * rows] * (n - 1)
        count = [length] + [rows] * (n - 1)
        return [
            lax.dynamic_slice(normed, (first[d], (place[0] ^ d) * width), (count[d], width))
            for d in range(n)
        ]
    shapes = [jax.ShapeDtypeStruct((length, width), jnp.bfloat16)]
    shapes += [jax.ShapeDtypeStruct((rows, width), jnp.bfloat16)] * (n - 1)
    return pl.pallas_call(
        norm_kernel,
        out_shape=shapes,
        in_specs=[SMEM, SMEM, VMEM, VMEM],
        out_specs=[VMEM] * n,
        scratch_shapes=[pltpu.VMEM((length, depth), jnp.bfloat16)],
        cost_estimate=pl.CostEstimate(
            flops=6 * length * depth, bytes_accessed=4 * length * depth, transcendentals=length
        ),
        compiler_params=pltpu.CompilerParams(vmem_limit_bytes=12 * 1024 * 1024),
        name="norm",
    )(place, modality, tokens, norm_gain)


def partial_kernel(counts, narrow, place, modality, begins, *rest):
    total = sum(counts)
    sources, refs, outs = rest[:6], rest[6 : 6 + total], rest[6 + total : -8]
    both, other, held_kv, held_q, arrived = rest[-8:-3]
    wide_kv, wide_q, left = rest[-3:]
    kv_half = held_kv.shape[2] // 2
    depth = held_kv.shape[1] // 2
    copies = []
    for i in (4, 5, 0, 1, 2, 3):
        source = sources[i]
        core = place[3] if i % 2 == 0 else 1 - place[3]
        at = pl.ds(pl.multiple_of(core * depth, depth), depth)
        target = (
            held_kv.at[:, at, 0:kv_half],
            held_kv.at[:, at, kv_half : 2 * kv_half],
            held_q.at[:, at],
        )[i // 2]
        copies.append(pltpu.make_async_copy(source, target, arrived.at[i]))
        copies[-1].start()
    stores = []
    length = both.shape[0] // len(counts)
    at = 0
    for number, count in enumerate(counts):
        base = number * length
        if count == 1:
            both[base : base + length] = refs[at][...]
        else:
            half = length // 2
            both[pl.ds(pl.multiple_of(base + place[1] * half, half), half)] = refs[at][...]
            both[pl.ds(pl.multiple_of(base + (1 - place[1]) * half, half), half)] = refs[at + 1][...]
        at += count
    for number in range(len(counts)):
        for step in range(0, length, RUN):
            at = pl.ds(number * length + step, RUN)
            generate = modality[begins[number] + step] == 1
            block = both[at]
            zero = jnp.zeros_like(block)
            both[at] = jnp.where(generate, zero, block)
            other[at] = jnp.where(generate, block, zero)
    first, second = both[...], other[...]
    for i, held, wide in ((1, held_q, wide_q), (0, held_kv, wide_kv)):
        for copy in (copies[2:], copies[:2])[i]:
            copy.wait()
        value = jnp.dot(first, held[0], preferred_element_type=jnp.float32) + jnp.dot(
            second, held[1], preferred_element_type=jnp.float32
        )
        wide[...] = value
        stores.append(pltpu.make_async_copy(wide, outs[i], left.at[i]))
        stores[-1].start()
        if narrow and i == 0:
            outs[2][...] = value.astype(jnp.bfloat16)
        elif narrow:
            for number in range(len(counts)):
                part = value[number * length : (number + 1) * length]
                outs[3 + number][...] = part.astype(jnp.bfloat16)
    for store in stores:
        store.wait()


def partial(blocks, begins, length, modality, weights, place, narrow):
    counts = tuple(len(block) for block in blocks)
    arrays = [array for block in blocks for array in block]
    rows, width = length * len(blocks), arrays[0].shape[1]
    kv_cols, q_cols = 2 * weights[0].shape[2], weights[4].shape[2]
    shapes = [pltpu.HBM((rows, cols), jnp.float32) for cols in (kv_cols, q_cols)]
    if narrow:
        shapes.append(jax.ShapeDtypeStruct((rows, kv_cols), jnp.bfloat16))
        shapes += [jax.ShapeDtypeStruct((length, q_cols), jnp.bfloat16)] * len(blocks)
    values = pl.pallas_call(
        functools.partial(partial_kernel, counts, narrow),
        out_shape=shapes,
        in_specs=[SMEM] * 3 + [HBM] * len(weights) + [VMEM] * len(arrays),
        out_specs=[HBM] * 2 + [VMEM] * (len(shapes) - 2),
        scratch_shapes=[
            pltpu.VMEM((rows, width), jnp.bfloat16),
            pltpu.VMEM((rows, width), jnp.bfloat16),
            pltpu.VMEM((2, width, kv_cols), jnp.bfloat16),
            pltpu.VMEM((2, width, q_cols), jnp.bfloat16),
            pltpu.SemaphoreType.DMA((len(weights),)),
            pltpu.VMEM((rows, kv_cols), jnp.float32),
            pltpu.VMEM((rows, q_cols), jnp.float32),
            pltpu.SemaphoreType.DMA((2,)),
        ],
        cost_estimate=pl.CostEstimate(
            flops=4 * rows * width * (kv_cols + q_cols),
            bytes_accessed=4 * (width + rows) * (kv_cols + q_cols),
            transcendentals=0,
        ),
        compiler_params=pltpu.CompilerParams(vmem_limit_bytes=24 * 1024 * 1024),
        name="partial",
    )(place, modality, begins, *[in_hbm(w) for w in weights], *arrays)
    return [value.reshape(len(blocks), length, -1) for value in values[:3]] + list(values[3:])


def halving(parts):
    n = len(parts)
    sums = dict(enumerate(parts))
    for bit in [1 << i for i in range(n.bit_length() - 1)]:
        for d in [d for d in range(n) if d in sums and d & bit]:
            sums[d ^ bit] = sums[d ^ bit] + cross(sums.pop(d).astype(jnp.bfloat16), "seq", bit)
    return sums[0].astype(jnp.bfloat16)


def along_four(parts, three, two):
    wide = [p.astype(jnp.float32) for p in parts]

    def hop(value, bit, among):
        return cross(value, "seq", bit, among)

    def plus(a, b):
        return (a + b.astype(jnp.float32)).astype(jnp.bfloat16)

    if two is None:
        got = hop(three, 1, (1, 2))
        got = hop(plus(jnp.stack([wide[2], wide[3]]), got), 3, (1, 2))
        across, own = got[0], got[1]
    else:
        far = hop(three, 1, (1, 2))
        close = hop(two, 1, (1, 2))
        send = plus(wide[2], far)
        across = hop(send, 3, (1, 2))
        own = hop(plus(wide[3], after(close, send)), 3, (1, 2))
    last = hop(plus(wide[1], across), 1, None)
    return (wide[0] + last.astype(jnp.float32) + own.astype(jnp.float32)).astype(jnp.bfloat16)


def gather_weights(mine):
    n = lax.axis_size("seq")
    if n == 4:
        z = lax.axis_index("seq")
        inner = (z == 1) | (z == 2)
        one = cross(mine, "seq", 1)
        middle = cross(mine, "seq", 3, (1, 2))
        middle_two = cross(one, "seq", 3, (1, 2))
        outer_two = cross(middle, "seq", 1, (0, 3))
        outer_three = cross(middle_two, "seq", 1, (0, 3))
        near = [mine, one, jnp.where(inner, middle_two, outer_two), jnp.where(inner, middle, outer_three)]
    else:
        near = [mine]
        for bit in reversed([1 << i for i in range(n.bit_length() - 1)]):
            got = cross(jnp.stack(near), "seq", bit)
            near = near + [got[i] for i in range(len(near))]
        order = [0]
        for bit in reversed([1 << i for i in range(n.bit_length() - 1)]):
            order = order + [d ^ bit for d in order]
        near = [near[order.index(d)] for d in range(n)]
    far = []
    for d in range(1, n):
        far.append(swap(near[d], "grp"))
    return near[1:], far


def spans(modality, doc_ids, own_mod, own_doc, own_pos):
    changed = (modality[1:] != modality[:-1]) | (doc_ids[1:] != doc_ids[:-1])
    begins = jnp.concatenate([jnp.ones((1,), jnp.int32), changed.astype(jnp.int32)])
    blocks = jnp.cumsum(begins)
    own_block = lax.dynamic_slice_in_dim(blocks, own_pos[0], own_pos.shape[0])
    low = jnp.sum((doc_ids[None, :] < own_doc[:, None]).astype(jnp.int32), axis=1)
    end = jnp.sum((blocks[None, :] <= own_block[:, None]).astype(jnp.int32), axis=1) - 1
    return low, jnp.where(own_mod == 1, end, own_pos)


def attention_kernel(starts, limits, q_ref, kv_ref, low_ref, high_ref, o_ref, queries, top, total, acc):
    count, size, _ = kv_ref.shape
    rows = q_ref.shape[0]
    kv_local, many = queries.shape[0], queries.shape[1]
    repeat = many // rows
    scale = math.log2(math.e) / math.sqrt(HEAD_DIM)
    top[...] = jnp.full_like(top, LOW / 10)
    total[...] = jnp.zeros_like(total)
    acc[...] = jnp.zeros_like(acc)
    for head in range(kv_local * repeat):
        g, r = head // repeat, head % repeat
        queries[g, r * rows : (r + 1) * rows] = q_ref[:, head * HEAD_DIM : (head + 1) * HEAD_DIM]
    transposed = (((1,), (1,)), ((), ()))

    def visit(number, _):
        start = starts[number]
        last = start + size - 1

        def block(masked):
            for g in range(kv_local):
                keys = kv_ref[number, :, g * HEAD_DIM : (g + 1) * HEAD_DIM]
                values = kv_ref[number, :, (kv_local + g) * HEAD_DIM : (kv_local + g + 1) * HEAD_DIM]
                scores = lax.dot_general(
                    queries[g], keys, transposed, preferred_element_type=jnp.float32
                )
                if masked:
                    key_pos = start + lax.broadcasted_iota(jnp.int32, (many, size), 1)
                    seen = (key_pos >= low_ref[...]) & (key_pos <= high_ref[...])
                    scores = jnp.where(seen, scores, LOW)
                old = top[g]
                new = jnp.maximum(old, jnp.max(scores, axis=1, keepdims=True))
                weights = jnp.exp2((scores - jnp.tile(new, (1, size // 128))) * scale)
                shrink = jnp.exp2((old - new) * scale)
                total[g] = total[g] * shrink + jnp.sum(weights, axis=1, keepdims=True)
                top[g] = new
                acc[g] = acc[g] * shrink + jnp.dot(
                    weights.astype(jnp.bfloat16), values, preferred_element_type=jnp.float32
                )

        inside = (start >= limits[2]) & (last <= limits[3])

        @pl.when(inside)
        def _():
            block(False)

        @pl.when(jnp.logical_not(inside) & (start <= limits[1]) & (last >= limits[0]))
        def _():
            block(True)

        return 0

    lax.fori_loop(0, count, visit, 0)
    for head in range(kv_local * repeat):
        g, at = head // repeat, pl.ds((head % repeat) * rows, rows)
        o_ref[:, head * HEAD_DIM : (head + 1) * HEAD_DIM] = (acc[g, at] / total[g, at]).astype(
            jnp.bfloat16
        )


def attend(query, kv, starts, low, high, low_column, high_column):
    rows, width = query.shape
    heads = width // HEAD_DIM
    count, size, _ = kv.shape
    kv_local = kv.shape[2] // (2 * HEAD_DIM)
    many = rows * heads // kv_local
    limits = jnp.stack([low[0], high[-1], low[-1], high[0]])
    return pl.pallas_call(
        attention_kernel,
        out_shape=jax.ShapeDtypeStruct((rows, width), jnp.bfloat16),
        in_specs=[SMEM, SMEM, VMEM, VMEM, VMEM, VMEM],
        out_specs=VMEM,
        scratch_shapes=[
            pltpu.VMEM((kv_local, many, HEAD_DIM), jnp.bfloat16),
            pltpu.VMEM((kv_local, many, HEAD_DIM), jnp.float32),
            pltpu.VMEM((kv_local, many, HEAD_DIM), jnp.float32),
            pltpu.VMEM((kv_local, many, HEAD_DIM), jnp.float32),
        ],
        cost_estimate=pl.CostEstimate(
            flops=4 * rows * count * size * width,
            bytes_accessed=2 * (2 * rows * width + kv.size),
            transcendentals=rows * count * size * heads,
        ),
        compiler_params=pltpu.CompilerParams(vmem_limit_bytes=20 * 1024 * 1024),
        name="attend",
    )(starts, limits, query, kv, low_column, high_column)


def project_kernel(turns, place, ours_ref, beside_ref, ours_near, beside_near, own_ref, *rest):
    n = (len(rest) - 5) // 2 + 1
    near, far = rest[: n - 1], rest[n - 1 : 2 * n - 2]
    o_ours, o_beside, held, lhs, arrived = rest[2 * n - 2 :]
    count = turns.shape[0]
    first = place[2]

    def fetch(i, d):
        @pl.when(turns[i] == d)
        def _():
            sources = (near[d - 1], far[d - 1]) if d else (own_ref.at[first], own_ref.at[1 - first])
            for kind, source in enumerate(sources):
                pltpu.make_async_copy(source, held.at[kind, i], arrived.at[kind, i]).start()

    for i in range(count):
        for d in range(n):
            fetch(i, d)

    rows = ours_ref.shape[0]
    for base, a_ref, near_ref in ((0, ours_ref, ours_near), (rows, beside_ref, beside_near)):
        a = a_ref[...]
        mine = near_ref[...] != 0
        zero = jnp.zeros_like(a)
        lhs[0, base : base + rows] = jnp.where(mine, a, zero)
        lhs[1, base : base + rows] = jnp.where(mine, zero, a)
    contract = (((1,), (1,)), ((), ()))
    for i in range(count):
        value = None
        for kind in range(2):
            pltpu.make_async_copy(own_ref.at[0], held.at[kind, i], arrived.at[kind, i]).wait()
            term = lax.dot_general(
                lhs[kind], held[kind, i], contract, preferred_element_type=jnp.float32
            )
            value = term if value is None else value + term
        value = value.astype(jnp.bfloat16)
        o_ours[i] = value[:rows]
        o_beside[i] = value[rows:]


def project(ours, beside, ours_near, beside_near, weights, turns, place):
    rows, depth = ours.shape
    count = turns.shape[0]
    width = weights[0].shape[1]
    shape = jax.ShapeDtypeStruct((count, rows, width), jnp.bfloat16)
    return pl.pallas_call(
        project_kernel,
        out_shape=(shape, shape),
        in_specs=[SMEM, SMEM] + [VMEM] * 4 + [HBM] * len(weights),
        out_specs=(VMEM, VMEM),
        scratch_shapes=[
            pltpu.VMEM((2, count, width, depth), jnp.bfloat16),
            pltpu.VMEM((2, 2 * rows, depth), jnp.bfloat16),
            pltpu.SemaphoreType.DMA((2, count)),
        ],
        cost_estimate=pl.CostEstimate(
            flops=8 * count * rows * depth * width,
            bytes_accessed=4 * count * depth * width + 4 * count * rows * width,
            transcendentals=0,
        ),
        compiler_params=pltpu.CompilerParams(vmem_limit_bytes=16 * 1024 * 1024),
        name="project",
    )(turns, place, ours, beside, ours_near[:, None], beside_near[:, None], *weights)


def body(tokens, norm_gain, w_query, w_key, w_value, w_out, modality, doc_ids):
    length, _ = tokens.shape
    n = lax.axis_size("seq")
    subs = lax.axis_size("sub")
    heads_over = lax.axis_size("head")
    z, s = lax.axis_index("seq"), lax.axis_index("sub")
    x, y = lax.axis_index("head"), lax.axis_index("grp")
    place = jnp.stack([z, x, y, s, (z * subs + s) * length]).astype(jnp.int32)

    kv_local = max(KV_HEADS // heads_over, 1)
    kv_first = x * KV_HEADS // heads_over
    w_out = jnp.swapaxes(w_out, 1, 2)

    def part_of(array, place, core):
        return lax.dynamic_slice_in_dim(array, (place * subs + core) * length, length)

    mine = lax.dynamic_index_in_dim(w_out, y, 0, keepdims=False)
    near, far = gather_weights(mine)
    weights = [w_out] + near + far

    own_mod = part_of(modality, z, s)
    share_rows = heads_over == 2
    rows = length // 2 if share_rows else length
    sends = norm_columns(tokens, norm_gain, modality, own_mod, place, n, rows)
    blocks = {0: (sends[0],)}
    for d in range(n - 1, 0, -1):
        blocks[d] = (cross(sends[d], "seq", d),)

    w_query, w_key, w_value = after((w_query, w_key, w_value), sends[0])

    key_cols = lax.dynamic_slice_in_dim(w_key, kv_first * HEAD_DIM, kv_local * HEAD_DIM, 2)
    value_cols = lax.dynamic_slice_in_dim(w_value, kv_first * HEAD_DIM, kv_local * HEAD_DIM, 2)
    row_weights = []
    for weight in (key_cols, value_cols, w_query):
        row_weights += [weight, swap(weight, "sub")]
    modality, doc_ids = after((modality, doc_ids), sends[0])
    own_doc = part_of(doc_ids, z, s)
    own_pos = (z * subs + s) * length + jnp.arange(length, dtype=jnp.int32)
    low, high = spans(modality, doc_ids, part_of(modality, z, s), own_doc, own_pos)
    repeat = w_query.shape[2] // HEAD_DIM // kv_local
    low_column, high_column = jnp.tile(low, repeat)[:, None], jnp.tile(high, repeat)[:, None]

    if share_rows:
        for d in range(n - 1, 0, -1):
            blocks[d] = (*blocks[d], swap(blocks[d][0], "head"))
    blocks[n - 1] = after(blocks[n - 1], low_column, high_column)

    def parts_of(group, narrow):
        begins = jnp.stack([((z ^ d) * subs + s) * length for d in group]).astype(jnp.int32)
        arrays = [blocks[d] for d in group]
        return partial(arrays, begins, length, modality, row_weights, place, narrow)

    if n == 4:
        kv_early, q_early, kv_ends, q_three, q_two = parts_of([3, 2], True)
        kv_late, q_late = parts_of([1, 0], False)
        kv_early, q_early = after((kv_early, q_early), kv_late, q_late)
        kv = along_four([kv_late[1], kv_late[0], kv_early[1], kv_early[0]], kv_ends, None)
        query = along_four([q_late[1], q_late[0], q_early[1], q_early[0]], q_three, q_two)
    else:
        kv_parts, q_parts = [], []
        for d in range(n):
            kv_part, q_part = parts_of([d], False)
            kv_parts.append(kv_part[0])
            q_parts.append(q_part[0])
        kv, query = halving(kv_parts), halving(q_parts)

    same = [kv]
    for d in range(1, n):
        same.append(cross(kv, "seq", d))
    beside_0 = swap(kv, "sub")
    held = jnp.stack(same[1:])
    others = swap(held, "sub")
    kv_all = jnp.concatenate([jnp.stack(same), beside_0[None], others])
    starts = jnp.stack(
        [((z ^ d) * subs + s) * length for d in range(n)]
        + [((z ^ d) * subs + (1 - s)) * length for d in range(n)]
    ).astype(jnp.int32)
    attended = attend(query, kv_all, starts, low, high, low_column, high_column)

    beside = swap(attended, "sub")
    ours_near = (own_mod == y).astype(jnp.bfloat16)
    beside_near = (part_of(modality, z, 1 - s) == y).astype(jnp.bfloat16)

    def out(columns):
        turns = (columns ^ z).astype(jnp.int32)
        return project(attended, beside, ours_near, beside_near, weights, turns, place)

    if heads_over != 2:
        ours, theirs = out(jnp.arange(n))
        sibling = swap(theirs, "sub")
        pair = jnp.where(s == 0, jnp.stack([ours, sibling], 1), jnp.stack([sibling, ours], 1))
        wide = jnp.transpose(pair, (2, 0, 1, 3)).reshape(length, -1)
        return lax.psum_scatter(wide, "head", scatter_dimension=1, tiled=True)

    half = n // 2
    ours, theirs = [], []
    sent = [out((1 - x) * half + jnp.arange(i, i + 1)) for i in range(half)]
    for send_ours, send_beside in sent:
        theirs.append(swap(send_beside, "head"))
        ours.append(swap(send_ours, "head"))
    keep_ours, keep_beside = out(x * half + jnp.arange(half))
    done = add(keep_beside, jnp.concatenate(theirs))
    sibling = swap(done, "sub")
    return finish(place, keep_ours, ours, sibling)


def finish_kernel(place, keep_ref, *rest):
    got_refs, sibling_ref, o_ref = rest[:-2], rest[-2], rest[-1]
    width = keep_ref.shape[2]

    def fill(core):
        for i, got_ref in enumerate(got_refs):
            own = keep_ref[i].astype(jnp.float32) + got_ref[0].astype(jnp.float32)
            for piece, slot in ((own.astype(jnp.bfloat16), core), (sibling_ref[i], 1 - core)):
                at = (2 * i + slot) * width
                o_ref[:, at : at + width] = piece

    for core in range(2):

        @pl.when(place[3] == core)
        def _():
            fill(core)


def finish(place, keep, got, sibling):
    count, rows, width = keep.shape
    return pl.pallas_call(
        finish_kernel,
        out_shape=jax.ShapeDtypeStruct((rows, 2 * count * width), jnp.bfloat16),
        in_specs=[SMEM] + [VMEM] * (2 + len(got)),
        out_specs=VMEM,
        cost_estimate=pl.CostEstimate(
            flops=count * rows * width, bytes_accessed=12 * count * rows * width, transcendentals=0
        ),
        compiler_params=pltpu.CompilerParams(vmem_limit_bytes=12 * 1024 * 1024),
        name="finish",
    )(place, keep, *got, sibling)


def solution(mesh):
    placed = (
        P(("grp", "seq", "sub"), None),
        P(),
        P(None, ("seq", "sub"), "head"),
        P(None, ("seq", "sub"), None),
        P(None, ("seq", "sub"), None),
        P(None, "head", ("seq", "sub")),
        P("grp"),
        P("grp"),
    )
    return jax.shard_map(
        body,
        mesh=mesh,
        in_specs=placed,
        out_specs=P(("grp", "seq", "sub"), "head"),
        check_vma=False,
    )
```

```python
import functools
import math

import jax
import jax.numpy as jnp
from jax import lax
from jax.experimental import pallas as pl
from jax.experimental.pallas import tpu as pltpu
from jax.sharding import PartitionSpec as P


HEAD_DIM = 128
KV_HEADS = 4
RUN = 64
EPS = 1e-06
LOW = -1e30


def swap(x, axis):
    return lax.ppermute(x, axis, [(0, 1), (1, 0)])


def cross(x, axis, bit, among=None):
    size = lax.axis_size(axis)
    return lax.ppermute(x, axis, [(i ^ bit, i) for i in (among or range(size))])


def after(value, *done):
    return lax.optimization_barrier((value, *done))[0]


def add(a, b):
    return (a.astype(jnp.float32) + b.astype(jnp.float32)).astype(jnp.bfloat16)


VMEM = pl.BlockSpec(memory_space=pltpu.VMEM)
SMEM = pl.BlockSpec(memory_space=pltpu.SMEM)
HBM = pl.BlockSpec(memory_space=pltpu.HBM)


def in_hbm(x):
    return pltpu.with_memory_space_constraint(x, pltpu.HBM)


def norm_kernel(place, modality, tokens_ref, gain_ref, own_ref, *rest):
    send_refs, scratch = rest[:-1], rest[-1]
    width = own_ref.shape[1]
    for at in range(0, tokens_ref.shape[0], RUN):
        values = tokens_ref[at : at + RUN].astype(jnp.float32)
        factor = lax.rsqrt(jnp.mean(values * values, axis=1, keepdims=True) + EPS)
        gain = jnp.where(modality[place[4] + at] == 1, gain_ref[1:2, :], gain_ref[0:1, :])
        scratch[at : at + RUN] = (values * factor * gain).astype(jnp.bfloat16)

    def columns(d):
        return pl.ds(pl.multiple_of((place[0] ^ d) * width, width), width)

    own_ref[...] = scratch[:, columns(0)]
    for d, ref in enumerate(send_refs, 1):
        rows = ref.shape[0]
        ref[...] = scratch[pl.ds(pl.multiple_of(place[1] * rows, rows), rows), columns(d)]


def norm_columns(tokens, norm_gain, modality, mod, place, n, rows):
    length, depth = tokens.shape
    width = depth // n
    if width % 128:
        values32 = tokens.astype(jnp.float32)
        factor = lax.rsqrt(jnp.mean(values32 * values32, axis=1, keepdims=True) + EPS)
        gain = jnp.where((mod == 1)[:, None], norm_gain[1][None, :], norm_gain[0][None, :])
        normed = (values32 * factor * gain).astype(jnp.bfloat16)
        first = [0] + [place[1] * rows] * (n - 1)
        count = [length] + [rows] * (n - 1)
        return [
            lax.dynamic_slice(normed, (first[d], (place[0] ^ d) * width), (count[d], width))
            for d in range(n)
        ]
    shapes = [jax.ShapeDtypeStruct((length, width), jnp.bfloat16)]
    shapes += [jax.ShapeDtypeStruct((rows, width), jnp.bfloat16)] * (n - 1)
    return pl.pallas_call(
        norm_kernel,
        out_shape=shapes,
        in_specs=[SMEM, SMEM, VMEM, VMEM],
        out_specs=[VMEM] * n,
        scratch_shapes=[pltpu.VMEM((length, depth), jnp.bfloat16)],
        cost_estimate=pl.CostEstimate(
            flops=6 * length * depth, bytes_accessed=4 * length * depth, transcendentals=length
        ),
        compiler_params=pltpu.CompilerParams(vmem_limit_bytes=12 * 1024 * 1024),
        name="norm",
    )(place, modality, tokens, norm_gain)


def partial_kernel(counts, narrow, place, modality, begins, *rest):
    total = sum(counts)
    sources, refs, outs = rest[:6], rest[6 : 6 + total], rest[6 + total : -8]
    both, other, held_kv, held_q, wide_kv, wide_q, arrived, left = rest[-8:]
    length = both.shape[0] // len(counts)
    half = length // 2
    kv_half = held_kv.shape[2] // 2
    depth = held_kv.shape[1] // 2
    copies = []

    def fetch(source, target):
        copies.append(pltpu.make_async_copy(source, target, arrived.at[len(copies)]))
        copies[-1].start()

    at = 0
    for number, count in enumerate(counts):
        base = number * length
        if count == 1:
            fetch(refs[at], both.at[base : base + length])
        else:
            for which in range(2):
                row = base + (place[1] if which == 0 else 1 - place[1]) * half
                fetch(refs[at + which], both.at[pl.ds(pl.multiple_of(row, half), half)])
        at += count
    for i, source in enumerate(sources):
        core = place[3] if i % 2 == 0 else 1 - place[3]
        rows = pl.ds(pl.multiple_of(core * depth, depth), depth)
        target = (
            held_kv.at[:, rows, 0:kv_half],
            held_kv.at[:, rows, kv_half : 2 * kv_half],
            held_q.at[:, rows],
        )[i // 2]
        fetch(source, target)
    for copy in copies[:total]:
        copy.wait()
    for number in range(len(counts)):
        for step in range(0, length, RUN):
            rows = pl.ds(number * length + step, RUN)
            generate = modality[begins[number] + step] == 1
            block = both[rows]
            zero = jnp.zeros_like(block)
            both[rows] = jnp.where(generate, zero, block)
            other[rows] = jnp.where(generate, block, zero)
    first, second = both[...], other[...]
    pieces = wide_q.shape[0]
    width = wide_q.shape[2]
    stores = []

    def project(held, cols, wide, out):
        value = jnp.dot(first, held[0, :, cols], preferred_element_type=jnp.float32) + jnp.dot(
            second, held[1, :, cols], preferred_element_type=jnp.float32
        )
        wide[...] = value
        stores.append(pltpu.make_async_copy(wide, out, left.at[len(stores)]))
        stores[-1].start()
        return value.astype(jnp.bfloat16)

    for copy in copies[total : total + 4]:
        copy.wait()
    value = project(held_kv, slice(None), wide_kv, outs[0])
    if narrow:
        outs[2][...] = value
    for copy in copies[total + 4 :]:
        copy.wait()
    for piece in range(pieces):
        cols = slice(piece * width, (piece + 1) * width)
        value = project(held_q, cols, wide_q.at[piece], outs[1].at[:, cols])
        if narrow:
            for number in range(len(counts)):
                outs[3 + number][:, cols] = value[number * length : (number + 1) * length]
    for store in stores:
        store.wait()


def partial(blocks, begins, length, modality, weights, place, narrow):
    counts = tuple(len(block) for block in blocks)
    places = [pair for block in blocks for pair in enumerate(block)]
    arrays = [array for _, array in places]
    rows, width = length * len(blocks), arrays[0].shape[1]
    pieces = 2 if weights[4].shape[2] % 256 == 0 else 1
    kv_cols, q_cols = 2 * weights[0].shape[2], weights[4].shape[2]
    shapes = [pltpu.HBM((rows, cols), jnp.float32) for cols in (kv_cols, q_cols)]
    if narrow:
        shapes.append(jax.ShapeDtypeStruct((rows, kv_cols), jnp.bfloat16))
        shapes += [jax.ShapeDtypeStruct((length, q_cols), jnp.bfloat16)] * len(blocks)
    values = pl.pallas_call(
        functools.partial(partial_kernel, counts, narrow),
        out_shape=shapes,
        in_specs=[SMEM] * 3 + [HBM] * len(weights) + [VMEM if i else HBM for i, _ in places],
        out_specs=[HBM] * 2 + [VMEM] * (len(shapes) - 2),
        scratch_shapes=[
            pltpu.VMEM((rows, width), jnp.bfloat16),
            pltpu.VMEM((rows, width), jnp.bfloat16),
            pltpu.VMEM((2, width, kv_cols), jnp.bfloat16),
            pltpu.VMEM((2, width, q_cols), jnp.bfloat16),
            pltpu.VMEM((rows, kv_cols), jnp.float32),
            pltpu.VMEM((pieces, rows, q_cols // pieces), jnp.float32),
            pltpu.SemaphoreType.DMA((len(weights) + len(arrays),)),
            pltpu.SemaphoreType.DMA((1 + pieces,)),
        ],
        cost_estimate=pl.CostEstimate(
            flops=4 * rows * width * (kv_cols + q_cols),
            bytes_accessed=4 * (width + rows) * (kv_cols + q_cols),
            transcendentals=0,
        ),
        compiler_params=pltpu.CompilerParams(vmem_limit_bytes=24 * 1024 * 1024),
        name="partial",
    )(
        place,
        modality,
        begins,
        *[in_hbm(w) for w in weights],
        *[a if i else in_hbm(a) for i, a in places],
    )
    return [value.reshape(len(blocks), length, -1) for value in values[:3]] + list(values[3:])


def halving(parts):
    n = len(parts)
    sums = dict(enumerate(parts))
    for bit in [1 << i for i in range(n.bit_length() - 1)]:
        for d in [d for d in range(n) if d in sums and d & bit]:
            sums[d ^ bit] = sums[d ^ bit] + cross(sums.pop(d).astype(jnp.bfloat16), "seq", bit)
    return sums[0].astype(jnp.bfloat16)


def along_four(parts, three, two):
    wide = [p.astype(jnp.float32) for p in parts]

    def hop(value, bit, among):
        return cross(value, "seq", bit, among)

    def plus(a, b):
        return (a + b.astype(jnp.float32)).astype(jnp.bfloat16)

    if two is None:
        got = hop(three, 1, (1, 2))
        got = hop(plus(jnp.stack([wide[2], wide[3]]), got), 3, (1, 2))
        across, own = got[0], got[1]
    else:
        far = hop(three, 1, (1, 2))
        close = hop(two, 1, (1, 2))
        send = plus(wide[2], far)
        across = hop(send, 3, (1, 2))
        own = hop(plus(wide[3], after(close, send)), 3, (1, 2))
    last = hop(plus(wide[1], across), 1, None)
    return (wide[0] + last.astype(jnp.float32) + own.astype(jnp.float32)).astype(jnp.bfloat16)


def gather_weights(mine):
    n = lax.axis_size("seq")
    if n == 4:
        z = lax.axis_index("seq")
        inner = (z == 1) | (z == 2)
        one = cross(mine, "seq", 1)
        middle = cross(mine, "seq", 3, (1, 2))
        middle_two = cross(one, "seq", 3, (1, 2))
        outer_two = cross(middle, "seq", 1, (0, 3))
        outer_three = cross(middle_two, "seq", 1, (0, 3))
        near = [mine, one, jnp.where(inner, middle_two, outer_two), jnp.where(inner, middle, outer_three)]
    else:
        near = [mine]
        for bit in reversed([1 << i for i in range(n.bit_length() - 1)]):
            got = cross(jnp.stack(near), "seq", bit)
            near = near + [got[i] for i in range(len(near))]
        order = [0]
        for bit in reversed([1 << i for i in range(n.bit_length() - 1)]):
            order = order + [d ^ bit for d in order]
        near = [near[order.index(d)] for d in range(n)]
    far = []
    for d in range(1, n):
        far.append(swap(near[d], "grp"))
    return near[1:], far


def spans(modality, doc_ids, own_mod, own_doc, own_pos):
    changed = (modality[1:] != modality[:-1]) | (doc_ids[1:] != doc_ids[:-1])
    begins = jnp.concatenate([jnp.ones((1,), jnp.int32), changed.astype(jnp.int32)])
    blocks = jnp.cumsum(begins)
    own_block = lax.dynamic_slice_in_dim(blocks, own_pos[0], own_pos.shape[0])
    low = jnp.sum((doc_ids[None, :] < own_doc[:, None]).astype(jnp.int32), axis=1)
    end = jnp.sum((blocks[None, :] <= own_block[:, None]).astype(jnp.int32), axis=1) - 1
    return low, jnp.where(own_mod == 1, end, own_pos)


def attention_kernel(starts, limits, q_ref, span_ref, *rest):
    sources, (o_ref, kv_ref, queries, bounds, top, total, acc, arrived) = rest[:-8], rest[-8:]
    count, size, _ = kv_ref.shape
    for number, source in enumerate(sources):
        pltpu.make_async_copy(source, kv_ref.at[number], arrived.at[number]).start()
    rows = q_ref.shape[0]
    kv_local, many = queries.shape[0], queries.shape[1]
    repeat = many // rows
    scale = math.log2(math.e) / math.sqrt(HEAD_DIM)
    top[...] = jnp.full_like(top, LOW / 10)
    total[...] = jnp.zeros_like(total)
    acc[...] = jnp.zeros_like(acc)
    for head in range(kv_local * repeat):
        g, r = head // repeat, head % repeat
        queries[g, r * rows : (r + 1) * rows] = q_ref[:, head * HEAD_DIM : (head + 1) * HEAD_DIM]
    columns = span_ref[...].T
    for r in range(repeat):
        bounds[r * rows : (r + 1) * rows] = columns
    transposed = (((1,), (1,)), ((), ()))

    def visit(number, _):
        start = starts[number]
        last = start + size - 1
        pltpu.make_async_copy(sources[0], kv_ref.at[number], arrived.at[number]).wait()

        def block(masked):
            for g in range(kv_local):
                keys = kv_ref[number, :, g * HEAD_DIM : (g + 1) * HEAD_DIM]
                values = kv_ref[number, :, (kv_local + g) * HEAD_DIM : (kv_local + g + 1) * HEAD_DIM]
                scores = lax.dot_general(
                    queries[g], keys, transposed, preferred_element_type=jnp.float32
                )
                if masked:
                    key_pos = start + lax.broadcasted_iota(jnp.int32, (many, size), 1)
                    seen = (key_pos >= bounds[:, 0:1]) & (key_pos <= bounds[:, 1:2])
                    scores = jnp.where(seen, scores, LOW)
                old = top[g]
                new = jnp.maximum(old, jnp.max(scores, axis=1, keepdims=True))
                weights = jnp.exp2((scores - jnp.tile(new, (1, size // 128))) * scale)
                shrink = jnp.exp2((old - new) * scale)
                total[g] = total[g] * shrink + jnp.sum(weights, axis=1, keepdims=True)
                top[g] = new
                acc[g] = acc[g] * shrink + jnp.dot(
                    weights.astype(jnp.bfloat16), values, preferred_element_type=jnp.float32
                )

        inside = (start >= limits[2]) & (last <= limits[3])

        @pl.when(inside)
        def _():
            block(False)

        @pl.when(jnp.logical_not(inside) & (start <= limits[1]) & (last >= limits[0]))
        def _():
            block(True)

        return 0

    lax.fori_loop(0, count, visit, 0)
    for head in range(kv_local * repeat):
        g, at = head // repeat, pl.ds((head % repeat) * rows, rows)
        o_ref[:, head * HEAD_DIM : (head + 1) * HEAD_DIM] = (acc[g, at] / total[g, at]).astype(
            jnp.bfloat16
        )


def attend(query, kv, starts, limits, span):
    rows, width = query.shape
    heads = width // HEAD_DIM
    count, (size, kv_cols) = len(kv), kv[0].shape
    kv_local = kv_cols // (2 * HEAD_DIM)
    many = rows * heads // kv_local
    return pl.pallas_call(
        attention_kernel,
        out_shape=jax.ShapeDtypeStruct((rows, width), jnp.bfloat16),
        in_specs=[SMEM, SMEM, VMEM, VMEM] + [HBM] * (count // 2) + [VMEM] * (count // 2),
        out_specs=VMEM,
        scratch_shapes=[
            pltpu.VMEM((count, size, kv_cols), jnp.bfloat16),
            pltpu.VMEM((kv_local, many, HEAD_DIM), jnp.bfloat16),
            pltpu.VMEM((many, 8), jnp.int32),
            pltpu.VMEM((kv_local, many, HEAD_DIM), jnp.float32),
            pltpu.VMEM((kv_local, many, HEAD_DIM), jnp.float32),
            pltpu.VMEM((kv_local, many, HEAD_DIM), jnp.float32),
            pltpu.SemaphoreType.DMA((count,)),
        ],
        cost_estimate=pl.CostEstimate(
            flops=4 * rows * count * size * width,
            bytes_accessed=2 * (2 * rows * width + count * size * kv_cols),
            transcendentals=rows * count * size * heads,
        ),
        compiler_params=pltpu.CompilerParams(vmem_limit_bytes=20 * 1024 * 1024),
        name="attend",
    )(
        starts,
        limits,
        query,
        span,
        *[in_hbm(block) for block in kv[: count // 2]],
        *kv[count // 2 :],
    )


def project_kernel(turns, place, ours_ref, beside_ref, ours_near, beside_near, own_ref, *rest):
    n = (len(rest) - 5) // 2 + 1
    near, far = rest[: n - 1], rest[n - 1 : 2 * n - 2]
    o_ours, o_beside, held, lhs, arrived = rest[2 * n - 2 :]
    count = turns.shape[0]
    first = place[2]

    def fetch(i, d):
        @pl.when(turns[i] == d)
        def _():
            sources = (near[d - 1], far[d - 1]) if d else (own_ref.at[first], own_ref.at[1 - first])
            for kind, source in enumerate(sources):
                pltpu.make_async_copy(source, held.at[kind, i], arrived.at[kind, i]).start()

    for i in range(count):
        for d in range(n):
            fetch(i, d)

    rows = ours_ref.shape[0]
    for base, a_ref, near_ref in ((0, ours_ref, ours_near), (rows, beside_ref, beside_near)):
        a = a_ref[...]
        mine = near_ref[...] != 0
        zero = jnp.zeros_like(a)
        lhs[0, base : base + rows] = jnp.where(mine, a, zero)
        lhs[1, base : base + rows] = jnp.where(mine, zero, a)
    contract = (((1,), (1,)), ((), ()))
    for i in range(count):
        value = None
        for kind in range(2):
            pltpu.make_async_copy(own_ref.at[0], held.at[kind, i], arrived.at[kind, i]).wait()
            term = lax.dot_general(
                lhs[kind], held[kind, i], contract, preferred_element_type=jnp.float32
            )
            value = term if value is None else value + term
        value = value.astype(jnp.bfloat16)
        o_ours[i] = value[:rows]
        o_beside[i] = value[rows:]


def project(ours, beside, ours_near, beside_near, weights, turns, place):
    rows, depth = ours.shape
    count = turns.shape[0]
    width = weights[0].shape[1]
    shape = jax.ShapeDtypeStruct((count, rows, width), jnp.bfloat16)
    return pl.pallas_call(
        project_kernel,
        out_shape=(shape, shape),
        in_specs=[SMEM, SMEM] + [VMEM] * 4 + [HBM] * len(weights),
        out_specs=(VMEM, VMEM),
        scratch_shapes=[
            pltpu.VMEM((2, count, width, depth), jnp.bfloat16),
            pltpu.VMEM((2, 2 * rows, depth), jnp.bfloat16),
            pltpu.SemaphoreType.DMA((2, count)),
        ],
        cost_estimate=pl.CostEstimate(
            flops=8 * count * rows * depth * width,
            bytes_accessed=4 * count * depth * width + 4 * count * rows * width,
            transcendentals=0,
        ),
        compiler_params=pltpu.CompilerParams(vmem_limit_bytes=16 * 1024 * 1024),
        name="project",
    )(turns, place, ours, beside, ours_near[:, None], beside_near[:, None], *weights)


def body(tokens, norm_gain, w_query, w_key, w_value, w_out, modality, doc_ids):
    length, _ = tokens.shape
    n = lax.axis_size("seq")
    subs = lax.axis_size("sub")
    heads_over = lax.axis_size("head")
    z, s = lax.axis_index("seq"), lax.axis_index("sub")
    x, y = lax.axis_index("head"), lax.axis_index("grp")
    place = jnp.stack([z, x, y, s, (z * subs + s) * length]).astype(jnp.int32)

    kv_local = max(KV_HEADS // heads_over, 1)
    kv_first = x * KV_HEADS // heads_over
    w_out = jnp.swapaxes(w_out, 1, 2)

    def part_of(array, place, core):
        return lax.dynamic_slice_in_dim(array, (place * subs + core) * length, length)

    mine = lax.dynamic_index_in_dim(w_out, y, 0, keepdims=False)
    near, far = gather_weights(mine)
    weights = [w_out] + near + far

    own_mod = part_of(modality, z, s)
    share_rows = heads_over == 2
    rows = length // 2 if share_rows else length
    sends = norm_columns(tokens, norm_gain, modality, own_mod, place, n, rows)
    blocks = {0: (sends[0],)}
    for d in range(n - 1, 0, -1):
        blocks[d] = (cross(sends[d], "seq", d),)

    w_query, w_key, w_value = after((w_query, w_key, w_value), sends[0])

    key_cols = lax.dynamic_slice_in_dim(w_key, kv_first * HEAD_DIM, kv_local * HEAD_DIM, 2)
    value_cols = lax.dynamic_slice_in_dim(w_value, kv_first * HEAD_DIM, kv_local * HEAD_DIM, 2)
    row_weights = []
    for weight in (key_cols, value_cols, w_query):
        row_weights += [weight, swap(weight, "sub")]
    modality, doc_ids = after((modality, doc_ids), sends[0])
    own_doc = part_of(doc_ids, z, s)
    own_pos = (z * subs + s) * length + jnp.arange(length, dtype=jnp.int32)
    low, high = spans(modality, doc_ids, part_of(modality, z, s), own_doc, own_pos)
    span = jnp.concatenate([low[None], high[None], jnp.zeros((6, length), jnp.int32)])
    limits = jnp.stack([low[0], high[-1], low[-1], high[0]])

    if share_rows:
        for d in range(n - 1, 0, -1):
            blocks[d] = (*blocks[d], swap(blocks[d][0], "head"))
    blocks[n - 1] = after(blocks[n - 1], span, limits)

    def parts_of(group, narrow):
        begins = jnp.stack([((z ^ d) * subs + s) * length for d in group]).astype(jnp.int32)
        arrays = [blocks[d] for d in group]
        return partial(arrays, begins, length, modality, row_weights, place, narrow)

    if n == 4:
        kv_early, q_early, kv_ends, q_three, q_two = parts_of([3, 2], True)
        kv_late, q_late = parts_of([1, 0], False)
        kv_early, q_early = after((kv_early, q_early), kv_late, q_late)
        kv = along_four([kv_late[1], kv_late[0], kv_early[1], kv_early[0]], kv_ends, None)
        query = along_four([q_late[1], q_late[0], q_early[1], q_early[0]], q_three, q_two)
    else:
        kv_parts, q_parts = [], []
        for d in range(n):
            kv_part, q_part = parts_of([d], False)
            kv_parts.append(kv_part[0])
            q_parts.append(q_part[0])
        kv, query = halving(kv_parts), halving(q_parts)

    same = [kv]
    for d in range(1, n):
        same.append(cross(kv, "seq", d))
    beside = []
    for d in range(n):
        beside.append(swap(same[d], "sub"))
    starts = jnp.stack(
        [((z ^ d) * subs + s) * length for d in range(n)]
        + [((z ^ d) * subs + (1 - s)) * length for d in range(n)]
    ).astype(jnp.int32)
    attended = attend(query, same + beside, starts, limits, span)

    beside = swap(attended, "sub")
    ours_near = (own_mod == y).astype(jnp.bfloat16)
    beside_near = (part_of(modality, z, 1 - s) == y).astype(jnp.bfloat16)

    def out(columns):
        turns = (columns ^ z).astype(jnp.int32)
        return project(attended, beside, ours_near, beside_near, weights, turns, place)

    if heads_over != 2:
        ours, theirs = out(jnp.arange(n))
        sibling = swap(theirs, "sub")
        pair = jnp.where(s == 0, jnp.stack([ours, sibling], 1), jnp.stack([sibling, ours], 1))
        wide = jnp.transpose(pair, (2, 0, 1, 3)).reshape(length, -1)
        return lax.psum_scatter(wide, "head", scatter_dimension=1, tiled=True)

    half = n // 2
    ours, theirs = [], []
    sent = [out((1 - x) * half + jnp.arange(i, i + 1)) for i in range(half)]
    for send_ours, send_beside in sent:
        theirs.append(swap(send_beside, "head"))
        ours.append(swap(send_ours, "head"))
    keep_ours, keep_beside = out(x * half + jnp.arange(half))
    done = add(keep_beside, jnp.concatenate(theirs))
    sibling = swap(done, "sub")
    return finish(place, keep_ours, ours, sibling)


def finish_kernel(place, keep_ref, *rest):
    got_refs, sibling_ref, o_ref = rest[:-2], rest[-2], rest[-1]
    width = keep_ref.shape[2]

    def fill(core):
        for i, got_ref in enumerate(got_refs):
            own = keep_ref[i].astype(jnp.float32) + got_ref[0].astype(jnp.float32)
            for piece, slot in ((own.astype(jnp.bfloat16), core), (sibling_ref[i], 1 - core)):
                at = (2 * i + slot) * width
                o_ref[:, at : at + width] = piece

    for core in range(2):

        @pl.when(place[3] == core)
        def _():
            fill(core)


def finish(place, keep, got, sibling):
    count, rows, width = keep.shape
    return pl.pallas_call(
        finish_kernel,
        out_shape=jax.ShapeDtypeStruct((rows, 2 * count * width), jnp.bfloat16),
        in_specs=[SMEM] + [VMEM] * (2 + len(got)),
        out_specs=VMEM,
        cost_estimate=pl.CostEstimate(
            flops=count * rows * width, bytes_accessed=12 * count * rows * width, transcendentals=0
        ),
        compiler_params=pltpu.CompilerParams(vmem_limit_bytes=12 * 1024 * 1024),
        name="finish",
    )(place, keep, *got, sibling)


def solution(mesh):
    placed = (
        P(("grp", "seq", "sub"), None),
        P(),
        P(None, ("seq", "sub"), "head"),
        P(None, ("seq", "sub"), None),
        P(None, ("seq", "sub"), None),
        P(None, "head", ("seq", "sub")),
        P("grp"),
        P("grp"),
    )
    return jax.shard_map(
        body,
        mesh=mesh,
        in_specs=placed,
        out_specs=P(("grp", "seq", "sub"), "head"),
        check_vma=False,
    )
```

```python
import functools
import math

import jax
import jax.numpy as jnp
from jax import lax
from jax.experimental import pallas as pl
from jax.experimental.pallas import tpu as pltpu
from jax.sharding import PartitionSpec as P


HEAD_DIM = 128
KV_HEADS = 4
RUN = 64
EPS = 1e-06
LOW = -1e30


def swap(x, axis):
    return lax.ppermute(x, axis, [(0, 1), (1, 0)])


def cross(x, axis, bit, among=None):
    size = lax.axis_size(axis)
    return lax.ppermute(x, axis, [(i ^ bit, i) for i in (among or range(size))])


def after(value, *done):
    return lax.optimization_barrier((value, *done))[0]


def add(a, b):
    return (a.astype(jnp.float32) + b.astype(jnp.float32)).astype(jnp.bfloat16)


VMEM = pl.BlockSpec(memory_space=pltpu.VMEM)
SMEM = pl.BlockSpec(memory_space=pltpu.SMEM)
HBM = pl.BlockSpec(memory_space=pltpu.HBM)


def in_hbm(x):
    return pltpu.with_memory_space_constraint(x, pltpu.HBM)


def norm_kernel(place, modality, tokens_ref, gain_ref, own_ref, *rest):
    send_refs, scratch = rest[:-1], rest[-1]
    width = own_ref.shape[1]
    for at in range(0, tokens_ref.shape[0], RUN):
        values = tokens_ref[at : at + RUN].astype(jnp.float32)
        factor = lax.rsqrt(jnp.mean(values * values, axis=1, keepdims=True) + EPS)
        gain = jnp.where(modality[place[4] + at] == 1, gain_ref[1:2, :], gain_ref[0:1, :])
        scratch[at : at + RUN] = (values * factor * gain).astype(jnp.bfloat16)

    def columns(d):
        return pl.ds(pl.multiple_of((place[0] ^ d) * width, width), width)

    own_ref[...] = scratch[:, columns(0)]
    for d, ref in enumerate(send_refs, 1):
        rows = ref.shape[0]
        ref[...] = scratch[pl.ds(pl.multiple_of(place[1] * rows, rows), rows), columns(d)]


def norm_columns(tokens, norm_gain, modality, mod, place, n, rows):
    length, depth = tokens.shape
    width = depth // n
    if width % 128:
        values32 = tokens.astype(jnp.float32)
        factor = lax.rsqrt(jnp.mean(values32 * values32, axis=1, keepdims=True) + EPS)
        gain = jnp.where((mod == 1)[:, None], norm_gain[1][None, :], norm_gain[0][None, :])
        normed = (values32 * factor * gain).astype(jnp.bfloat16)
        first = [0] + [place[1] * rows] * (n - 1)
        count = [length] + [rows] * (n - 1)
        return [
            lax.dynamic_slice(normed, (first[d], (place[0] ^ d) * width), (count[d], width))
            for d in range(n)
        ]
    shapes = [jax.ShapeDtypeStruct((length, width), jnp.bfloat16)]
    shapes += [jax.ShapeDtypeStruct((rows, width), jnp.bfloat16)] * (n - 1)
    return pl.pallas_call(
        norm_kernel,
        out_shape=shapes,
        in_specs=[SMEM, SMEM, VMEM, VMEM],
        out_specs=[VMEM] * n,
        scratch_shapes=[pltpu.VMEM((length, depth), jnp.bfloat16)],
        cost_estimate=pl.CostEstimate(
            flops=6 * length * depth, bytes_accessed=4 * length * depth, transcendentals=length
        ),
        compiler_params=pltpu.CompilerParams(vmem_limit_bytes=12 * 1024 * 1024),
        name="norm",
    )(place, modality, tokens, norm_gain)


def partial_kernel(counts, narrow, place, modality, begins, *rest):
    total = sum(counts)
    sources, refs, outs = rest[:6], rest[6 : 6 + total], rest[6 + total : -8]
    both, other, held_kv, held_q, wide_kv, wide_q, arrived, left = rest[-8:]
    length = both.shape[0] // len(counts)
    half = length // 2
    kv_half = held_kv.shape[2] // 2
    depth = held_kv.shape[1] // 2
    copies = []

    def fetch(source, target):
        copies.append(pltpu.make_async_copy(source, target, arrived.at[len(copies)]))
        copies[-1].start()

    at = 0
    for number, count in enumerate(counts):
        base = number * length
        if count == 1:
            fetch(refs[at], both.at[base : base + length])
        else:
            for which in range(2):
                row = base + (place[1] if which == 0 else 1 - place[1]) * half
                fetch(refs[at + which], both.at[pl.ds(pl.multiple_of(row, half), half)])
        at += count
    for i, source in enumerate(sources):
        core = place[3] if i % 2 == 0 else 1 - place[3]
        rows = pl.ds(pl.multiple_of(core * depth, depth), depth)
        target = (
            held_kv.at[:, rows, 0:kv_half],
            held_kv.at[:, rows, kv_half : 2 * kv_half],
            held_q.at[:, rows],
        )[i // 2]
        fetch(source, target)
    for copy in copies[:total]:
        copy.wait()
    for number in range(len(counts)):
        for step in range(0, length, RUN):
            rows = pl.ds(number * length + step, RUN)
            generate = modality[begins[number] + step] == 1
            block = both[rows]
            zero = jnp.zeros_like(block)
            both[rows] = jnp.where(generate, zero, block)
            other[rows] = jnp.where(generate, block, zero)
    first, second = both[...], other[...]
    pieces = wide_q.shape[0]
    width = wide_q.shape[2]
    stores = []

    def project(held, cols, wide, out):
        value = jnp.dot(first, held[0, :, cols], preferred_element_type=jnp.float32) + jnp.dot(
            second, held[1, :, cols], preferred_element_type=jnp.float32
        )
        wide[...] = value
        stores.append(pltpu.make_async_copy(wide, out, left.at[len(stores)]))
        stores[-1].start()
        return value.astype(jnp.bfloat16)

    for copy in copies[total : total + 4]:
        copy.wait()
    value = project(held_kv, slice(None), wide_kv, outs[0])
    if narrow:
        outs[2][...] = value
    for copy in copies[total + 4 :]:
        copy.wait()
    for piece in range(pieces):
        cols = slice(piece * width, (piece + 1) * width)
        value = project(held_q, cols, wide_q.at[piece], outs[1].at[:, cols])
        if narrow:
            for number in range(len(counts)):
                outs[3 + number][:, cols] = value[number * length : (number + 1) * length]
    for store in stores:
        store.wait()


def partial(blocks, begins, length, modality, weights, place, narrow):
    counts = tuple(len(block) for block in blocks)
    places = [pair for block in blocks for pair in enumerate(block)]
    arrays = [array for _, array in places]
    rows, width = length * len(blocks), arrays[0].shape[1]
    pieces = 2 if weights[4].shape[2] % 256 == 0 else 1
    kv_cols, q_cols = 2 * weights[0].shape[2], weights[4].shape[2]
    shapes = [pltpu.HBM((rows, cols), jnp.float32) for cols in (kv_cols, q_cols)]
    if narrow:
        shapes.append(jax.ShapeDtypeStruct((rows, kv_cols), jnp.bfloat16))
        shapes += [jax.ShapeDtypeStruct((length, q_cols), jnp.bfloat16)] * len(blocks)
    values = pl.pallas_call(
        functools.partial(partial_kernel, counts, narrow),
        out_shape=shapes,
        in_specs=[SMEM] * 3 + [HBM] * len(weights) + [VMEM if i else HBM for i, _ in places],
        out_specs=[HBM] * 2 + [VMEM] * (len(shapes) - 2),
        scratch_shapes=[
            pltpu.VMEM((rows, width), jnp.bfloat16),
            pltpu.VMEM((rows, width), jnp.bfloat16),
            pltpu.VMEM((2, width, kv_cols), jnp.bfloat16),
            pltpu.VMEM((2, width, q_cols), jnp.bfloat16),
            pltpu.VMEM((rows, kv_cols), jnp.float32),
            pltpu.VMEM((pieces, rows, q_cols // pieces), jnp.float32),
            pltpu.SemaphoreType.DMA((len(weights) + len(arrays),)),
            pltpu.SemaphoreType.DMA((1 + pieces,)),
        ],
        cost_estimate=pl.CostEstimate(
            flops=4 * rows * width * (kv_cols + q_cols),
            bytes_accessed=4 * (width + rows) * (kv_cols + q_cols),
            transcendentals=0,
        ),
        compiler_params=pltpu.CompilerParams(vmem_limit_bytes=24 * 1024 * 1024),
        name="partial",
    )(
        place,
        modality,
        begins,
        *[in_hbm(w) for w in weights],
        *[a if i else in_hbm(a) for i, a in places],
    )
    return [value.reshape(len(blocks), length, -1) for value in values[:3]] + list(values[3:])


def halving(parts):
    n = len(parts)
    sums = dict(enumerate(parts))
    for bit in [1 << i for i in range(n.bit_length() - 1)]:
        for d in [d for d in range(n) if d in sums and d & bit]:
            sums[d ^ bit] = sums[d ^ bit] + cross(sums.pop(d).astype(jnp.bfloat16), "seq", bit)
    return sums[0].astype(jnp.bfloat16)


def along_four(parts, three, two):
    wide = [p.astype(jnp.float32) for p in parts]

    def hop(value, bit, among):
        return cross(value, "seq", bit, among)

    def plus(a, b):
        return (a + b.astype(jnp.float32)).astype(jnp.bfloat16)

    if two is None:
        got = hop(three, 1, (1, 2))
        got = hop(plus(jnp.stack([wide[2], wide[3]]), got), 3, (1, 2))
        across, own = got[0], got[1]
    else:
        far = hop(three, 1, (1, 2))
        close = hop(two, 1, (1, 2))
        send = plus(wide[2], far)
        across = hop(send, 3, (1, 2))
        own = hop(plus(wide[3], after(close, send)), 3, (1, 2))
    last = hop(plus(wide[1], across), 1, None)
    return (wide[0] + last.astype(jnp.float32) + own.astype(jnp.float32)).astype(jnp.bfloat16)


def gather_weights(mine):
    n = lax.axis_size("seq")
    if n == 4:
        z = lax.axis_index("seq")
        inner = (z == 1) | (z == 2)
        one = cross(mine, "seq", 1)
        middle = cross(mine, "seq", 3, (1, 2))
        middle_two = cross(one, "seq", 3, (1, 2))
        outer_two = cross(middle, "seq", 1, (0, 3))
        outer_three = cross(middle_two, "seq", 1, (0, 3))
        near = [mine, one, jnp.where(inner, middle_two, outer_two), jnp.where(inner, middle, outer_three)]
    else:
        near = [mine]
        for bit in reversed([1 << i for i in range(n.bit_length() - 1)]):
            got = cross(jnp.stack(near), "seq", bit)
            near = near + [got[i] for i in range(len(near))]
        order = [0]
        for bit in reversed([1 << i for i in range(n.bit_length() - 1)]):
            order = order + [d ^ bit for d in order]
        near = [near[order.index(d)] for d in range(n)]
    far = []
    for d in range(1, n):
        far.append(swap(near[d], "grp"))
    return near[1:], far


def spans(modality, doc_ids, own_mod, own_doc, own_pos):
    changed = (modality[1:] != modality[:-1]) | (doc_ids[1:] != doc_ids[:-1])
    begins = jnp.concatenate([jnp.ones((1,), jnp.int32), changed.astype(jnp.int32)])
    blocks = jnp.cumsum(begins)
    own_block = lax.dynamic_slice_in_dim(blocks, own_pos[0], own_pos.shape[0])
    low = jnp.sum((doc_ids[None, :] < own_doc[:, None]).astype(jnp.int32), axis=1)
    end = jnp.sum((blocks[None, :] <= own_block[:, None]).astype(jnp.int32), axis=1) - 1
    return low, jnp.where(own_mod == 1, end, own_pos)


def attention_kernel(starts, limits, q_ref, span_ref, *rest):
    sources, (o_ref, kv_ref, queries, bounds, top, total, acc, arrived) = rest[:-8], rest[-8:]
    count, size, _ = kv_ref.shape
    for number, source in enumerate(sources):
        pltpu.make_async_copy(source, kv_ref.at[number], arrived.at[number]).start()
    rows = q_ref.shape[0]
    kv_local, many = queries.shape[0], queries.shape[1]
    repeat = many // rows
    scale = math.log2(math.e) / math.sqrt(HEAD_DIM)
    top[...] = jnp.full_like(top, LOW / 10)
    total[...] = jnp.zeros_like(total)
    acc[...] = jnp.zeros_like(acc)
    for head in range(kv_local * repeat):
        g, r = head // repeat, head % repeat
        queries[g, r * rows : (r + 1) * rows] = q_ref[:, head * HEAD_DIM : (head + 1) * HEAD_DIM]
    columns = span_ref[...].T
    for r in range(repeat):
        bounds[r * rows : (r + 1) * rows] = columns
    transposed = (((1,), (1,)), ((), ()))

    def visit(number, _):
        start = starts[number]
        last = start + size - 1
        pltpu.make_async_copy(sources[0], kv_ref.at[number], arrived.at[number]).wait()

        def block(masked):
            for g in range(kv_local):
                keys = kv_ref[number, :, g * HEAD_DIM : (g + 1) * HEAD_DIM]
                values = kv_ref[number, :, (kv_local + g) * HEAD_DIM : (kv_local + g + 1) * HEAD_DIM]
                scores = lax.dot_general(
                    queries[g], keys, transposed, preferred_element_type=jnp.float32
                )
                if masked:
                    key_pos = start + lax.broadcasted_iota(jnp.int32, (many, size), 1)
                    seen = (key_pos >= bounds[:, 0:1]) & (key_pos <= bounds[:, 1:2])
                    scores = jnp.where(seen, scores, LOW)
                old = top[g]
                new = jnp.maximum(old, jnp.max(scores, axis=1, keepdims=True))
                weights = jnp.exp2((scores - jnp.tile(new, (1, size // 128))) * scale)
                shrink = jnp.exp2((old - new) * scale)
                total[g] = total[g] * shrink + jnp.sum(weights, axis=1, keepdims=True)
                top[g] = new
                acc[g] = acc[g] * shrink + jnp.dot(
                    weights.astype(jnp.bfloat16), values, preferred_element_type=jnp.float32
                )

        inside = (start >= limits[2]) & (last <= limits[3])

        @pl.when(inside)
        def _():
            block(False)

        @pl.when(jnp.logical_not(inside) & (start <= limits[1]) & (last >= limits[0]))
        def _():
            block(True)

        return 0

    lax.fori_loop(0, count, visit, 0)
    for head in range(kv_local * repeat):
        g, at = head // repeat, pl.ds((head % repeat) * rows, rows)
        o_ref[:, head * HEAD_DIM : (head + 1) * HEAD_DIM] = (acc[g, at] / total[g, at]).astype(
            jnp.bfloat16
        )


def attend(query, kv, starts, limits, span):
    rows, width = query.shape
    heads = width // HEAD_DIM
    count, (size, kv_cols) = len(kv), kv[0].shape
    kv_local = kv_cols // (2 * HEAD_DIM)
    many = rows * heads // kv_local
    return pl.pallas_call(
        attention_kernel,
        out_shape=jax.ShapeDtypeStruct((rows, width), jnp.bfloat16),
        in_specs=[SMEM, SMEM, VMEM, VMEM] + [HBM] * (count // 2 + 1) + [VMEM] * (count // 2 - 1),
        out_specs=VMEM,
        scratch_shapes=[
            pltpu.VMEM((count, size, kv_cols), jnp.bfloat16),
            pltpu.VMEM((kv_local, many, HEAD_DIM), jnp.bfloat16),
            pltpu.VMEM((many, 8), jnp.int32),
            pltpu.VMEM((kv_local, many, HEAD_DIM), jnp.float32),
            pltpu.VMEM((kv_local, many, HEAD_DIM), jnp.float32),
            pltpu.VMEM((kv_local, many, HEAD_DIM), jnp.float32),
            pltpu.SemaphoreType.DMA((count,)),
        ],
        cost_estimate=pl.CostEstimate(
            flops=4 * rows * count * size * width,
            bytes_accessed=2 * (2 * rows * width + count * size * kv_cols),
            transcendentals=rows * count * size * heads,
        ),
        compiler_params=pltpu.CompilerParams(vmem_limit_bytes=20 * 1024 * 1024),
        name="attend",
    )(
        starts,
        limits,
        query,
        span,
        *[in_hbm(block) for block in kv[: count // 2 + 1]],
        *kv[count // 2 + 1 :],
    )


def project_kernel(n, groups, turns, place, *rest):
    inputs, own_ref, near, far = (
        rest[: 2 * groups],
        rest[2 * groups],
        rest[2 * groups + 1 : 2 * groups + n],
        rest[2 * groups + n : 2 * groups + 2 * n - 1],
    )
    outs, (held, lhs, arrived) = rest[2 * groups + 2 * n - 1 : -3], rest[-3:]
    count = turns.shape[0]
    first = place[2]

    def fetch(i, d):
        @pl.when(turns[i] == d)
        def _():
            sources = (near[d - 1], far[d - 1]) if d else (own_ref.at[first], own_ref.at[1 - first])
            for kind, source in enumerate(sources):
                pltpu.make_async_copy(source, held.at[kind, i], arrived.at[kind, i]).start()

    for i in range(count):
        for d in range(n):
            fetch(i, d)

    rows = inputs[0].shape[0]
    for group in range(groups):
        a = inputs[2 * group][...]
        mine = inputs[2 * group + 1][...] != 0
        zero = jnp.zeros_like(a)
        lhs[0, group * rows : (group + 1) * rows] = jnp.where(mine, a, zero)
        lhs[1, group * rows : (group + 1) * rows] = jnp.where(mine, zero, a)
    contract = (((1,), (1,)), ((), ()))
    for i in range(count):
        value = None
        for kind in range(2):
            pltpu.make_async_copy(own_ref.at[0], held.at[kind, i], arrived.at[kind, i]).wait()
            term = lax.dot_general(
                lhs[kind], held[kind, i], contract, preferred_element_type=jnp.float32
            )
            value = term if value is None else value + term
        value = value.astype(jnp.bfloat16)
        for group in range(groups):
            outs[group][i] = value[group * rows : (group + 1) * rows]


def project(tokens, weights, turns, place):
    rows, depth = tokens[0][0].shape
    groups, count = len(tokens), turns.shape[0]
    width = weights[0].shape[1]
    return pl.pallas_call(
        functools.partial(project_kernel, (len(weights) + 1) // 2, groups),
        out_shape=[jax.ShapeDtypeStruct((count, rows, width), jnp.bfloat16)] * groups,
        in_specs=[SMEM, SMEM] + [VMEM] * (2 * groups) + [HBM] * len(weights),
        out_specs=[VMEM] * groups,
        scratch_shapes=[
            pltpu.VMEM((2, count, width, depth), jnp.bfloat16),
            pltpu.VMEM((2, groups * rows, depth), jnp.bfloat16),
            pltpu.SemaphoreType.DMA((2, count)),
        ],
        cost_estimate=pl.CostEstimate(
            flops=4 * groups * count * rows * depth * width,
            bytes_accessed=4 * count * depth * width + 2 * groups * count * rows * width,
            transcendentals=0,
        ),
        compiler_params=pltpu.CompilerParams(vmem_limit_bytes=16 * 1024 * 1024),
        name="project",
    )(turns, place, *[a for pair in tokens for a in (pair[0], pair[1][:, None])], *weights)


def body(tokens, norm_gain, w_query, w_key, w_value, w_out, modality, doc_ids):
    length, _ = tokens.shape
    n = lax.axis_size("seq")
    subs = lax.axis_size("sub")
    heads_over = lax.axis_size("head")
    z, s = lax.axis_index("seq"), lax.axis_index("sub")
    x, y = lax.axis_index("head"), lax.axis_index("grp")
    place = jnp.stack([z, x, y, s, (z * subs + s) * length]).astype(jnp.int32)

    kv_local = max(KV_HEADS // heads_over, 1)
    kv_first = x * KV_HEADS // heads_over
    w_out = jnp.swapaxes(w_out, 1, 2)

    def part_of(array, place, core):
        return lax.dynamic_slice_in_dim(array, (place * subs + core) * length, length)

    mine = lax.dynamic_index_in_dim(w_out, y, 0, keepdims=False)
    near, far = gather_weights(mine)
    weights = [w_out] + near + far

    own_mod = part_of(modality, z, s)
    share_rows = heads_over == 2
    rows = length // 2 if share_rows else length
    sends = norm_columns(tokens, norm_gain, modality, own_mod, place, n, rows)
    blocks = {0: (sends[0],)}
    for d in range(n - 1, 0, -1):
        blocks[d] = (cross(sends[d], "seq", d),)

    w_query, w_key, w_value = after((w_query, w_key, w_value), sends[0])

    key_cols = lax.dynamic_slice_in_dim(w_key, kv_first * HEAD_DIM, kv_local * HEAD_DIM, 2)
    value_cols = lax.dynamic_slice_in_dim(w_value, kv_first * HEAD_DIM, kv_local * HEAD_DIM, 2)
    row_weights = []
    for weight in (key_cols, value_cols, w_query):
        row_weights += [weight, swap(weight, "sub")]
    modality, doc_ids = after((modality, doc_ids), sends[0])
    own_doc = part_of(doc_ids, z, s)
    own_pos = (z * subs + s) * length + jnp.arange(length, dtype=jnp.int32)
    low, high = spans(modality, doc_ids, part_of(modality, z, s), own_doc, own_pos)
    span = jnp.concatenate([low[None], high[None], jnp.zeros((6, length), jnp.int32)])
    limits = jnp.stack([low[0], high[-1], low[-1], high[0]])

    if share_rows:
        for d in range(n - 1, 0, -1):
            blocks[d] = (*blocks[d], swap(blocks[d][0], "head"))
    blocks[n - 1] = after(blocks[n - 1], span, limits)

    def parts_of(group, narrow):
        begins = jnp.stack([((z ^ d) * subs + s) * length for d in group]).astype(jnp.int32)
        arrays = [blocks[d] for d in group]
        return partial(arrays, begins, length, modality, row_weights, place, narrow)

    if n == 4:
        kv_early, q_early, kv_ends, q_three, q_two = parts_of([3, 2], True)
        kv_late, q_late = parts_of([1, 0], False)
        kv_early, q_early = after((kv_early, q_early), kv_late, q_late)
        kv = along_four([kv_late[1], kv_late[0], kv_early[1], kv_early[0]], kv_ends, None)
        query = along_four([q_late[1], q_late[0], q_early[1], q_early[0]], q_three, q_two)
    else:
        kv_parts, q_parts = [], []
        for d in range(n):
            kv_part, q_part = parts_of([d], False)
            kv_parts.append(kv_part[0])
            q_parts.append(q_part[0])
        kv, query = halving(kv_parts), halving(q_parts)

    same = [kv]
    for d in range(1, n):
        same.append(cross(kv, "seq", d))
    beside = []
    for d in range(n):
        beside.append(swap(same[d], "sub"))
    starts = jnp.stack(
        [((z ^ d) * subs + s) * length for d in range(n)]
        + [((z ^ d) * subs + (1 - s)) * length for d in range(n)]
    ).astype(jnp.int32)
    attended = attend(query, same + beside, starts, limits, span)

    beside = swap(attended, "sub")
    ours_near = (own_mod == y).astype(jnp.bfloat16)
    beside_near = (part_of(modality, z, 1 - s) == y).astype(jnp.bfloat16)

    our_rows, beside_rows = (attended, ours_near), (beside, beside_near)

    def out(tokens, columns):
        return project(tokens, weights, (columns ^ z).astype(jnp.int32), place)

    if heads_over != 2:
        ours, theirs = out([our_rows, beside_rows], jnp.arange(n))
        sibling = swap(theirs, "sub")
        pair = jnp.where(s == 0, jnp.stack([ours, sibling], 1), jnp.stack([sibling, ours], 1))
        wide = jnp.transpose(pair, (2, 0, 1, 3)).reshape(length, -1)
        return lax.psum_scatter(wide, "head", scatter_dimension=1, tiled=True)

    half = n // 2
    ours, theirs = [], []

    def piece(tokens, i):
        return out([tokens], (1 - x) * half + jnp.arange(i, i + 1))[0]

    for i in range(half):
        sent = piece(our_rows, i)
        ours.append(swap(sent, "head"))
    for i in range(half):
        sent = piece(beside_rows, i)
        theirs.append(swap(sent, "head"))
    keep_ours, keep_beside = out([our_rows, beside_rows], x * half + jnp.arange(half))
    done = add(keep_beside, jnp.concatenate(theirs))
    sibling = swap(done, "sub")
    return finish(place, keep_ours, ours, sibling)


def finish_kernel(place, keep_ref, *rest):
    got_refs, sibling_ref, o_ref = rest[:-2], rest[-2], rest[-1]
    width = keep_ref.shape[2]

    def fill(core):
        for i, got_ref in enumerate(got_refs):
            own = keep_ref[i].astype(jnp.float32) + got_ref[0].astype(jnp.float32)
            for piece, slot in ((own.astype(jnp.bfloat16), core), (sibling_ref[i], 1 - core)):
                at = (2 * i + slot) * width
                o_ref[:, at : at + width] = piece

    for core in range(2):

        @pl.when(place[3] == core)
        def _():
            fill(core)


def finish(place, keep, got, sibling):
    count, rows, width = keep.shape
    return pl.pallas_call(
        finish_kernel,
        out_shape=jax.ShapeDtypeStruct((rows, 2 * count * width), jnp.bfloat16),
        in_specs=[SMEM] + [VMEM] * (2 + len(got)),
        out_specs=VMEM,
        cost_estimate=pl.CostEstimate(
            flops=count * rows * width, bytes_accessed=12 * count * rows * width, transcendentals=0
        ),
        compiler_params=pltpu.CompilerParams(vmem_limit_bytes=12 * 1024 * 1024),
        name="finish",
    )(place, keep, *got, sibling)


def solution(mesh):
    placed = (
        P(("grp", "seq", "sub"), None),
        P(),
        P(None, ("seq", "sub"), "head"),
        P(None, ("seq", "sub"), None),
        P(None, ("seq", "sub"), None),
        P(None, "head", ("seq", "sub")),
        P("grp"),
        P("grp"),
    )
    return jax.shard_map(
        body,
        mesh=mesh,
        in_specs=placed,
        out_specs=P(("grp", "seq", "sub"), "head"),
        check_vma=False,
    )
```

```python
import functools
import math

import jax
import jax.numpy as jnp
from jax import lax
from jax.experimental import pallas as pl
from jax.experimental.pallas import tpu as pltpu
from jax.sharding import PartitionSpec as P


HEAD_DIM = 128
KV_HEADS = 4
RUN = 64
EPS = 1e-06
LOW = -1e30


def swap(x, axis):
    return lax.ppermute(x, axis, [(0, 1), (1, 0)])


def cross(x, axis, bit, among=None):
    size = lax.axis_size(axis)
    return lax.ppermute(x, axis, [(i ^ bit, i) for i in (among or range(size))])


def after(value, *done):
    return lax.optimization_barrier((value, *done))[0]


def add(a, b):
    return (a.astype(jnp.float32) + b.astype(jnp.float32)).astype(jnp.bfloat16)


VMEM = pl.BlockSpec(memory_space=pltpu.VMEM)
SMEM = pl.BlockSpec(memory_space=pltpu.SMEM)
HBM = pl.BlockSpec(memory_space=pltpu.HBM)


def in_hbm(x):
    return pltpu.with_memory_space_constraint(x, pltpu.HBM)


def norm_kernel(place, modality, tokens_ref, gain_ref, own_ref, *rest):
    send_refs, (scratch, arrived) = rest[:-2], rest[-2:]
    width = own_ref.shape[1]
    copies = []
    for i, at in enumerate(range(0, tokens_ref.shape[0], RUN)):
        rows = pl.ds(at, RUN)
        copies.append(pltpu.make_async_copy(tokens_ref.at[rows], scratch.at[rows], arrived.at[i]))
        copies[-1].start()
    for i, at in enumerate(range(0, tokens_ref.shape[0], RUN)):
        copies[i].wait()
        values = scratch[at : at + RUN].astype(jnp.float32)
        factor = lax.rsqrt(jnp.mean(values * values, axis=1, keepdims=True) + EPS)
        gain = jnp.where(modality[place[4] + at] == 1, gain_ref[1:2, :], gain_ref[0:1, :])
        scratch[at : at + RUN] = (values * factor * gain).astype(jnp.bfloat16)

    def columns(d):
        return pl.ds(pl.multiple_of((place[0] ^ d) * width, width), width)

    own_ref[...] = scratch[:, columns(0)]
    for d, ref in enumerate(send_refs, 1):
        rows = ref.shape[0]
        ref[...] = scratch[pl.ds(pl.multiple_of(place[1] * rows, rows), rows), columns(d)]


def norm_columns(tokens, norm_gain, modality, mod, place, n, rows):
    length, depth = tokens.shape
    width = depth // n
    if width % 128:
        values32 = tokens.astype(jnp.float32)
        factor = lax.rsqrt(jnp.mean(values32 * values32, axis=1, keepdims=True) + EPS)
        gain = jnp.where((mod == 1)[:, None], norm_gain[1][None, :], norm_gain[0][None, :])
        normed = (values32 * factor * gain).astype(jnp.bfloat16)
        first = [0] + [place[1] * rows] * (n - 1)
        count = [length] + [rows] * (n - 1)
        return [
            lax.dynamic_slice(normed, (first[d], (place[0] ^ d) * width), (count[d], width))
            for d in range(n)
        ]
    shapes = [jax.ShapeDtypeStruct((length, width), jnp.bfloat16)]
    shapes += [jax.ShapeDtypeStruct((rows, width), jnp.bfloat16)] * (n - 1)
    return pl.pallas_call(
        norm_kernel,
        out_shape=shapes,
        in_specs=[SMEM, SMEM, HBM, VMEM],
        out_specs=[VMEM] * n,
        scratch_shapes=[
            pltpu.VMEM((length, depth), jnp.bfloat16),
            pltpu.SemaphoreType.DMA((length // RUN,)),
        ],
        cost_estimate=pl.CostEstimate(
            flops=6 * length * depth, bytes_accessed=4 * length * depth, transcendentals=length
        ),
        compiler_params=pltpu.CompilerParams(vmem_limit_bytes=12 * 1024 * 1024),
        name="norm",
    )(place, modality, in_hbm(tokens), norm_gain)


def partial_kernel(counts, narrow, place, modality, begins, *rest):
    total = sum(counts)
    sources, refs, outs = rest[:6], rest[6 : 6 + total], rest[6 + total : -8]
    both, other, held_kv, held_q, wide_kv, wide_q, arrived, left = rest[-8:]
    length = both.shape[0] // len(counts)
    half = length // 2
    kv_half = held_kv.shape[2] // 2
    depth = held_kv.shape[1] // 2
    copies = []

    def fetch(source, target):
        copies.append(pltpu.make_async_copy(source, target, arrived.at[len(copies)]))
        copies[-1].start()

    at = 0
    for number, count in enumerate(counts):
        base = number * length
        if count == 1:
            fetch(refs[at], both.at[base : base + length])
        else:
            for which in range(2):
                row = base + (place[1] if which == 0 else 1 - place[1]) * half
                fetch(refs[at + which], both.at[pl.ds(pl.multiple_of(row, half), half)])
        at += count
    for i, source in enumerate(sources):
        core = place[3] if i % 2 == 0 else 1 - place[3]
        rows = pl.ds(pl.multiple_of(core * depth, depth), depth)
        target = (
            held_kv.at[:, rows, 0:kv_half],
            held_kv.at[:, rows, kv_half : 2 * kv_half],
            held_q.at[:, rows],
        )[i // 2]
        fetch(source, target)
    for copy in copies[:total]:
        copy.wait()
    for number in range(len(counts)):
        for step in range(0, length, RUN):
            rows = pl.ds(number * length + step, RUN)
            generate = modality[begins[number] + step] == 1
            block = both[rows]
            zero = jnp.zeros_like(block)
            both[rows] = jnp.where(generate, zero, block)
            other[rows] = jnp.where(generate, block, zero)
    first, second = both[...], other[...]
    pieces = wide_q.shape[0]
    width = wide_q.shape[2]
    stores = []

    def project(held, cols, wide, out):
        value = jnp.dot(first, held[0, :, cols], preferred_element_type=jnp.float32) + jnp.dot(
            second, held[1, :, cols], preferred_element_type=jnp.float32
        )
        wide[...] = value
        stores.append(pltpu.make_async_copy(wide, out, left.at[len(stores)]))
        stores[-1].start()
        return value.astype(jnp.bfloat16)

    for copy in copies[total : total + 4]:
        copy.wait()
    value = project(held_kv, slice(None), wide_kv, outs[0])
    if narrow:
        outs[2][...] = value
    for copy in copies[total + 4 :]:
        copy.wait()
    for piece in range(pieces):
        cols = slice(piece * width, (piece + 1) * width)
        value = project(held_q, cols, wide_q.at[piece], outs[1].at[:, cols])
        if narrow:
            for number in range(len(counts)):
                outs[3 + number][:, cols] = value[number * length : (number + 1) * length]
    for store in stores:
        store.wait()


def partial(blocks, begins, length, modality, weights, place, narrow):
    counts = tuple(len(block) for block in blocks)
    places = [pair for block in blocks for pair in enumerate(block)]
    arrays = [array for _, array in places]
    rows, width = length * len(blocks), arrays[0].shape[1]
    pieces = 2 if weights[4].shape[2] % 256 == 0 else 1
    kv_cols, q_cols = 2 * weights[0].shape[2], weights[4].shape[2]
    shapes = [pltpu.HBM((rows, cols), jnp.float32) for cols in (kv_cols, q_cols)]
    if narrow:
        shapes.append(jax.ShapeDtypeStruct((rows, kv_cols), jnp.bfloat16))
        shapes += [jax.ShapeDtypeStruct((length, q_cols), jnp.bfloat16)] * len(blocks)
    values = pl.pallas_call(
        functools.partial(partial_kernel, counts, narrow),
        out_shape=shapes,
        in_specs=[SMEM] * 3 + [HBM] * len(weights) + [VMEM if i else HBM for i, _ in places],
        out_specs=[HBM] * 2 + [VMEM] * (len(shapes) - 2),
        scratch_shapes=[
            pltpu.VMEM((rows, width), jnp.bfloat16),
            pltpu.VMEM((rows, width), jnp.bfloat16),
            pltpu.VMEM((2, width, kv_cols), jnp.bfloat16),
            pltpu.VMEM((2, width, q_cols), jnp.bfloat16),
            pltpu.VMEM((rows, kv_cols), jnp.float32),
            pltpu.VMEM((pieces, rows, q_cols // pieces), jnp.float32),
            pltpu.SemaphoreType.DMA((len(weights) + len(arrays),)),
            pltpu.SemaphoreType.DMA((1 + pieces,)),
        ],
        cost_estimate=pl.CostEstimate(
            flops=4 * rows * width * (kv_cols + q_cols),
            bytes_accessed=4 * (width + rows) * (kv_cols + q_cols),
            transcendentals=0,
        ),
        compiler_params=pltpu.CompilerParams(vmem_limit_bytes=24 * 1024 * 1024),
        name="partial",
    )(
        place,
        modality,
        begins,
        *[in_hbm(w) for w in weights],
        *[a if i else in_hbm(a) for i, a in places],
    )
    return [value.reshape(len(blocks), length, -1) for value in values[:3]] + list(values[3:])


def halving(parts):
    n = len(parts)
    sums = dict(enumerate(parts))
    for bit in [1 << i for i in range(n.bit_length() - 1)]:
        for d in [d for d in range(n) if d in sums and d & bit]:
            sums[d ^ bit] = sums[d ^ bit] + cross(sums.pop(d).astype(jnp.bfloat16), "seq", bit)
    return sums[0].astype(jnp.bfloat16)


def along_four(parts, three, two, whole):
    wide = [p.astype(jnp.float32) for p in parts]

    def hop(value, bit, among):
        return cross(value, "seq", bit, among)

    def plus(a, b):
        return (a + b.astype(jnp.float32)).astype(jnp.bfloat16)

    if two is None:
        got = hop(three, 1, (1, 2))
        got = hop(plus(jnp.stack([wide[2], wide[3]]), got), 3, (1, 2))
        across, own = got[0], got[1]
    else:
        far = hop(three, 1, (1, 2))
        close = hop(two, 1, (1, 2))
        send = plus(wide[2], far)
        across = hop(send, 3, (1, 2))
        own = hop(plus(wide[3], after(close, send)), 3, (1, 2))
    last = hop(plus(wide[1], across), 1, None)
    if not whole:
        return last, own
    return (wide[0] + last.astype(jnp.float32) + own.astype(jnp.float32)).astype(jnp.bfloat16)


def gather_weights(mine):
    n = lax.axis_size("seq")
    if n == 4:
        z = lax.axis_index("seq")
        inner = (z == 1) | (z == 2)
        one = cross(mine, "seq", 1)
        middle = cross(mine, "seq", 3, (1, 2))
        middle_two = cross(one, "seq", 3, (1, 2))
        outer_two = cross(middle, "seq", 1, (0, 3))
        outer_three = cross(middle_two, "seq", 1, (0, 3))
        near = [mine, one, jnp.where(inner, middle_two, outer_two), jnp.where(inner, middle, outer_three)]
    else:
        near = [mine]
        for bit in reversed([1 << i for i in range(n.bit_length() - 1)]):
            got = cross(jnp.stack(near), "seq", bit)
            near = near + [got[i] for i in range(len(near))]
        order = [0]
        for bit in reversed([1 << i for i in range(n.bit_length() - 1)]):
            order = order + [d ^ bit for d in order]
        near = [near[order.index(d)] for d in range(n)]
    far = []
    for d in range(1, n):
        far.append(swap(near[d], "grp"))
    return near[1:], far


def spans(modality, doc_ids, own_mod, own_doc, own_pos):
    changed = (modality[1:] != modality[:-1]) | (doc_ids[1:] != doc_ids[:-1])
    begins = jnp.concatenate([jnp.ones((1,), jnp.int32), changed.astype(jnp.int32)])
    blocks = jnp.cumsum(begins)
    own_block = lax.dynamic_slice_in_dim(blocks, own_pos[0], own_pos.shape[0])
    low = jnp.sum((doc_ids[None, :] < own_doc[:, None]).astype(jnp.int32), axis=1)
    end = jnp.sum((blocks[None, :] <= own_block[:, None]).astype(jnp.int32), axis=1) - 1
    return low, jnp.where(own_mod == 1, end, own_pos)


def attention_kernel(terms, starts, limits, span_ref, *rest):
    q_refs, sources = rest[:terms], rest[terms:-8]
    (o_ref, kv_ref, queries, bounds, top, total, acc, arrived) = rest[-8:]
    count, size, _ = kv_ref.shape
    for number, source in enumerate(sources):
        pltpu.make_async_copy(source, kv_ref.at[number], arrived.at[number]).start()
    rows = o_ref.shape[0]
    kv_local, many = queries.shape[0], queries.shape[1]
    repeat = many // rows
    scale = math.log2(math.e) / math.sqrt(HEAD_DIM)
    top[...] = jnp.full_like(top, LOW / 10)
    total[...] = jnp.zeros_like(total)
    acc[...] = jnp.zeros_like(acc)
    for head in range(kv_local * repeat):
        g, r = head // repeat, head % repeat
        cols = slice(head * HEAD_DIM, (head + 1) * HEAD_DIM)
        query = q_refs[0][0, :, cols].astype(jnp.float32)
        for term in q_refs[1:]:
            query = query + term[:, cols].astype(jnp.float32)
        queries[g, r * rows : (r + 1) * rows] = query.astype(jnp.bfloat16)
    columns = span_ref[...].T
    for r in range(repeat):
        bounds[r * rows : (r + 1) * rows] = columns
    transposed = (((1,), (1,)), ((), ()))

    def visit(number, _):
        start = starts[number]
        last = start + size - 1
        pltpu.make_async_copy(sources[0], kv_ref.at[number], arrived.at[number]).wait()

        def block(masked):
            for g in range(kv_local):
                keys = kv_ref[number, :, g * HEAD_DIM : (g + 1) * HEAD_DIM]
                values = kv_ref[number, :, (kv_local + g) * HEAD_DIM : (kv_local + g + 1) * HEAD_DIM]
                scores = lax.dot_general(
                    queries[g], keys, transposed, preferred_element_type=jnp.float32
                )
                if masked:
                    key_pos = start + lax.broadcasted_iota(jnp.int32, (many, size), 1)
                    seen = (key_pos >= bounds[:, 0:1]) & (key_pos <= bounds[:, 1:2])
                    scores = jnp.where(seen, scores, LOW)
                old = top[g]
                new = jnp.maximum(old, jnp.max(scores, axis=1, keepdims=True))
                weights = jnp.exp2((scores - jnp.tile(new, (1, size // 128))) * scale)
                shrink = jnp.exp2((old - new) * scale)
                total[g] = total[g] * shrink + jnp.sum(weights, axis=1, keepdims=True)
                top[g] = new
                acc[g] = acc[g] * shrink + jnp.dot(
                    weights.astype(jnp.bfloat16), values, preferred_element_type=jnp.float32
                )

        inside = (start >= limits[2]) & (last <= limits[3])

        @pl.when(inside)
        def _():
            block(False)

        @pl.when(jnp.logical_not(inside) & (start <= limits[1]) & (last >= limits[0]))
        def _():
            block(True)

        return 0

    lax.fori_loop(0, count, visit, 0)
    for head in range(kv_local * repeat):
        g, at = head // repeat, pl.ds((head % repeat) * rows, rows)
        o_ref[:, head * HEAD_DIM : (head + 1) * HEAD_DIM] = (acc[g, at] / total[g, at]).astype(
            jnp.bfloat16
        )


def attend(query, kv, starts, limits, span):
    rows, width = query[0].shape[1:]
    heads = width // HEAD_DIM
    count, (size, kv_cols) = len(kv), kv[0].shape
    kv_local = kv_cols // (2 * HEAD_DIM)
    many = rows * heads // kv_local
    return pl.pallas_call(
        functools.partial(attention_kernel, len(query)),
        out_shape=jax.ShapeDtypeStruct((rows, width), jnp.bfloat16),
        in_specs=[SMEM, SMEM, VMEM] + [VMEM] * len(query) + [HBM] * (count // 2 + 1) + [VMEM] * (count // 2 - 1),
        out_specs=VMEM,
        scratch_shapes=[
            pltpu.VMEM((count, size, kv_cols), jnp.bfloat16),
            pltpu.VMEM((kv_local, many, HEAD_DIM), jnp.bfloat16),
            pltpu.VMEM((many, 8), jnp.int32),
            pltpu.VMEM((kv_local, many, HEAD_DIM), jnp.float32),
            pltpu.VMEM((kv_local, many, HEAD_DIM), jnp.float32),
            pltpu.VMEM((kv_local, many, HEAD_DIM), jnp.float32),
            pltpu.SemaphoreType.DMA((count,)),
        ],
        cost_estimate=pl.CostEstimate(
            flops=4 * rows * count * size * width,
            bytes_accessed=2 * (2 * rows * width + count * size * kv_cols),
            transcendentals=rows * count * size * heads,
        ),
        compiler_params=pltpu.CompilerParams(vmem_limit_bytes=20 * 1024 * 1024),
        name="attend",
    )(
        starts,
        limits,
        span,
        *query,
        *[in_hbm(block) for block in kv[: count // 2 + 1]],
        *kv[count // 2 + 1 :],
    )


def project_kernel(n, groups, turns, place, *rest):
    inputs, own_ref, near, far = (
        rest[: 2 * groups],
        rest[2 * groups],
        rest[2 * groups + 1 : 2 * groups + n],
        rest[2 * groups + n : 2 * groups + 2 * n - 1],
    )
    outs, (held, lhs, arrived) = rest[2 * groups + 2 * n - 1 : -3], rest[-3:]
    count = turns.shape[0]
    first = place[2]

    def fetch(i, d):
        @pl.when(turns[i] == d)
        def _():
            sources = (near[d - 1], far[d - 1]) if d else (own_ref.at[first], own_ref.at[1 - first])
            for kind, source in enumerate(sources):
                pltpu.make_async_copy(source, held.at[kind, i], arrived.at[kind, i]).start()

    for i in range(count):
        for d in range(n):
            fetch(i, d)

    rows = inputs[0].shape[0]
    for group in range(groups):
        a = inputs[2 * group][...]
        mine = inputs[2 * group + 1][...] != 0
        zero = jnp.zeros_like(a)
        lhs[0, group * rows : (group + 1) * rows] = jnp.where(mine, a, zero)
        lhs[1, group * rows : (group + 1) * rows] = jnp.where(mine, zero, a)
    contract = (((1,), (1,)), ((), ()))
    for i in range(count):
        value = None
        for kind in range(2):
            pltpu.make_async_copy(own_ref.at[0], held.at[kind, i], arrived.at[kind, i]).wait()
            term = lax.dot_general(
                lhs[kind], held[kind, i], contract, preferred_element_type=jnp.float32
            )
            value = term if value is None else value + term
        value = value.astype(jnp.bfloat16)
        for group in range(groups):
            outs[group][i] = value[group * rows : (group + 1) * rows]


def project(tokens, weights, turns, place):
    rows, depth = tokens[0][0].shape
    groups, count = len(tokens), turns.shape[0]
    width = weights[0].shape[1]
    return pl.pallas_call(
        functools.partial(project_kernel, (len(weights) + 1) // 2, groups),
        out_shape=[jax.ShapeDtypeStruct((count, rows, width), jnp.bfloat16)] * groups,
        in_specs=[SMEM, SMEM] + [VMEM] * (2 * groups) + [HBM] * len(weights),
        out_specs=[VMEM] * groups,
        scratch_shapes=[
            pltpu.VMEM((2, count, width, depth), jnp.bfloat16),
            pltpu.VMEM((2, groups * rows, depth), jnp.bfloat16),
            pltpu.SemaphoreType.DMA((2, count)),
        ],
        cost_estimate=pl.CostEstimate(
            flops=4 * groups * count * rows * depth * width,
            bytes_accessed=4 * count * depth * width + 2 * groups * count * rows * width,
            transcendentals=0,
        ),
        compiler_params=pltpu.CompilerParams(vmem_limit_bytes=16 * 1024 * 1024),
        name="project",
    )(turns, place, *[a for pair in tokens for a in (pair[0], pair[1][:, None])], *weights)


def body(tokens, norm_gain, w_query, w_key, w_value, w_out, modality, doc_ids):
    length, _ = tokens.shape
    n = lax.axis_size("seq")
    subs = lax.axis_size("sub")
    heads_over = lax.axis_size("head")
    z, s = lax.axis_index("seq"), lax.axis_index("sub")
    x, y = lax.axis_index("head"), lax.axis_index("grp")
    place = jnp.stack([z, x, y, s, (z * subs + s) * length]).astype(jnp.int32)

    kv_local = max(KV_HEADS // heads_over, 1)
    kv_first = x * KV_HEADS // heads_over
    w_out = jnp.swapaxes(w_out, 1, 2)

    def part_of(array, place, core):
        return lax.dynamic_slice_in_dim(array, (place * subs + core) * length, length)

    mine = lax.dynamic_index_in_dim(w_out, y, 0, keepdims=False)
    near, far = gather_weights(mine)
    weights = [w_out] + near + far

    own_mod = part_of(modality, z, s)
    share_rows = heads_over == 2
    rows = length // 2 if share_rows else length
    sends = norm_columns(tokens, norm_gain, modality, own_mod, place, n, rows)
    blocks = {0: (sends[0],)}
    for d in range(n - 1, 0, -1):
        blocks[d] = (cross(sends[d], "seq", d),)

    w_query, w_key, w_value = after((w_query, w_key, w_value), sends[0])

    key_cols = lax.dynamic_slice_in_dim(w_key, kv_first * HEAD_DIM, kv_local * HEAD_DIM, 2)
    value_cols = lax.dynamic_slice_in_dim(w_value, kv_first * HEAD_DIM, kv_local * HEAD_DIM, 2)
    row_weights = []
    for weight in (key_cols, value_cols, w_query):
        row_weights += [weight, swap(weight, "sub")]
    modality, doc_ids = after((modality, doc_ids), sends[0])
    own_doc = part_of(doc_ids, z, s)
    own_pos = (z * subs + s) * length + jnp.arange(length, dtype=jnp.int32)
    low, high = spans(modality, doc_ids, part_of(modality, z, s), own_doc, own_pos)
    span = jnp.concatenate([low[None], high[None], jnp.zeros((6, length), jnp.int32)])
    limits = jnp.stack([low[0], high[-1], low[-1], high[0]])

    if share_rows:
        for d in range(n - 1, 0, -1):
            blocks[d] = (*blocks[d], swap(blocks[d][0], "head"))
    blocks[n - 1] = after(blocks[n - 1], span, limits)

    def parts_of(group, narrow):
        begins = jnp.stack([((z ^ d) * subs + s) * length for d in group]).astype(jnp.int32)
        arrays = [blocks[d] for d in group]
        return partial(arrays, begins, length, modality, row_weights, place, narrow)

    if n == 4:
        kv_early, q_early, kv_ends, q_three, q_two = parts_of([3, 2], True)
        kv_late, q_late = parts_of([1, 0], False)
        kv_early, q_early = after((kv_early, q_early), kv_late, q_late)
        kv = along_four([kv_late[1], kv_late[0], kv_early[1], kv_early[0]], kv_ends, None, True)
        parts = [q_late[1], q_late[0], q_early[1], q_early[0]]
        query = (q_late[1:], *along_four(parts, q_three, q_two, False))
    else:
        kv_parts, q_parts = [], []
        for d in range(n):
            kv_part, q_part = parts_of([d], False)
            kv_parts.append(kv_part[0])
            q_parts.append(q_part[0])
        kv, query = halving(kv_parts), (halving(q_parts)[None],)

    same = [kv]
    for d in range(1, n):
        same.append(cross(kv, "seq", d))
    beside = []
    for d in range(n):
        beside.append(swap(same[d], "sub"))
    starts = jnp.stack(
        [((z ^ d) * subs + s) * length for d in range(n)]
        + [((z ^ d) * subs + (1 - s)) * length for d in range(n)]
    ).astype(jnp.int32)
    attended = attend(query, same + beside, starts, limits, span)

    beside = swap(attended, "sub")
    ours_near = (own_mod == y).astype(jnp.bfloat16)
    beside_near = (part_of(modality, z, 1 - s) == y).astype(jnp.bfloat16)

    our_rows, beside_rows = (attended, ours_near), (beside, beside_near)

    def out(tokens, columns):
        return project(tokens, weights, (columns ^ z).astype(jnp.int32), place)

    if heads_over != 2:
        ours, theirs = out([our_rows, beside_rows], jnp.arange(n))
        sibling = swap(theirs, "sub")
        pair = jnp.where(s == 0, jnp.stack([ours, sibling], 1), jnp.stack([sibling, ours], 1))
        wide = jnp.transpose(pair, (2, 0, 1, 3)).reshape(length, -1)
        return lax.psum_scatter(wide, "head", scatter_dimension=1, tiled=True)

    half = n // 2
    ours, theirs = [], []

    def piece(tokens, i):
        return out([tokens], (1 - x) * half + jnp.arange(i, i + 1))[0]

    for i in range(half):
        sent = piece(our_rows, i)
        ours.append(swap(sent, "head"))
    for i in range(half):
        sent = piece(beside_rows, i)
        theirs.append(swap(sent, "head"))
    keep_ours, keep_beside = out([our_rows, beside_rows], x * half + jnp.arange(half))
    done = add(keep_beside, jnp.concatenate(theirs))
    sibling = swap(done, "sub")
    return finish(place, keep_ours, ours, sibling)


def finish_kernel(place, keep_ref, *rest):
    got_refs, sibling_ref, o_ref = rest[:-2], rest[-2], rest[-1]
    width = keep_ref.shape[2]

    def fill(core):
        for i, got_ref in enumerate(got_refs):
            own = keep_ref[i].astype(jnp.float32) + got_ref[0].astype(jnp.float32)
            for piece, slot in ((own.astype(jnp.bfloat16), core), (sibling_ref[i], 1 - core)):
                at = (2 * i + slot) * width
                o_ref[:, at : at + width] = piece

    for core in range(2):

        @pl.when(place[3] == core)
        def _():
            fill(core)


def finish(place, keep, got, sibling):
    count, rows, width = keep.shape
    return pl.pallas_call(
        finish_kernel,
        out_shape=jax.ShapeDtypeStruct((rows, 2 * count * width), jnp.bfloat16),
        in_specs=[SMEM] + [VMEM] * (2 + len(got)),
        out_specs=VMEM,
        cost_estimate=pl.CostEstimate(
            flops=count * rows * width, bytes_accessed=12 * count * rows * width, transcendentals=0
        ),
        compiler_params=pltpu.CompilerParams(vmem_limit_bytes=12 * 1024 * 1024),
        name="finish",
    )(place, keep, *got, sibling)


def solution(mesh):
    placed = (
        P(("grp", "seq", "sub"), None),
        P(),
        P(None, ("seq", "sub"), "head"),
        P(None, ("seq", "sub"), None),
        P(None, ("seq", "sub"), None),
        P(None, "head", ("seq", "sub")),
        P("grp"),
        P("grp"),
    )
    return jax.shard_map(
        body,
        mesh=mesh,
        in_specs=placed,
        out_specs=P(("grp", "seq", "sub"), "head"),
        check_vma=False,
    )
```

```python
import functools
import math

import jax
import jax.numpy as jnp
from jax import lax
from jax.experimental import pallas as pl
from jax.experimental.pallas import tpu as pltpu
from jax.sharding import PartitionSpec as P


HEAD_DIM = 128
KV_HEADS = 4
RUN = 64
EPS = 1e-06
LOW = -1e30


def swap(x, axis):
    return lax.ppermute(x, axis, [(0, 1), (1, 0)])


def cross(x, axis, bit, among=None):
    size = lax.axis_size(axis)
    return lax.ppermute(x, axis, [(i ^ bit, i) for i in (among or range(size))])


def after(value, *done):
    return lax.optimization_barrier((value, *done))[0]


def add(a, b):
    return (a.astype(jnp.float32) + b.astype(jnp.float32)).astype(jnp.bfloat16)


VMEM = pl.BlockSpec(memory_space=pltpu.VMEM)
SMEM = pl.BlockSpec(memory_space=pltpu.SMEM)
HBM = pl.BlockSpec(memory_space=pltpu.HBM)


def in_hbm(x):
    return pltpu.with_memory_space_constraint(x, pltpu.HBM)


def norm_kernel(place, modality, tokens_ref, gain_ref, own_ref, *rest):
    send_refs, (scratch, arrived) = rest[:-2], rest[-2:]
    width = own_ref.shape[1]
    copies = []
    for i, at in enumerate(range(0, tokens_ref.shape[0], RUN)):
        rows = pl.ds(at, RUN)
        copies.append(pltpu.make_async_copy(tokens_ref.at[rows], scratch.at[rows], arrived.at[i]))
        copies[-1].start()
    for i, at in enumerate(range(0, tokens_ref.shape[0], RUN)):
        copies[i].wait()
        values = scratch[at : at + RUN].astype(jnp.float32)
        factor = lax.rsqrt(jnp.mean(values * values, axis=1, keepdims=True) + EPS)
        gain = jnp.where(modality[place[4] + at] == 1, gain_ref[1:2, :], gain_ref[0:1, :])
        scratch[at : at + RUN] = (values * factor * gain).astype(jnp.bfloat16)

    def columns(d):
        return pl.ds(pl.multiple_of((place[0] ^ d) * width, width), width)

    own_ref[...] = scratch[:, columns(0)]
    for d, ref in enumerate(send_refs, 1):
        rows = ref.shape[0]
        ref[...] = scratch[pl.ds(pl.multiple_of(place[1] * rows, rows), rows), columns(d)]


def norm_columns(tokens, norm_gain, modality, mod, place, n, rows):
    length, depth = tokens.shape
    width = depth // n
    if width % 128:
        values32 = tokens.astype(jnp.float32)
        factor = lax.rsqrt(jnp.mean(values32 * values32, axis=1, keepdims=True) + EPS)
        gain = jnp.where((mod == 1)[:, None], norm_gain[1][None, :], norm_gain[0][None, :])
        normed = (values32 * factor * gain).astype(jnp.bfloat16)
        first = [0] + [place[1] * rows] * (n - 1)
        count = [length] + [rows] * (n - 1)
        return [
            lax.dynamic_slice(normed, (first[d], (place[0] ^ d) * width), (count[d], width))
            for d in range(n)
        ]
    shapes = [jax.ShapeDtypeStruct((length, width), jnp.bfloat16)]
    shapes += [jax.ShapeDtypeStruct((rows, width), jnp.bfloat16)] * (n - 1)
    return pl.pallas_call(
        norm_kernel,
        out_shape=shapes,
        in_specs=[SMEM, SMEM, HBM, VMEM],
        out_specs=[VMEM] * n,
        scratch_shapes=[
            pltpu.VMEM((length, depth), jnp.bfloat16),
            pltpu.SemaphoreType.DMA((length // RUN,)),
        ],
        cost_estimate=pl.CostEstimate(
            flops=6 * length * depth, bytes_accessed=4 * length * depth, transcendentals=length
        ),
        compiler_params=pltpu.CompilerParams(vmem_limit_bytes=12 * 1024 * 1024),
        name="norm",
    )(place, modality, in_hbm(tokens), norm_gain)


def partial_kernel(counts, narrow, place, modality, begins, *rest):
    total = sum(counts)
    sources, refs, outs = rest[:6], rest[6 : 6 + total], rest[6 + total : -8]
    both, other, held_kv, held_q, wide_kv, wide_q, arrived, left = rest[-8:]
    length = both.shape[0] // len(counts)
    half = length // 2
    kv_half = held_kv.shape[2] // 2
    depth = held_kv.shape[1] // 2
    copies = []

    def fetch(source, target):
        copies.append(pltpu.make_async_copy(source, target, arrived.at[len(copies)]))
        copies[-1].start()

    at = 0
    for number, count in enumerate(counts):
        base = number * length
        if count == 1:
            fetch(refs[at], both.at[base : base + length])
        else:
            for which in range(2):
                row = base + (place[1] if which == 0 else 1 - place[1]) * half
                fetch(refs[at + which], both.at[pl.ds(pl.multiple_of(row, half), half)])
        at += count
    for i, source in enumerate(sources):
        core = place[3] if i % 2 == 0 else 1 - place[3]
        rows = pl.ds(pl.multiple_of(core * depth, depth), depth)
        target = (
            held_kv.at[:, rows, 0:kv_half],
            held_kv.at[:, rows, kv_half : 2 * kv_half],
            held_q.at[:, rows],
        )[i // 2]
        fetch(source, target)
    for copy in copies[:total]:
        copy.wait()
    for number in range(len(counts)):
        for step in range(0, length, RUN):
            rows = pl.ds(number * length + step, RUN)
            generate = modality[begins[number] + step] == 1
            block = both[rows]
            zero = jnp.zeros_like(block)
            both[rows] = jnp.where(generate, zero, block)
            other[rows] = jnp.where(generate, block, zero)
    first, second = both[...], other[...]
    pieces = wide_q.shape[0]
    width = wide_q.shape[2]
    stores = []

    def project(held, cols, wide, out):
        value = jnp.dot(first, held[0, :, cols], preferred_element_type=jnp.float32) + jnp.dot(
            second, held[1, :, cols], preferred_element_type=jnp.float32
        )
        wide[...] = value
        stores.append(pltpu.make_async_copy(wide, out, left.at[len(stores)]))
        stores[-1].start()
        return value.astype(jnp.bfloat16)

    for copy in copies[total : total + 4]:
        copy.wait()
    value = project(held_kv, slice(None), wide_kv, outs[0])
    if narrow:
        outs[2][...] = value
    for copy in copies[total + 4 :]:
        copy.wait()
    for piece in range(pieces):
        cols = slice(piece * width, (piece + 1) * width)
        value = project(held_q, cols, wide_q.at[piece], outs[1].at[:, cols])
        if narrow:
            for number in range(len(counts)):
                outs[3 + number][:, cols] = value[number * length : (number + 1) * length]
    for store in stores:
        store.wait()


def partial(blocks, begins, length, modality, weights, place, narrow):
    counts = tuple(len(block) for block in blocks)
    places = [pair for block in blocks for pair in enumerate(block)]
    arrays = [array for _, array in places]
    rows, width = length * len(blocks), arrays[0].shape[1]
    pieces = 2 if weights[4].shape[2] % 256 == 0 else 1
    kv_cols, q_cols = 2 * weights[0].shape[2], weights[4].shape[2]
    shapes = [pltpu.HBM((rows, cols), jnp.float32) for cols in (kv_cols, q_cols)]
    if narrow:
        shapes.append(jax.ShapeDtypeStruct((rows, kv_cols), jnp.bfloat16))
        shapes += [jax.ShapeDtypeStruct((length, q_cols), jnp.bfloat16)] * len(blocks)
    values = pl.pallas_call(
        functools.partial(partial_kernel, counts, narrow),
        out_shape=shapes,
        in_specs=[SMEM] * 3 + [HBM] * len(weights) + [VMEM if i else HBM for i, _ in places],
        out_specs=[HBM] * 2 + [VMEM] * (len(shapes) - 2),
        scratch_shapes=[
            pltpu.VMEM((rows, width), jnp.bfloat16),
            pltpu.VMEM((rows, width), jnp.bfloat16),
            pltpu.VMEM((2, width, kv_cols), jnp.bfloat16),
            pltpu.VMEM((2, width, q_cols), jnp.bfloat16),
            pltpu.VMEM((rows, kv_cols), jnp.float32),
            pltpu.VMEM((pieces, rows, q_cols // pieces), jnp.float32),
            pltpu.SemaphoreType.DMA((len(weights) + len(arrays),)),
            pltpu.SemaphoreType.DMA((1 + pieces,)),
        ],
        cost_estimate=pl.CostEstimate(
            flops=4 * rows * width * (kv_cols + q_cols),
            bytes_accessed=4 * (width + rows) * (kv_cols + q_cols),
            transcendentals=0,
        ),
        compiler_params=pltpu.CompilerParams(vmem_limit_bytes=24 * 1024 * 1024),
        name="partial",
    )(
        place,
        modality,
        begins,
        *[in_hbm(w) for w in weights],
        *[a if i else in_hbm(a) for i, a in places],
    )
    return [value.reshape(len(blocks), length, -1) for value in values[:3]] + list(values[3:])


def halving(parts):
    n = len(parts)
    sums = dict(enumerate(parts))
    for bit in [1 << i for i in range(n.bit_length() - 1)]:
        for d in [d for d in range(n) if d in sums and d & bit]:
            sums[d ^ bit] = sums[d ^ bit] + cross(sums.pop(d).astype(jnp.bfloat16), "seq", bit)
    return sums[0].astype(jnp.bfloat16)


def along_four(parts, three, two, whole):
    wide = [p.astype(jnp.float32) for p in parts]

    def hop(value, bit, among):
        return cross(value, "seq", bit, among)

    def plus(a, b):
        return (a + b.astype(jnp.float32)).astype(jnp.bfloat16)

    if two is None:
        got = hop(three, 1, (1, 2))
        got = hop(plus(jnp.stack([wide[2], wide[3]]), got), 3, (1, 2))
        across, own = got[0], got[1]
    else:
        far = hop(three, 1, (1, 2))
        close = hop(two, 1, (1, 2))
        send = plus(wide[2], far)
        across = hop(send, 3, (1, 2))
        own = hop(plus(wide[3], after(close, send)), 3, (1, 2))
    last = hop(plus(wide[1], across), 1, None)
    if not whole:
        return last, own
    return (wide[0] + last.astype(jnp.float32) + own.astype(jnp.float32)).astype(jnp.bfloat16)


def gather_weights(mine):
    n = lax.axis_size("seq")
    if n == 4:
        z = lax.axis_index("seq")
        inner = (z == 1) | (z == 2)
        one = cross(mine, "seq", 1)
        middle = cross(mine, "seq", 3, (1, 2))
        middle_two = cross(one, "seq", 3, (1, 2))
        outer_two = cross(middle, "seq", 1, (0, 3))
        outer_three = cross(middle_two, "seq", 1, (0, 3))
        near = [mine, one, jnp.where(inner, middle_two, outer_two), jnp.where(inner, middle, outer_three)]
    else:
        near = [mine]
        for bit in reversed([1 << i for i in range(n.bit_length() - 1)]):
            got = cross(jnp.stack(near), "seq", bit)
            near = near + [got[i] for i in range(len(near))]
        order = [0]
        for bit in reversed([1 << i for i in range(n.bit_length() - 1)]):
            order = order + [d ^ bit for d in order]
        near = [near[order.index(d)] for d in range(n)]
    far = []
    for d in range(1, n):
        far.append(swap(near[d], "grp"))
    return near[1:], far


def spans(modality, doc_ids, own_mod, own_doc, own_pos):
    changed = (modality[1:] != modality[:-1]) | (doc_ids[1:] != doc_ids[:-1])
    begins = jnp.concatenate([jnp.ones((1,), jnp.int32), changed.astype(jnp.int32)])
    blocks = jnp.cumsum(begins)
    own_block = lax.dynamic_slice_in_dim(blocks, own_pos[0], own_pos.shape[0])
    low = jnp.sum((doc_ids[None, :] < own_doc[:, None]).astype(jnp.int32), axis=1)
    end = jnp.sum((blocks[None, :] <= own_block[:, None]).astype(jnp.int32), axis=1) - 1
    return low, jnp.where(own_mod == 1, end, own_pos)


def attention_kernel(terms, starts, limits, span_ref, *rest):
    inner = len(rest) - 9 - terms
    q_sources, sources, q_refs = rest[:terms], rest[terms:inner], rest[inner + 1 : inner + 1 + terms]
    o_ref = rest[inner]
    kv_ref, queries, bounds, top, total, acc, arrived, landed = rest[-8:]
    count, size, _ = kv_ref.shape
    landing = []
    for i, (source, held) in enumerate(zip(q_sources, q_refs)):
        source = source if i else source.at[source.shape[0] - 1]
        landing.append(pltpu.make_async_copy(source, held, landed.at[i]))
        landing[-1].start()
    for number, source in enumerate(sources):
        pltpu.make_async_copy(source, kv_ref.at[number], arrived.at[number]).start()
    rows = o_ref.shape[0]
    kv_local, many = queries.shape[0], queries.shape[1]
    repeat = many // rows
    scale = math.log2(math.e) / math.sqrt(HEAD_DIM)
    top[...] = jnp.full_like(top, LOW / 10)
    total[...] = jnp.zeros_like(total)
    acc[...] = jnp.zeros_like(acc)
    columns = span_ref[...].T
    for r in range(repeat):
        bounds[r * rows : (r + 1) * rows] = columns
    for copy in landing:
        copy.wait()
    for head in range(kv_local * repeat):
        g, r = head // repeat, head % repeat
        cols = slice(head * HEAD_DIM, (head + 1) * HEAD_DIM)
        query = q_refs[0][:, cols].astype(jnp.float32)
        for term in q_refs[1:]:
            query = query + term[:, cols].astype(jnp.float32)
        queries[g, r * rows : (r + 1) * rows] = query.astype(jnp.bfloat16)
    transposed = (((1,), (1,)), ((), ()))

    def visit(number, _):
        start = starts[number]
        last = start + size - 1
        pltpu.make_async_copy(sources[0], kv_ref.at[number], arrived.at[number]).wait()

        def block(masked):
            for g in range(kv_local):
                keys = kv_ref[number, :, g * HEAD_DIM : (g + 1) * HEAD_DIM]
                values = kv_ref[number, :, (kv_local + g) * HEAD_DIM : (kv_local + g + 1) * HEAD_DIM]
                scores = lax.dot_general(
                    queries[g], keys, transposed, preferred_element_type=jnp.float32
                )
                if masked:
                    key_pos = start + lax.broadcasted_iota(jnp.int32, (many, size), 1)
                    seen = (key_pos >= bounds[:, 0:1]) & (key_pos <= bounds[:, 1:2])
                    scores = jnp.where(seen, scores, LOW)
                old = top[g]
                new = jnp.maximum(old, jnp.max(scores, axis=1, keepdims=True))
                weights = jnp.exp2((scores - jnp.tile(new, (1, size // 128))) * scale)
                shrink = jnp.exp2((old - new) * scale)
                total[g] = total[g] * shrink + jnp.sum(weights, axis=1, keepdims=True)
                top[g] = new
                acc[g] = acc[g] * shrink + jnp.dot(
                    weights.astype(jnp.bfloat16), values, preferred_element_type=jnp.float32
                )

        inside = (start >= limits[2]) & (last <= limits[3])

        @pl.when(inside)
        def _():
            block(False)

        @pl.when(jnp.logical_not(inside) & (start <= limits[1]) & (last >= limits[0]))
        def _():
            block(True)

        return 0

    lax.fori_loop(0, count, visit, 0)
    for head in range(kv_local * repeat):
        g, at = head // repeat, pl.ds((head % repeat) * rows, rows)
        o_ref[:, head * HEAD_DIM : (head + 1) * HEAD_DIM] = (acc[g, at] / total[g, at]).astype(
            jnp.bfloat16
        )


def attend(query, kv, starts, limits, span):
    rows, width = query[0].shape[1:]
    heads = width // HEAD_DIM
    count, (size, kv_cols) = len(kv), kv[0].shape
    kv_local = kv_cols // (2 * HEAD_DIM)
    many = rows * heads // kv_local
    return pl.pallas_call(
        functools.partial(attention_kernel, len(query)),
        out_shape=jax.ShapeDtypeStruct((rows, width), jnp.bfloat16),
        in_specs=[SMEM, SMEM, VMEM]
        + [HBM] * (len(query) + count // 2 + 1)
        + [VMEM] * (count // 2 - 1),
        out_specs=VMEM,
        scratch_shapes=[
            *[pltpu.VMEM((rows, width), term.dtype) for term in query],
            pltpu.VMEM((count, size, kv_cols), jnp.bfloat16),
            pltpu.VMEM((kv_local, many, HEAD_DIM), jnp.bfloat16),
            pltpu.VMEM((many, 8), jnp.int32),
            pltpu.VMEM((kv_local, many, HEAD_DIM), jnp.float32),
            pltpu.VMEM((kv_local, many, HEAD_DIM), jnp.float32),
            pltpu.VMEM((kv_local, many, HEAD_DIM), jnp.float32),
            pltpu.SemaphoreType.DMA((count,)),
            pltpu.SemaphoreType.DMA((len(query),)),
        ],
        cost_estimate=pl.CostEstimate(
            flops=4 * rows * count * size * width,
            bytes_accessed=2 * (2 * rows * width + count * size * kv_cols),
            transcendentals=rows * count * size * heads,
        ),
        compiler_params=pltpu.CompilerParams(vmem_limit_bytes=20 * 1024 * 1024),
        name="attend",
    )(
        starts,
        limits,
        span,
        *[in_hbm(array) for array in (*query, *kv[: count // 2 + 1])],
        *kv[count // 2 + 1 :],
    )


def project_kernel(n, groups, turns, place, *rest):
    inputs, own_ref, near, far = (
        rest[: 2 * groups],
        rest[2 * groups],
        rest[2 * groups + 1 : 2 * groups + n],
        rest[2 * groups + n : 2 * groups + 2 * n - 1],
    )
    outs, (held, lhs, arrived) = rest[2 * groups + 2 * n - 1 : -3], rest[-3:]
    count = turns.shape[0]
    first = place[2]

    def fetch(i, d):
        @pl.when(turns[i] == d)
        def _():
            sources = (near[d - 1], far[d - 1]) if d else (own_ref.at[first], own_ref.at[1 - first])
            for kind, source in enumerate(sources):
                pltpu.make_async_copy(source, held.at[kind, i], arrived.at[kind, i]).start()

    for i in range(count):
        for d in range(n):
            fetch(i, d)

    rows = inputs[0].shape[0]
    for group in range(groups):
        a = inputs[2 * group][...]
        mine = inputs[2 * group + 1][...] != 0
        zero = jnp.zeros_like(a)
        lhs[0, group * rows : (group + 1) * rows] = jnp.where(mine, a, zero)
        lhs[1, group * rows : (group + 1) * rows] = jnp.where(mine, zero, a)
    contract = (((1,), (1,)), ((), ()))
    for i in range(count):
        value = None
        for kind in range(2):
            pltpu.make_async_copy(own_ref.at[0], held.at[kind, i], arrived.at[kind, i]).wait()
            term = lax.dot_general(
                lhs[kind], held[kind, i], contract, preferred_element_type=jnp.float32
            )
            value = term if value is None else value + term
        value = value.astype(jnp.bfloat16)
        for group in range(groups):
            outs[group][i] = value[group * rows : (group + 1) * rows]


def project(tokens, weights, turns, place):
    rows, depth = tokens[0][0].shape
    groups, count = len(tokens), turns.shape[0]
    width = weights[0].shape[1]
    return pl.pallas_call(
        functools.partial(project_kernel, (len(weights) + 1) // 2, groups),
        out_shape=[jax.ShapeDtypeStruct((count, rows, width), jnp.bfloat16)] * groups,
        in_specs=[SMEM, SMEM] + [VMEM] * (2 * groups) + [HBM] * len(weights),
        out_specs=[VMEM] * groups,
        scratch_shapes=[
            pltpu.VMEM((2, count, width, depth), jnp.bfloat16),
            pltpu.VMEM((2, groups * rows, depth), jnp.bfloat16),
            pltpu.SemaphoreType.DMA((2, count)),
        ],
        cost_estimate=pl.CostEstimate(
            flops=4 * groups * count * rows * depth * width,
            bytes_accessed=4 * count * depth * width + 2 * groups * count * rows * width,
            transcendentals=0,
        ),
        compiler_params=pltpu.CompilerParams(vmem_limit_bytes=16 * 1024 * 1024),
        name="project",
    )(turns, place, *[a for pair in tokens for a in (pair[0], pair[1][:, None])], *weights)


def body(tokens, norm_gain, w_query, w_key, w_value, w_out, modality, doc_ids):
    length, _ = tokens.shape
    n = lax.axis_size("seq")
    subs = lax.axis_size("sub")
    heads_over = lax.axis_size("head")
    z, s = lax.axis_index("seq"), lax.axis_index("sub")
    x, y = lax.axis_index("head"), lax.axis_index("grp")
    place = jnp.stack([z, x, y, s, (z * subs + s) * length]).astype(jnp.int32)

    kv_local = max(KV_HEADS // heads_over, 1)
    kv_first = x * KV_HEADS // heads_over
    w_out = jnp.swapaxes(w_out, 1, 2)

    def part_of(array, place, core):
        return lax.dynamic_slice_in_dim(array, (place * subs + core) * length, length)

    mine = lax.dynamic_index_in_dim(w_out, y, 0, keepdims=False)
    near, far = gather_weights(mine)
    weights = [w_out] + near + far

    own_mod = part_of(modality, z, s)
    share_rows = heads_over == 2
    rows = length // 2 if share_rows else length
    sends = norm_columns(tokens, norm_gain, modality, own_mod, place, n, rows)
    blocks = {0: (sends[0],)}
    for d in range(n - 1, 0, -1):
        blocks[d] = (cross(sends[d], "seq", d),)

    w_query, w_key, w_value = after((w_query, w_key, w_value), sends[0])

    key_cols = lax.dynamic_slice_in_dim(w_key, kv_first * HEAD_DIM, kv_local * HEAD_DIM, 2)
    value_cols = lax.dynamic_slice_in_dim(w_value, kv_first * HEAD_DIM, kv_local * HEAD_DIM, 2)
    row_weights = []
    for weight in (key_cols, value_cols, w_query):
        row_weights += [weight, swap(weight, "sub")]
    modality, doc_ids = after((modality, doc_ids), sends[0])
    own_doc = part_of(doc_ids, z, s)
    own_pos = (z * subs + s) * length + jnp.arange(length, dtype=jnp.int32)
    low, high = spans(modality, doc_ids, part_of(modality, z, s), own_doc, own_pos)
    span = jnp.concatenate([low[None], high[None], jnp.zeros((6, length), jnp.int32)])
    limits = jnp.stack([low[0], high[-1], low[-1], high[0]])

    if share_rows:
        for d in range(n - 1, 0, -1):
            blocks[d] = (*blocks[d], swap(blocks[d][0], "head"))
    blocks[n - 1] = after(blocks[n - 1], span, limits)

    def parts_of(group, narrow):
        begins = jnp.stack([((z ^ d) * subs + s) * length for d in group]).astype(jnp.int32)
        arrays = [blocks[d] for d in group]
        return partial(arrays, begins, length, modality, row_weights, place, narrow)

    if n == 4:
        kv_early, q_early, kv_ends, q_three, q_two = parts_of([3, 2], True)
        kv_late, q_late = parts_of([1, 0], False)
        kv_early, q_early = after((kv_early, q_early), kv_late, q_late)
        kv = along_four([kv_late[1], kv_late[0], kv_early[1], kv_early[0]], kv_ends, None, True)
        parts = [q_late[1], q_late[0], q_early[1], q_early[0]]
        query = (q_late, *along_four(parts, q_three, q_two, False))
    else:
        kv_parts, q_parts = [], []
        for d in range(n):
            kv_part, q_part = parts_of([d], False)
            kv_parts.append(kv_part[0])
            q_parts.append(q_part[0])
        kv, query = halving(kv_parts), (halving(q_parts)[None],)

    same = [kv]
    for d in range(1, n):
        same.append(cross(kv, "seq", d))
    beside = []
    for d in range(n):
        beside.append(swap(same[d], "sub"))
    starts = jnp.stack(
        [((z ^ d) * subs + s) * length for d in range(n)]
        + [((z ^ d) * subs + (1 - s)) * length for d in range(n)]
    ).astype(jnp.int32)
    attended = attend(query, same + beside, starts, limits, span)

    beside = swap(attended, "sub")
    ours_near = (own_mod == y).astype(jnp.bfloat16)
    beside_near = (part_of(modality, z, 1 - s) == y).astype(jnp.bfloat16)

    our_rows, beside_rows = (attended, ours_near), (beside, beside_near)

    def out(tokens, columns):
        return project(tokens, weights, (columns ^ z).astype(jnp.int32), place)

    if heads_over != 2:
        ours, theirs = out([our_rows, beside_rows], jnp.arange(n))
        sibling = swap(theirs, "sub")
        pair = jnp.where(s == 0, jnp.stack([ours, sibling], 1), jnp.stack([sibling, ours], 1))
        wide = jnp.transpose(pair, (2, 0, 1, 3)).reshape(length, -1)
        return lax.psum_scatter(wide, "head", scatter_dimension=1, tiled=True)

    half = n // 2
    ours, theirs = [], []

    def piece(tokens, i):
        return out([tokens], (1 - x) * half + jnp.arange(i, i + 1))[0]

    for i in range(half):
        sent = piece(our_rows, i)
        ours.append(swap(sent, "head"))
    for i in range(half):
        sent = piece(beside_rows, i)
        theirs.append(swap(sent, "head"))
    keep_ours, keep_beside = out([our_rows, beside_rows], x * half + jnp.arange(half))
    done = add(keep_beside, jnp.concatenate(theirs))
    sibling = swap(done, "sub")
    return finish(place, keep_ours, ours, sibling)


def finish_kernel(place, keep_ref, *rest):
    got_refs, sibling_ref, o_ref = rest[:-2], rest[-2], rest[-1]
    width = keep_ref.shape[2]

    def fill(core):
        for i, got_ref in enumerate(got_refs):
            own = keep_ref[i].astype(jnp.float32) + got_ref[0].astype(jnp.float32)
            for piece, slot in ((own.astype(jnp.bfloat16), core), (sibling_ref[i], 1 - core)):
                at = (2 * i + slot) * width
                o_ref[:, at : at + width] = piece

    for core in range(2):

        @pl.when(place[3] == core)
        def _():
            fill(core)


def finish(place, keep, got, sibling):
    count, rows, width = keep.shape
    return pl.pallas_call(
        finish_kernel,
        out_shape=jax.ShapeDtypeStruct((rows, 2 * count * width), jnp.bfloat16),
        in_specs=[SMEM] + [VMEM] * (2 + len(got)),
        out_specs=VMEM,
        cost_estimate=pl.CostEstimate(
            flops=count * rows * width, bytes_accessed=12 * count * rows * width, transcendentals=0
        ),
        compiler_params=pltpu.CompilerParams(vmem_limit_bytes=12 * 1024 * 1024),
        name="finish",
    )(place, keep, *got, sibling)


def solution(mesh):
    placed = (
        P(("grp", "seq", "sub"), None),
        P(),
        P(None, ("seq", "sub"), "head"),
        P(None, ("seq", "sub"), None),
        P(None, ("seq", "sub"), None),
        P(None, "head", ("seq", "sub")),
        P("grp"),
        P("grp"),
    )
    return jax.shard_map(
        body,
        mesh=mesh,
        in_specs=placed,
        out_specs=P(("grp", "seq", "sub"), "head"),
        check_vma=False,
    )
```

```python
import functools
import math

import jax
import jax.numpy as jnp
from jax import lax
from jax.experimental import pallas as pl
from jax.experimental.pallas import tpu as pltpu
from jax.sharding import PartitionSpec as P


HEAD_DIM = 128
KV_HEADS = 4
RUN = 64
EPS = 1e-06
LOW = -1e30


def swap(x, axis):
    return lax.ppermute(x, axis, [(0, 1), (1, 0)])


def cross(x, axis, bit, among=None):
    size = lax.axis_size(axis)
    return lax.ppermute(x, axis, [(i ^ bit, i) for i in (among or range(size))])


def after(value, *done):
    return lax.optimization_barrier((value, *done))[0]


def add(a, b):
    return (a.astype(jnp.float32) + b.astype(jnp.float32)).astype(jnp.bfloat16)


VMEM = pl.BlockSpec(memory_space=pltpu.VMEM)
SMEM = pl.BlockSpec(memory_space=pltpu.SMEM)
HBM = pl.BlockSpec(memory_space=pltpu.HBM)


def in_hbm(x):
    return pltpu.with_memory_space_constraint(x, pltpu.HBM)


def norm_kernel(place, modality, tokens_ref, gain_ref, own_ref, *rest):
    send_refs, (scratch, arrived) = rest[:-2], rest[-2:]
    width = own_ref.shape[1]
    copies = []
    for i, at in enumerate(range(0, tokens_ref.shape[0], RUN)):
        rows = pl.ds(at, RUN)
        copies.append(pltpu.make_async_copy(tokens_ref.at[rows], scratch.at[rows], arrived.at[i]))
        copies[-1].start()
    for i, at in enumerate(range(0, tokens_ref.shape[0], RUN)):
        copies[i].wait()
        values = scratch[at : at + RUN].astype(jnp.float32)
        factor = lax.rsqrt(jnp.mean(values * values, axis=1, keepdims=True) + EPS)
        gain = jnp.where(modality[place[4] + at] == 1, gain_ref[1:2, :], gain_ref[0:1, :])
        scratch[at : at + RUN] = (values * factor * gain).astype(jnp.bfloat16)

    def columns(d):
        return pl.ds(pl.multiple_of((place[0] ^ d) * width, width), width)

    own_ref[...] = scratch[:, columns(0)]
    for d, ref in enumerate(send_refs, 1):
        rows = ref.shape[0]
        ref[...] = scratch[pl.ds(pl.multiple_of(place[1] * rows, rows), rows), columns(d)]


def norm_columns(tokens, norm_gain, modality, mod, place, n, rows):
    length, depth = tokens.shape
    width = depth // n
    if width % 128:
        values32 = tokens.astype(jnp.float32)
        factor = lax.rsqrt(jnp.mean(values32 * values32, axis=1, keepdims=True) + EPS)
        gain = jnp.where((mod == 1)[:, None], norm_gain[1][None, :], norm_gain[0][None, :])
        normed = (values32 * factor * gain).astype(jnp.bfloat16)
        first = [0] + [place[1] * rows] * (n - 1)
        count = [length] + [rows] * (n - 1)
        return [
            lax.dynamic_slice(normed, (first[d], (place[0] ^ d) * width), (count[d], width))
            for d in range(n)
        ]
    shapes = [jax.ShapeDtypeStruct((length, width), jnp.bfloat16)]
    shapes += [jax.ShapeDtypeStruct((rows, width), jnp.bfloat16)] * (n - 1)
    return pl.pallas_call(
        norm_kernel,
        out_shape=shapes,
        in_specs=[SMEM, SMEM, HBM, VMEM],
        out_specs=[VMEM] * n,
        scratch_shapes=[
            pltpu.VMEM((length, depth), jnp.bfloat16),
            pltpu.SemaphoreType.DMA((length // RUN,)),
        ],
        cost_estimate=pl.CostEstimate(
            flops=6 * length * depth, bytes_accessed=4 * length * depth, transcendentals=length
        ),
        compiler_params=pltpu.CompilerParams(vmem_limit_bytes=12 * 1024 * 1024),
        name="norm",
    )(place, modality, in_hbm(tokens), norm_gain)


def partial_kernel(counts, narrow, place, modality, begins, *rest):
    total = sum(counts)
    sources, refs, outs = rest[:6], rest[6 : 6 + total], rest[6 + total : -8]
    both, other, held_kv, held_q, wide_kv, wide_q, arrived, left = rest[-8:]
    length = both.shape[0] // len(counts)
    half = length // 2
    kv_half = held_kv.shape[2] // 2
    depth = held_kv.shape[1] // 2
    copies = []

    def fetch(source, target):
        copies.append(pltpu.make_async_copy(source, target, arrived.at[len(copies)]))
        copies[-1].start()

    at = 0
    for number, count in enumerate(counts):
        base = number * length
        if count == 1:
            fetch(refs[at], both.at[base : base + length])
        else:
            for which in range(2):
                row = base + (place[1] if which == 0 else 1 - place[1]) * half
                fetch(refs[at + which], both.at[pl.ds(pl.multiple_of(row, half), half)])
        at += count
    for i, source in enumerate(sources):
        core = place[3] if i % 2 == 0 else 1 - place[3]
        rows = pl.ds(pl.multiple_of(core * depth, depth), depth)
        target = (
            held_kv.at[:, rows, 0:kv_half],
            held_kv.at[:, rows, kv_half : 2 * kv_half],
            held_q.at[:, rows],
        )[i // 2]
        fetch(source, target)
    for copy in copies[:total]:
        copy.wait()
    for number in range(len(counts)):
        for step in range(0, length, RUN):
            rows = pl.ds(number * length + step, RUN)
            generate = modality[begins[number] + step] == 1
            block = both[rows]
            zero = jnp.zeros_like(block)
            both[rows] = jnp.where(generate, zero, block)
            other[rows] = jnp.where(generate, block, zero)
    first, second = both[...], other[...]
    pieces = wide_q.shape[0]
    width = wide_q.shape[2]
    stores = []

    def project(held, cols, wide, out):
        value = jnp.dot(first, held[0, :, cols], preferred_element_type=jnp.float32) + jnp.dot(
            second, held[1, :, cols], preferred_element_type=jnp.float32
        )
        wide[...] = value
        stores.append(pltpu.make_async_copy(wide, out, left.at[len(stores)]))
        stores[-1].start()
        return value.astype(jnp.bfloat16)

    for copy in copies[total : total + 4]:
        copy.wait()
    value = project(held_kv, slice(None), wide_kv, outs[0])
    if narrow:
        outs[2][...] = value
    for copy in copies[total + 4 :]:
        copy.wait()
    for piece in range(pieces):
        cols = slice(piece * width, (piece + 1) * width)
        value = project(held_q, cols, wide_q.at[piece], outs[1].at[:, cols])
        if narrow:
            for number in range(len(counts)):
                outs[3 + number][:, cols] = value[number * length : (number + 1) * length]
    for store in stores:
        store.wait()


def partial(blocks, begins, length, modality, weights, place, narrow):
    counts = tuple(len(block) for block in blocks)
    places = [pair for block in blocks for pair in enumerate(block)]
    arrays = [array for _, array in places]
    rows, width = length * len(blocks), arrays[0].shape[1]
    pieces = 2 if weights[4].shape[2] % 256 == 0 else 1
    kv_cols, q_cols = 2 * weights[0].shape[2], weights[4].shape[2]
    shapes = [pltpu.HBM((rows, cols), jnp.float32) for cols in (kv_cols, q_cols)]
    if narrow:
        shapes.append(jax.ShapeDtypeStruct((rows, kv_cols), jnp.bfloat16))
        shapes += [jax.ShapeDtypeStruct((length, q_cols), jnp.bfloat16)] * len(blocks)
    values = pl.pallas_call(
        functools.partial(partial_kernel, counts, narrow),
        out_shape=shapes,
        in_specs=[SMEM] * 3 + [HBM] * len(weights) + [VMEM if i else HBM for i, _ in places],
        out_specs=[HBM] * 2 + [VMEM] * (len(shapes) - 2),
        scratch_shapes=[
            pltpu.VMEM((rows, width), jnp.bfloat16),
            pltpu.VMEM((rows, width), jnp.bfloat16),
            pltpu.VMEM((2, width, kv_cols), jnp.bfloat16),
            pltpu.VMEM((2, width, q_cols), jnp.bfloat16),
            pltpu.VMEM((rows, kv_cols), jnp.float32),
            pltpu.VMEM((pieces, rows, q_cols // pieces), jnp.float32),
            pltpu.SemaphoreType.DMA((len(weights) + len(arrays),)),
            pltpu.SemaphoreType.DMA((1 + pieces,)),
        ],
        cost_estimate=pl.CostEstimate(
            flops=4 * rows * width * (kv_cols + q_cols),
            bytes_accessed=4 * (width + rows) * (kv_cols + q_cols),
            transcendentals=0,
        ),
        compiler_params=pltpu.CompilerParams(vmem_limit_bytes=24 * 1024 * 1024),
        name="partial",
    )(
        place,
        modality,
        begins,
        *[in_hbm(w) for w in weights],
        *[a if i else in_hbm(a) for i, a in places],
    )
    return [value.reshape(len(blocks), length, -1) for value in values[:3]] + list(values[3:])


def halving(parts):
    n = len(parts)
    sums = dict(enumerate(parts))
    for bit in [1 << i for i in range(n.bit_length() - 1)]:
        for d in [d for d in range(n) if d in sums and d & bit]:
            sums[d ^ bit] = sums[d ^ bit] + cross(sums.pop(d).astype(jnp.bfloat16), "seq", bit)
    return sums[0].astype(jnp.bfloat16)


def along_four(parts, three, two, whole):
    wide = [p.astype(jnp.float32) for p in parts]

    def hop(value, bit, among):
        return cross(value, "seq", bit, among)

    def plus(a, b):
        return (a + b.astype(jnp.float32)).astype(jnp.bfloat16)

    if two is None:
        got = hop(three, 1, (1, 2))
        got = hop(plus(jnp.stack([wide[2], wide[3]]), got), 3, (1, 2))
        across, own = got[0], got[1]
    else:
        far = hop(three, 1, (1, 2))
        close = hop(two, 1, (1, 2))
        send = plus(wide[2], far)
        across = hop(send, 3, (1, 2))
        own = hop(plus(wide[3], after(close, send)), 3, (1, 2))
    last = hop(plus(wide[1], across), 1, None)
    if not whole:
        return last, own
    return (wide[0] + last.astype(jnp.float32) + own.astype(jnp.float32)).astype(jnp.bfloat16)


def gather_weights(mine):
    n = lax.axis_size("seq")
    if n == 4:
        z = lax.axis_index("seq")
        inner = (z == 1) | (z == 2)
        one = cross(mine, "seq", 1)
        middle = cross(mine, "seq", 3, (1, 2))
        middle_two = cross(one, "seq", 3, (1, 2))
        outer_two = cross(middle, "seq", 1, (0, 3))
        outer_three = cross(middle_two, "seq", 1, (0, 3))
        near = [mine, one, jnp.where(inner, middle_two, outer_two), jnp.where(inner, middle, outer_three)]
    else:
        near = [mine]
        for bit in reversed([1 << i for i in range(n.bit_length() - 1)]):
            got = cross(jnp.stack(near), "seq", bit)
            near = near + [got[i] for i in range(len(near))]
        order = [0]
        for bit in reversed([1 << i for i in range(n.bit_length() - 1)]):
            order = order + [d ^ bit for d in order]
        near = [near[order.index(d)] for d in range(n)]
    far = []
    for d in range(1, n):
        far.append(swap(near[d], "grp"))
    return near[1:], far


def spans(modality, doc_ids, own_mod, own_doc, own_pos):
    changed = (modality[1:] != modality[:-1]) | (doc_ids[1:] != doc_ids[:-1])
    begins = jnp.concatenate([jnp.ones((1,), jnp.int32), changed.astype(jnp.int32)])
    blocks = jnp.cumsum(begins)
    own_block = lax.dynamic_slice_in_dim(blocks, own_pos[0], own_pos.shape[0])
    low = jnp.sum((doc_ids[None, :] < own_doc[:, None]).astype(jnp.int32), axis=1)
    end = jnp.sum((blocks[None, :] <= own_block[:, None]).astype(jnp.int32), axis=1) - 1
    return low, jnp.where(own_mod == 1, end, own_pos)


def attention_kernel(terms, starts, limits, span_ref, *rest):
    inner = len(rest) - 9 - terms
    q_sources, sources, q_refs = rest[:terms], rest[terms:inner], rest[inner + 1 : inner + 1 + terms]
    o_ref = rest[inner]
    kv_ref, queries, bounds, top, total, acc, arrived, landed = rest[-8:]
    count, size, _ = kv_ref.shape
    landing = []
    for i, (source, held) in enumerate(zip(q_sources, q_refs)):
        source = source if i else source.at[source.shape[0] - 1]
        landing.append(pltpu.make_async_copy(source, held, landed.at[i]))
        landing[-1].start()
    for number, source in enumerate(sources):
        pltpu.make_async_copy(source, kv_ref.at[number], arrived.at[number]).start()
    rows = o_ref.shape[0]
    kv_local, many = queries.shape[0], queries.shape[1]
    repeat = many // rows
    scale = math.log2(math.e) / math.sqrt(HEAD_DIM)
    top[...] = jnp.full_like(top, LOW / 10)
    total[...] = jnp.zeros_like(total)
    acc[...] = jnp.zeros_like(acc)
    columns = span_ref[...].T
    for r in range(repeat):
        bounds[r * rows : (r + 1) * rows] = columns
    for copy in landing:
        copy.wait()
    for head in range(kv_local * repeat):
        g, r = head // repeat, head % repeat
        cols = slice(head * HEAD_DIM, (head + 1) * HEAD_DIM)
        query = q_refs[0][:, cols].astype(jnp.float32)
        for term in q_refs[1:]:
            query = query + term[:, cols].astype(jnp.float32)
        queries[g, r * rows : (r + 1) * rows] = query.astype(jnp.bfloat16)
    transposed = (((1,), (1,)), ((), ()))

    def visit(number, _):
        start = starts[number]
        last = start + size - 1
        pltpu.make_async_copy(sources[0], kv_ref.at[number], arrived.at[number]).wait()

        def block(masked):
            for g in range(kv_local):
                keys = kv_ref[number, :, g * HEAD_DIM : (g + 1) * HEAD_DIM]
                values = kv_ref[number, :, (kv_local + g) * HEAD_DIM : (kv_local + g + 1) * HEAD_DIM]
                scores = lax.dot_general(
                    queries[g], keys, transposed, preferred_element_type=jnp.float32
                )
                if masked:
                    key_pos = start + lax.broadcasted_iota(jnp.int32, (many, size), 1)
                    seen = (key_pos >= bounds[:, 0:1]) & (key_pos <= bounds[:, 1:2])
                    scores = jnp.where(seen, scores, LOW)
                old = top[g]
                new = jnp.maximum(old, jnp.max(scores, axis=1, keepdims=True))
                weights = jnp.exp2((scores - jnp.tile(new, (1, size // 128))) * scale)
                shrink = jnp.exp2((old - new) * scale)
                total[g] = total[g] * shrink + jnp.sum(weights, axis=1, keepdims=True)
                top[g] = new
                acc[g] = acc[g] * shrink + jnp.dot(
                    weights.astype(jnp.bfloat16), values, preferred_element_type=jnp.float32
                )

        inside = (start >= limits[2]) & (last <= limits[3])

        @pl.when(inside)
        def _():
            block(False)

        @pl.when(jnp.logical_not(inside) & (start <= limits[1]) & (last >= limits[0]))
        def _():
            block(True)

        return 0

    lax.fori_loop(0, count, visit, 0)
    for head in range(kv_local * repeat):
        g, at = head // repeat, pl.ds((head % repeat) * rows, rows)
        o_ref[:, head * HEAD_DIM : (head + 1) * HEAD_DIM] = (acc[g, at] / total[g, at]).astype(
            jnp.bfloat16
        )


def attend(query, kv, starts, limits, span):
    rows, width = query[0].shape[1:]
    heads = width // HEAD_DIM
    count, (size, kv_cols) = len(kv), kv[0].shape
    kv_local = kv_cols // (2 * HEAD_DIM)
    many = rows * heads // kv_local
    return pl.pallas_call(
        functools.partial(attention_kernel, len(query)),
        out_shape=jax.ShapeDtypeStruct((rows, width), jnp.bfloat16),
        in_specs=[SMEM, SMEM, VMEM]
        + [HBM] * (len(query) + count),
        out_specs=VMEM,
        scratch_shapes=[
            *[pltpu.VMEM((rows, width), term.dtype) for term in query],
            pltpu.VMEM((count, size, kv_cols), jnp.bfloat16),
            pltpu.VMEM((kv_local, many, HEAD_DIM), jnp.bfloat16),
            pltpu.VMEM((many, 8), jnp.int32),
            pltpu.VMEM((kv_local, many, HEAD_DIM), jnp.float32),
            pltpu.VMEM((kv_local, many, HEAD_DIM), jnp.float32),
            pltpu.VMEM((kv_local, many, HEAD_DIM), jnp.float32),
            pltpu.SemaphoreType.DMA((count,)),
            pltpu.SemaphoreType.DMA((len(query),)),
        ],
        cost_estimate=pl.CostEstimate(
            flops=4 * rows * count * size * width,
            bytes_accessed=2 * (2 * rows * width + count * size * kv_cols),
            transcendentals=rows * count * size * heads,
        ),
        compiler_params=pltpu.CompilerParams(vmem_limit_bytes=20 * 1024 * 1024),
        name="attend",
    )(
        starts,
        limits,
        span,
        *[in_hbm(array) for array in (*query, *kv)],
    )


def project_kernel(n, groups, turns, place, *rest):
    inputs, own_ref, near, far = (
        rest[: 2 * groups],
        rest[2 * groups],
        rest[2 * groups + 1 : 2 * groups + n],
        rest[2 * groups + n : 2 * groups + 2 * n - 1],
    )
    outs, (held, lhs, arrived) = rest[2 * groups + 2 * n - 1 : -3], rest[-3:]
    count = turns.shape[0]
    first = place[2]

    def fetch(i, d):
        @pl.when(turns[i] == d)
        def _():
            sources = (near[d - 1], far[d - 1]) if d else (own_ref.at[first], own_ref.at[1 - first])
            for kind, source in enumerate(sources):
                pltpu.make_async_copy(source, held.at[kind, i], arrived.at[kind, i]).start()

    for i in range(count):
        for d in range(n):
            fetch(i, d)

    rows = inputs[0].shape[0]
    for group in range(groups):
        a = inputs[2 * group][...]
        mine = inputs[2 * group + 1][...] != 0
        zero = jnp.zeros_like(a)
        lhs[0, group * rows : (group + 1) * rows] = jnp.where(mine, a, zero)
        lhs[1, group * rows : (group + 1) * rows] = jnp.where(mine, zero, a)
    contract = (((1,), (1,)), ((), ()))
    for i in range(count):
        value = None
        for kind in range(2):
            pltpu.make_async_copy(own_ref.at[0], held.at[kind, i], arrived.at[kind, i]).wait()
            term = lax.dot_general(
                lhs[kind], held[kind, i], contract, preferred_element_type=jnp.float32
            )
            value = term if value is None else value + term
        value = value.astype(jnp.bfloat16)
        for group in range(groups):
            outs[group][i] = value[group * rows : (group + 1) * rows]


def project(tokens, weights, turns, place):
    rows, depth = tokens[0][0].shape
    groups, count = len(tokens), turns.shape[0]
    width = weights[0].shape[1]
    return pl.pallas_call(
        functools.partial(project_kernel, (len(weights) + 1) // 2, groups),
        out_shape=[jax.ShapeDtypeStruct((count, rows, width), jnp.bfloat16)] * groups,
        in_specs=[SMEM, SMEM] + [VMEM] * (2 * groups) + [HBM] * len(weights),
        out_specs=[VMEM] * groups,
        scratch_shapes=[
            pltpu.VMEM((2, count, width, depth), jnp.bfloat16),
            pltpu.VMEM((2, groups * rows, depth), jnp.bfloat16),
            pltpu.SemaphoreType.DMA((2, count)),
        ],
        cost_estimate=pl.CostEstimate(
            flops=4 * groups * count * rows * depth * width,
            bytes_accessed=4 * count * depth * width + 2 * groups * count * rows * width,
            transcendentals=0,
        ),
        compiler_params=pltpu.CompilerParams(vmem_limit_bytes=16 * 1024 * 1024),
        name="project",
    )(turns, place, *[a for pair in tokens for a in (pair[0], pair[1][:, None])], *weights)


def body(tokens, norm_gain, w_query, w_key, w_value, w_out, modality, doc_ids):
    length, _ = tokens.shape
    n = lax.axis_size("seq")
    subs = lax.axis_size("sub")
    heads_over = lax.axis_size("head")
    z, s = lax.axis_index("seq"), lax.axis_index("sub")
    x, y = lax.axis_index("head"), lax.axis_index("grp")
    place = jnp.stack([z, x, y, s, (z * subs + s) * length]).astype(jnp.int32)

    kv_local = max(KV_HEADS // heads_over, 1)
    kv_first = x * KV_HEADS // heads_over
    w_out = jnp.swapaxes(w_out, 1, 2)

    def part_of(array, place, core):
        return lax.dynamic_slice_in_dim(array, (place * subs + core) * length, length)

    mine = lax.dynamic_index_in_dim(w_out, y, 0, keepdims=False)
    near, far = gather_weights(mine)
    weights = [w_out] + near + far

    own_mod = part_of(modality, z, s)
    share_rows = heads_over == 2
    rows = length // 2 if share_rows else length
    sends = norm_columns(tokens, norm_gain, modality, own_mod, place, n, rows)
    blocks = {0: (sends[0],)}
    for d in range(n - 1, 0, -1):
        blocks[d] = (cross(sends[d], "seq", d),)

    w_query, w_key, w_value = after((w_query, w_key, w_value), sends[0])

    key_cols = lax.dynamic_slice_in_dim(w_key, kv_first * HEAD_DIM, kv_local * HEAD_DIM, 2)
    value_cols = lax.dynamic_slice_in_dim(w_value, kv_first * HEAD_DIM, kv_local * HEAD_DIM, 2)
    row_weights = []
    for weight in (key_cols, value_cols, w_query):
        row_weights += [weight, swap(weight, "sub")]
    modality, doc_ids = after((modality, doc_ids), sends[0])
    own_doc = part_of(doc_ids, z, s)
    own_pos = (z * subs + s) * length + jnp.arange(length, dtype=jnp.int32)
    low, high = spans(modality, doc_ids, part_of(modality, z, s), own_doc, own_pos)
    span = jnp.concatenate([low[None], high[None], jnp.zeros((6, length), jnp.int32)])
    limits = jnp.stack([low[0], high[-1], low[-1], high[0]])

    if share_rows:
        for d in range(n - 1, 0, -1):
            blocks[d] = (*blocks[d], swap(blocks[d][0], "head"))
    blocks[n - 1] = after(blocks[n - 1], span, limits)

    def parts_of(group, narrow):
        begins = jnp.stack([((z ^ d) * subs + s) * length for d in group]).astype(jnp.int32)
        arrays = [blocks[d] for d in group]
        return partial(arrays, begins, length, modality, row_weights, place, narrow)

    if n == 4:
        kv_early, q_early, kv_ends, q_three, q_two = parts_of([3, 2], True)
        kv_late, q_late = parts_of([1, 0], False)
        kv_early, q_early = after((kv_early, q_early), kv_late, q_late)
        kv = along_four([kv_late[1], kv_late[0], kv_early[1], kv_early[0]], kv_ends, None, True)
        parts = [q_late[1], q_late[0], q_early[1], q_early[0]]
        query = (q_late, *along_four(parts, q_three, q_two, False))
    else:
        kv_parts, q_parts = [], []
        for d in range(n):
            kv_part, q_part = parts_of([d], False)
            kv_parts.append(kv_part[0])
            q_parts.append(q_part[0])
        kv, query = halving(kv_parts), (halving(q_parts)[None],)

    same = [kv]
    for d in range(1, n):
        same.append(cross(kv, "seq", d))
    beside = []
    for d in range(n):
        beside.append(swap(same[d], "sub"))
    starts = jnp.stack(
        [((z ^ d) * subs + s) * length for d in range(n)]
        + [((z ^ d) * subs + (1 - s)) * length for d in range(n)]
    ).astype(jnp.int32)
    attended = attend(query, same + beside, starts, limits, span)

    beside = swap(attended, "sub")
    ours_near = (own_mod == y).astype(jnp.bfloat16)
    beside_near = (part_of(modality, z, 1 - s) == y).astype(jnp.bfloat16)

    our_rows, beside_rows = (attended, ours_near), (beside, beside_near)

    def out(tokens, columns):
        return project(tokens, weights, (columns ^ z).astype(jnp.int32), place)

    if heads_over != 2:
        ours, theirs = out([our_rows, beside_rows], jnp.arange(n))
        sibling = swap(theirs, "sub")
        pair = jnp.where(s == 0, jnp.stack([ours, sibling], 1), jnp.stack([sibling, ours], 1))
        wide = jnp.transpose(pair, (2, 0, 1, 3)).reshape(length, -1)
        return lax.psum_scatter(wide, "head", scatter_dimension=1, tiled=True)

    half = n // 2
    ours, theirs = [], []

    def piece(tokens, i):
        return out([tokens], (1 - x) * half + jnp.arange(i, i + 1))[0]

    for i in range(half):
        sent = piece(our_rows, i)
        ours.append(swap(sent, "head"))
    for i in range(half):
        sent = piece(beside_rows, i)
        theirs.append(swap(sent, "head"))
    keep_ours, keep_beside = out([our_rows, beside_rows], x * half + jnp.arange(half))
    done = add(keep_beside, jnp.concatenate(theirs))
    sibling = swap(done, "sub")
    return finish(place, keep_ours, ours, sibling)


def finish_kernel(place, keep_ref, *rest):
    got_refs, sibling_ref, o_ref = rest[:-2], rest[-2], rest[-1]
    width = keep_ref.shape[2]

    def fill(core):
        for i, got_ref in enumerate(got_refs):
            own = keep_ref[i].astype(jnp.float32) + got_ref[0].astype(jnp.float32)
            for piece, slot in ((own.astype(jnp.bfloat16), core), (sibling_ref[i], 1 - core)):
                at = (2 * i + slot) * width
                o_ref[:, at : at + width] = piece

    for core in range(2):

        @pl.when(place[3] == core)
        def _():
            fill(core)


def finish(place, keep, got, sibling):
    count, rows, width = keep.shape
    return pl.pallas_call(
        finish_kernel,
        out_shape=jax.ShapeDtypeStruct((rows, 2 * count * width), jnp.bfloat16),
        in_specs=[SMEM] + [VMEM] * (2 + len(got)),
        out_specs=VMEM,
        cost_estimate=pl.CostEstimate(
            flops=count * rows * width, bytes_accessed=12 * count * rows * width, transcendentals=0
        ),
        compiler_params=pltpu.CompilerParams(vmem_limit_bytes=12 * 1024 * 1024),
        name="finish",
    )(place, keep, *got, sibling)


def solution(mesh):
    placed = (
        P(("grp", "seq", "sub"), None),
        P(),
        P(None, ("seq", "sub"), "head"),
        P(None, ("seq", "sub"), None),
        P(None, ("seq", "sub"), None),
        P(None, "head", ("seq", "sub")),
        P("grp"),
        P("grp"),
    )
    return jax.shard_map(
        body,
        mesh=mesh,
        in_specs=placed,
        out_specs=P(("grp", "seq", "sub"), "head"),
        check_vma=False,
    )
```
